32 devices in a mesh: seq: 8 (over y, x, core), wt: 4 (over z).
Axes of the slice: x: 2, y: 2, z: 4, core: 2. Of those that a mesh axis runs over, the one named last changes fastest.
Arguments:
- block_in: bfloat16 [8192, 768], P(('seq', 'wt')), may hold values from -6 to 6
- in_gain: bfloat16 [768], P('wt'), may hold values from 0.5 to 1.5
- proj_gate: bfloat16 [768, 1536], P(None, 'wt'), may hold values from -0.21875 to 0.21875
- proj_inner: bfloat16 [768, 1536], P(None, 'wt'), may hold values from -0.21875 to 0.21875
- proj_bcoef: bfloat16 [768, 256], P(None, 'wt'), may hold values from -0.21875 to 0.21875
- proj_step: bfloat16 [768, 24], P(None, 'wt'), may hold values from -0.21875 to 0.21875
- conv_inner: float32 [4, 1536], P(None, 'wt'), may hold values from -3 to 3
- conv_inner_bias: float32 [1536], P('wt'), may hold values from -0.5 to 0.5
- conv_bcoef: float32 [4, 256], P(None, 'wt'), may hold values from -3 to 3
- conv_bcoef_bias: float32 [256], P('wt'), may hold values from -0.5 to 0.5
- step_bias: float32 [24], P('wt'), may hold values from -6 to -2
- decay_log: float32 [24], P('wt'), may hold values from -4 to 1
- skip_gain: float32 [24], P('wt'), may hold values from 0.5 to 1.5
- norm_gain: float32 [1536], P('wt'), may hold values from 0.5 to 1.5
- proj_out: bfloat16 [1536, 768], P('wt'), may hold values from -0.15625 to 0.15625
- out_grad: bfloat16 [8192, 768], P(('seq', 'wt')), may hold values from -6 to 6
- doc_starts: int32 [1], replicated, may hold values from 0 to 0, as said below
Outputs:
- block_out: bfloat16 [8192, 768], P(('seq', 'wt'))
- input_grad: float32 [8192, 768], P(('seq', 'wt'))
- grad_in_gain: float32 [768], P('wt')
- grad_proj_gate: float32 [768, 1536], P(None, 'wt')
- grad_proj_inner: float32 [768, 1536], P(None, 'wt')
- grad_proj_bcoef: float32 [768, 256], P(None, 'wt')
- grad_proj_step: float32 [768, 24], P(None, 'wt')
- grad_conv_inner: float32 [4, 1536], P(None, 'wt')
- grad_conv_bcoef: float32 [4, 256], P(None, 'wt')
- grad_conv_inner_bias: float32 [1536], P('wt')
- grad_conv_bcoef_bias: float32 [256], P('wt')
- grad_step_bias: float32 [24], P('wt')
- grad_decay_log: float32 [24], P('wt')
- grad_skip_gain: float32 [24], P('wt')
- grad_norm_gain: float32 [1536], P('wt')
- grad_proj_out: float32 [1536, 768], P('wt')
The draws below stay inside these ranges and needn't reach their ends.
Inputs may be any that keep to these rules, and one draw needn't show every extreme that they name: `doc_starts`: document starts in rising order; the first is 0 and two consecutive starts are 4096 apart or more.
All inputs are finite; a program needn't handle non-finite values.
Results may differ from the reference program's by a relative error of at most 0.012.
The reference program's roundings to bfloat16 on the way (of `normed`, `bcoef`, `gated_norm` and `gate_b16`) count: a program that leaves them out, or rounds other values in their place, can miss the bound.
Values may be sent and summed in bfloat16 or wider, within the bound.
No kernel may reach another device: no remote copies, remote signals or barrier semaphores. Data moves between devices by JAX's collectives and lax.ppermute only.
A program may use at most 128 MiB of HBM per device.

```python
import jax
import jax.numpy as jnp
from jax import lax

D = 768
HEADS = 24
HEAD_DIM = 64
STATE = 128
CONV = 4
BLOCK = 256
INNER = 1536
TOK_DEV = 1024
SEQ_LEN = 8192
TOKENS = 8192
DOCS = 1


def draw_doc_starts(key, part):
    jitter = SEQ_LEN // 4
    offsets = jax.random.randint(jax.random.fold_in(key, 11), (DOCS,), -jitter, jitter + 1)
    base = jnp.arange(DOCS, dtype=jnp.int32) * SEQ_LEN
    starts = base + offsets.astype(jnp.int32)
    starts = jnp.where(jnp.arange(DOCS) == DOCS - 1, base + jitter, starts)
    return jnp.where(jnp.arange(DOCS) == 0, 0, starts).astype(jnp.int32)


def block_scale(rng, shape, cuts, smallest, high):
    def one(position, blocks):
        draws = jax.random.uniform(jax.random.fold_in(jax.random.fold_in(rng, 6), position), (blocks,), jnp.float32, smallest / len(cuts), high / len(cuts))
        return jnp.repeat(jnp.exp(draws), shape[position] // blocks).reshape((-1,) + (1,) * (len(shape) - position - 1))

    gain = one(*cuts[0])
    for cut in cuts[1:]:
        gain = gain * one(*cut)
    return gain


def gaussian(rng, shape, spread, most, split=(), kind=jnp.bfloat16):
    array = spread * jax.random.normal(rng, shape, jnp.float32)
    if split:
        array = array * block_scale(rng, shape, split, -0.22, 0.18)
    return jnp.clip(array, -most, most).astype(kind)


def setup_inputs(seed: int = 0) -> dict:
    keys = jax.random.split(jax.random.key(seed), 18)
    block_in = gaussian(keys[0], (TOKENS, D), 1.0, 6.0, ((0, 32),))
    in_gain = jnp.clip(0.5 + 1.0 * jax.random.uniform(keys[1], (D,), jnp.float32) ** block_scale(keys[1], (D,), ((0, 4),), -0.2, 0.2), 0.5, 1.5).astype(jnp.bfloat16)
    proj_gate = gaussian(keys[2], (D, INNER), D ** -0.5, 0.21875, ((1, 4),))
    proj_inner = gaussian(keys[3], (D, INNER), D ** -0.5, 0.21875, ((1, 4),))
    proj_bcoef = gaussian(keys[4], (D, 2 * STATE), D ** -0.5, 0.21875, ((1, 4),))
    proj_step = gaussian(keys[5], (D, HEADS), D ** -0.5, 0.21875, ((1, 4),))
    conv_inner = gaussian(keys[6], (CONV, INNER), CONV ** -0.5, 3.0, ((1, 4),), jnp.float32)
    conv_inner_bias = jnp.clip(jax.random.uniform(keys[7], (INNER,), jnp.float32, -0.5, 0.5) * block_scale(keys[7], (INNER,), ((0, 4),), -0.4, 0.0), -0.5, 0.5)
    conv_bcoef = gaussian(keys[8], (CONV, 2 * STATE), CONV ** -0.5, 3.0, ((1, 4),), jnp.float32)
    conv_bcoef_bias = jnp.clip(jax.random.uniform(keys[9], (2 * STATE,), jnp.float32, -0.5, 0.5) * block_scale(keys[9], (2 * STATE,), ((0, 4),), -0.4, 0.0), -0.5, 0.5)
    step_bias = jnp.clip(-6.0 + 4.0 * jax.random.uniform(keys[10], (HEADS,), jnp.float32) ** block_scale(keys[10], (HEADS,), ((0, 4),), -0.2, 0.2), -6.0, -2.0)
    decay_log = jnp.clip(-4.0 + 5.0 * jax.random.uniform(keys[11], (HEADS,), jnp.float32) ** block_scale(keys[11], (HEADS,), ((0, 4),), -0.2, 0.2), -4.0, 1.0)
    skip_gain = jnp.clip(0.5 + 1.0 * jax.random.uniform(keys[12], (HEADS,), jnp.float32) ** block_scale(keys[12], (HEADS,), ((0, 4),), -0.2, 0.2), 0.5, 1.5)
    norm_gain = jnp.clip(0.5 + 1.0 * jax.random.uniform(keys[13], (INNER,), jnp.float32) ** block_scale(keys[13], (INNER,), ((0, 4),), -0.2, 0.2), 0.5, 1.5)
    proj_out = gaussian(keys[14], (INNER, D), INNER ** -0.5, 0.15625, ((0, 4),))
    out_grad = gaussian(keys[15], (TOKENS, D), 1.0, 6.0, ((0, 32),))
    doc_starts = draw_doc_starts(jax.random.fold_in(keys[17], 71), 0)
    return dict(block_in=block_in, in_gain=in_gain, proj_gate=proj_gate, proj_inner=proj_inner, proj_bcoef=proj_bcoef, proj_step=proj_step, conv_inner=conv_inner, conv_inner_bias=conv_inner_bias, conv_bcoef=conv_bcoef, conv_bcoef_bias=conv_bcoef_bias, step_bias=step_bias, decay_log=decay_log, skip_gain=skip_gain, norm_gain=norm_gain, proj_out=proj_out, out_grad=out_grad, doc_starts=doc_starts)


EPSILON = 1e-05
HIGHEST = lax.Precision.HIGHEST

def doc_index(positions, starts):
    return lax.optimization_barrier(jnp.sum((starts[None, :] <= positions[:, None]).astype(jnp.int32), axis=1)) - 1

def silu_grad(values):
    sigmoid = jax.nn.sigmoid(values)
    return sigmoid * (1.0 + values * (1.0 - sigmoid))

def local_core(decay_c, bmat_c, cmat_c, docs_c, doc_prior):
    span = decay_c.shape[1]
    lower = jnp.arange(span)[:, None] >= jnp.arange(span)[None, :]
    triangle = lower.astype(jnp.float32)
    cums = jnp.einsum('ij,cjh->cih', triangle, decay_c, precision=HIGHEST)
    cums_t = jnp.transpose(cums, (0, 2, 1))
    same_doc = ((docs_c[:, :, None] == docs_c[:, None, :]) & lower[None])[:, None]
    cum_diff = cums_t[:, :, :, None] - cums_t[:, :, None, :]
    decay_mask = jnp.where(same_doc, jnp.exp(jnp.where(same_doc, cum_diff, 0.0)), 0.0)
    scores = jnp.einsum('cin,cjn->cij', cmat_c.astype(jnp.float32), bmat_c.astype(jnp.float32), precision=HIGHEST)
    mixing = scores[:, None] * decay_mask
    last_cums = cums[:, -1, :]
    enter_w = jnp.where((docs_c == doc_prior[:, None])[:, :, None], jnp.exp(cums), 0.0)
    end_w = jnp.where((docs_c == docs_c[:, -1:])[:, :, None], jnp.exp(last_cums[:, None, :] - cums), 0.0)
    carry_w = jnp.where((docs_c[:, -1] == doc_prior)[:, None], jnp.exp(last_cums), 0.0)
    return (triangle, decay_mask, scores, mixing, enter_w, end_w, carry_w)

def local_grads(core, scaled_c, bmat32, cmat32, entering, state_next, grad_ssd, inter_out):
    triangle, decay_mask, scores, mixing, enter_w, end_w, carry_w = core
    state_bmat = jnp.einsum('chpn,cjn->cjhp', state_next, bmat32, precision=HIGHEST)
    grad_scaled = jnp.einsum('chij,cihp->cjhp', mixing, grad_ssd, precision=HIGHEST) + end_w[..., None] * state_bmat
    pair_dots = jnp.einsum('cihp,cjhp->chij', grad_ssd, scaled_c, precision=HIGHEST)
    weighted = decay_mask * pair_dots
    grad_scores = lax.optimization_barrier(jnp.sum(weighted, axis=1))
    weighted_scores = scores[:, None] * weighted
    enter_grad = enter_w[..., None] * grad_ssd
    grad_cmat = jnp.einsum('cij,cjn->cin', grad_scores, bmat32, precision=HIGHEST) + jnp.einsum('cihp,chpn->cin', enter_grad, entering, precision=HIGHEST)
    grad_bmat = jnp.einsum('cij,cin->cjn', grad_scores, cmat32, precision=HIGHEST) + jnp.einsum('cjhp,chpn->cjn', end_w[..., None] * scaled_c, state_next, precision=HIGHEST)
    grad_cums = jnp.transpose(lax.optimization_barrier(jnp.sum(weighted_scores, axis=3)) - lax.optimization_barrier(jnp.sum(weighted_scores, axis=2)), (0, 2, 1)) + lax.optimization_barrier(jnp.sum(grad_ssd * inter_out, axis=3))
    end_terms = end_w * lax.optimization_barrier(jnp.sum(scaled_c * state_bmat, axis=3))
    closing = lax.optimization_barrier(jnp.sum(end_terms, axis=1)) + carry_w * lax.optimization_barrier(jnp.sum(state_next * entering, axis=(2, 3)))
    span = triangle.shape[0]
    final_row = (jnp.arange(span) == span - 1).astype(jnp.float32)
    grad_cums = grad_cums - end_terms + final_row[None, :, None] * closing[:, None, :]
    grad_decay = jnp.einsum('ij,cih->cjh', triangle, grad_cums, precision=HIGHEST)
    return (grad_scaled, grad_decay, grad_bmat, grad_cmat)

def chain_states(carry_w, end_states, state_in):

    def step_fn(carried, element):
        factor, added = element
        return (factor[:, None, None] * carried + added, carried)
    state_out, entering = lax.scan(step_fn, state_in, (carry_w, end_states))
    return (entering, state_out)

def chain_grads(carry_w, back_terms, state_after):

    def step_fn(carried, element):
        factor, added = element
        return (factor[:, None, None] * carried + added, carried)
    state_before, state_next = lax.scan(step_fn, state_after, (carry_w, back_terms), reverse=True)
    return (state_next, state_before)

def span_front(rows, first_pos, state_in, tail, params, starts):
    in_gain, proj_gate, proj_inner, proj_bcoef, proj_step, conv_w, conv_b, step_bias, decay_log, skip_gain, norm_gain, proj_out = params
    length = rows.shape[0]
    tap_count = conv_w.shape[0]
    rim_rows = tap_count - 1
    rows32 = rows.astype(jnp.float32)
    in_scale = lax.rsqrt(lax.optimization_barrier(jnp.mean(rows32 * rows32, axis=1)) + EPSILON)
    normed = (rows32 * in_scale[:, None] * in_gain.astype(jnp.float32)).astype(jnp.bfloat16)
    gate_raw = jnp.dot(normed, proj_gate, preferred_element_type=jnp.float32)
    inner_raw = jnp.dot(normed, proj_inner, preferred_element_type=jnp.float32)
    bcoef_raw = jnp.dot(normed, proj_bcoef, preferred_element_type=jnp.float32)
    step_raw = jnp.dot(normed, proj_step, preferred_element_type=jnp.float32)
    conv_vals = jnp.concatenate([inner_raw, bcoef_raw], axis=1)
    conv_ext = jnp.concatenate([tail, conv_vals], axis=0)
    positions = first_pos + jnp.arange(length, dtype=jnp.int32)
    doc_ids = doc_index(positions, starts)
    tap_masks = jnp.stack([(doc_index(positions - rim_rows + tap_index, starts) == doc_ids).astype(jnp.float32) for tap_index in range(tap_count)])
    conv_pre = conv_b + sum((conv_w[tap_index] * conv_ext[tap_index:tap_index + length] * tap_masks[tap_index][:, None] for tap_index in range(tap_count)))
    conv_act = jax.nn.silu(conv_pre)
    inner_width = proj_inner.shape[1]
    head_count = step_bias.shape[0]
    head_width = inner_width // head_count
    state_width = proj_bcoef.shape[1] // 2
    inner_act = conv_act[:, :inner_width]
    bcoef = conv_act[:, inner_width:].astype(jnp.bfloat16)
    step_size = jax.nn.softplus(step_raw + step_bias)
    rates = jnp.exp(decay_log)
    token_decay = -rates * step_size
    inner_heads = inner_act.reshape(length, head_count, head_width)
    scaled = step_size[:, :, None] * inner_heads
    piece_count = length // BLOCK
    scaled_c = scaled.reshape(piece_count, BLOCK, head_count, head_width)
    decay_c = token_decay.reshape(piece_count, BLOCK, head_count)
    bmat_c = bcoef[:, :state_width].reshape(piece_count, BLOCK, state_width)
    cmat_c = bcoef[:, state_width:].reshape(piece_count, BLOCK, state_width)
    docs_c = doc_ids.reshape(piece_count, BLOCK)
    doc_before = doc_index(jnp.reshape(first_pos - 1, (1,)).astype(jnp.int32), starts)
    doc_prior = jnp.concatenate([doc_before, docs_c[:-1, -1]])
    core = local_core(decay_c, bmat_c, cmat_c, docs_c, doc_prior)
    mixing, enter_w, end_w, carry_w = (core[3], core[4], core[5], core[6])
    bmat32 = bmat_c.astype(jnp.float32)
    cmat32 = cmat_c.astype(jnp.float32)
    intra_out = jnp.einsum('chij,cjhp->cihp', mixing, scaled_c, precision=HIGHEST)
    end_states = jnp.einsum('cjhp,cjn->chpn', end_w[..., None] * scaled_c, bmat32, precision=HIGHEST)
    entering, state_out = chain_states(carry_w, end_states, state_in)
    inter_out = enter_w[..., None] * jnp.einsum('chpn,cin->cihp', entering, cmat32, precision=HIGHEST)
    ssd_out = (intra_out + inter_out).reshape(length, head_count, head_width) + skip_gain[None, :, None] * inner_heads
    ssd_flat = ssd_out.reshape(length, inner_width)
    gate_act = jax.nn.silu(gate_raw)
    gated = ssd_flat * gate_act
    gated_rms = lax.rsqrt(lax.optimization_barrier(jnp.mean(gated * gated, axis=1)) + EPSILON)
    gated_norm = (gated * gated_rms[:, None] * norm_gain).astype(jnp.bfloat16)
    mixed = jnp.dot(gated_norm, proj_out, preferred_element_type=jnp.float32)
    block_out = (rows32 + mixed).astype(jnp.bfloat16)
    return {'rows32': rows32, 'in_scale': in_scale, 'normed': normed, 'gate_raw': gate_raw, 'step_raw': step_raw, 'conv_vals': conv_vals, 'conv_ext': conv_ext, 'tap_masks': tap_masks, 'conv_pre': conv_pre, 'inner_heads': inner_heads, 'step_size': step_size, 'rates': rates, 'scaled_c': scaled_c, 'bmat32': bmat32, 'cmat32': cmat32, 'core': core, 'entering': entering, 'inter_out': inter_out, 'ssd_flat': ssd_flat, 'gate_act': gate_act, 'gated': gated, 'gated_rms': gated_rms, 'gated_norm': gated_norm, 'block_out': block_out, 'state_out': state_out}

def span_back(front, cot, state_after, rim_after, params):
    in_gain, proj_gate, proj_inner, proj_bcoef, proj_step, conv_w, conv_b, step_bias, decay_log, skip_gain, norm_gain, proj_out = params
    rows32 = front['rows32']
    length = rows32.shape[0]
    tap_count = conv_w.shape[0]
    rim_rows = tap_count - 1
    inner_width = proj_inner.shape[1]
    head_count = step_bias.shape[0]
    head_width = inner_width // head_count
    state_width = proj_bcoef.shape[1] // 2
    piece_count = length // BLOCK
    gated, gated_rms, gate_act = (front['gated'], front['gated_rms'], front['gate_act'])
    cot32 = cot.astype(jnp.float32)
    grad_proj_out = jnp.dot(front['gated_norm'].T, cot, preferred_element_type=jnp.float32)
    grad_norm = jnp.dot(cot, proj_out.T, preferred_element_type=jnp.float32)
    grad_scaled_norm = norm_gain * grad_norm
    gate_dot = lax.optimization_barrier(jnp.sum(grad_scaled_norm * gated, axis=1))
    grad_gated = gated_rms[:, None] * grad_scaled_norm - gated * (gated_rms ** 3 * gate_dot / inner_width)[:, None]
    grad_norm_gain = lax.optimization_barrier(jnp.sum(grad_norm * gated * gated_rms[:, None], axis=0))
    grad_flat = grad_gated * gate_act
    grad_gate = grad_gated * front['ssd_flat'] * silu_grad(front['gate_raw'])
    grad_ssd = grad_flat.reshape(length, head_count, head_width)
    inner_heads = front['inner_heads']
    grad_skip_gain = lax.optimization_barrier(jnp.sum(grad_ssd * inner_heads, axis=(0, 2)))
    grad_ssd_c = grad_ssd.reshape(piece_count, BLOCK, head_count, head_width)
    core = front['core']
    enter_w, carry_w = (core[4], core[6])
    enter_grad = enter_w[..., None] * grad_ssd_c
    back_terms = jnp.einsum('cihp,cin->chpn', enter_grad, front['cmat32'], precision=HIGHEST)
    state_next, state_before = chain_grads(carry_w, back_terms, state_after)
    grad_scaled_c, grad_decay_c, grad_bmat, grad_cmat = local_grads(core, front['scaled_c'], front['bmat32'], front['cmat32'], front['entering'], state_next, grad_ssd_c, front['inter_out'])
    grad_scaled = grad_scaled_c.reshape(length, head_count, head_width)
    grad_decay = grad_decay_c.reshape(length, head_count)
    step_size, rates = (front['step_size'], front['rates'])
    grad_heads = step_size[:, :, None] * grad_scaled + skip_gain[None, :, None] * grad_ssd
    grad_step = lax.optimization_barrier(jnp.sum(grad_scaled * inner_heads, axis=2)) - rates * grad_decay
    grad_decay_log = -lax.optimization_barrier(jnp.sum(rates * step_size * grad_decay, axis=0))
    grad_step_raw = grad_step * jax.nn.sigmoid(front['step_raw'] + step_bias)
    grad_step_bias = lax.optimization_barrier(jnp.sum(grad_step_raw, axis=0))
    grad_act = jnp.concatenate([grad_heads.reshape(length, inner_width), grad_bmat.reshape(length, state_width), grad_cmat.reshape(length, state_width)], axis=1)
    grad_pre = grad_act * silu_grad(front['conv_pre'])
    grad_conv_b = lax.optimization_barrier(jnp.sum(grad_pre, axis=0))
    conv_ext, tap_masks = (front['conv_ext'], front['tap_masks'])
    grad_conv_w = jnp.stack([lax.optimization_barrier(jnp.sum(grad_pre * conv_ext[tap_index:tap_index + length] * tap_masks[tap_index][:, None], axis=0)) for tap_index in range(tap_count)])
    grad_ext = sum((jnp.pad(conv_w[tap_index] * grad_pre * tap_masks[tap_index][:, None], ((tap_index, rim_rows - tap_index), (0, 0))) for tap_index in range(tap_count)))
    rim_before = grad_ext[:rim_rows]
    grad_vals = grad_ext[rim_rows:] + jnp.pad(rim_after, ((length - rim_rows, 0), (0, 0)))
    gate_b16 = grad_gate.astype(jnp.bfloat16)
    inner_b16 = grad_vals[:, :inner_width].astype(jnp.bfloat16)
    bcoef_b16 = grad_vals[:, inner_width:].astype(jnp.bfloat16)
    step_b16 = grad_step_raw.astype(jnp.bfloat16)
    normed = front['normed']
    grad_proj_gate = jnp.dot(normed.T, gate_b16, preferred_element_type=jnp.float32)
    grad_proj_inner = jnp.dot(normed.T, inner_b16, preferred_element_type=jnp.float32)
    grad_proj_bcoef = jnp.dot(normed.T, bcoef_b16, preferred_element_type=jnp.float32)
    grad_proj_step = jnp.dot(normed.T, step_b16, preferred_element_type=jnp.float32)
    grad_normed = jnp.dot(gate_b16, proj_gate.T, preferred_element_type=jnp.float32) + jnp.dot(inner_b16, proj_inner.T, preferred_element_type=jnp.float32) + jnp.dot(bcoef_b16, proj_bcoef.T, preferred_element_type=jnp.float32) + jnp.dot(step_b16, proj_step.T, preferred_element_type=jnp.float32)
    in_scale = front['in_scale']
    grad_in_scaled = in_gain.astype(jnp.float32) * grad_normed
    in_dot = lax.optimization_barrier(jnp.sum(grad_in_scaled * rows32, axis=1))
    grad_rows = in_scale[:, None] * grad_in_scaled - rows32 * (in_scale ** 3 * in_dot / rows32.shape[1])[:, None]
    grad_in_gain = lax.optimization_barrier(jnp.sum(grad_normed * rows32 * in_scale[:, None], axis=0))
    input_grad = cot32 + grad_rows
    grads = (grad_in_gain, grad_proj_gate, grad_proj_inner, grad_proj_bcoef, grad_proj_step, grad_conv_w, grad_conv_b, grad_step_bias, grad_decay_log, grad_skip_gain, grad_norm_gain, grad_proj_out)
    return (grads, input_grad, state_before, rim_before)

def reference(block_in, in_gain, proj_gate, proj_inner, proj_bcoef, proj_step, conv_inner, conv_inner_bias, conv_bcoef, conv_bcoef_bias, step_bias, decay_log, skip_gain, norm_gain, proj_out, out_grad, doc_starts):
    conv_w = jnp.concatenate([conv_inner, conv_bcoef], axis=1)
    conv_b = jnp.concatenate([conv_inner_bias, conv_bcoef_bias], axis=0)
    params = (in_gain, proj_gate, proj_inner, proj_bcoef, proj_step, conv_w, conv_b, step_bias, decay_log, skip_gain, norm_gain, proj_out)
    span_count = TOKENS // TOK_DEV
    rows_in = block_in.reshape(span_count, TOK_DEV, D)
    cots = out_grad.reshape(span_count, TOK_DEV, D)
    firsts = jnp.arange(span_count, dtype=jnp.int32) * TOK_DEV
    channels = INNER + 2 * STATE
    state_zero = jnp.zeros((HEADS, HEAD_DIM, STATE), jnp.float32)
    tail_zero = jnp.zeros((CONV - 1, channels), jnp.float32)

    def front_step(carried, element):
        state_in, tail = carried
        rows, first_pos = element
        front = span_front(rows, first_pos, state_in, tail, params, doc_starts)
        return ((front['state_out'], front['conv_vals'][TOK_DEV - (CONV - 1):]), (front['block_out'], state_in, tail))
    unused, (outs, states_in, tails) = lax.scan(front_step, (state_zero, tail_zero), (rows_in, firsts))
    zero_grads = tuple((jnp.zeros(param.shape, jnp.float32) for param in params))

    def back_step(carried, element):
        state_after, rim_after, totals = carried
        rows, cot, first_pos, state_in, tail = element
        front = span_front(rows, first_pos, state_in, tail, params, doc_starts)
        grads, input_rows, state_before, rim_before = span_back(front, cot, state_after, rim_after, params)
        totals = tuple((left_term + right_term for left_term, right_term in zip(totals, grads)))
        return ((state_before, rim_before, totals), input_rows)
    (unused_state, unused_rim, totals), in_grads = lax.scan(back_step, (state_zero, tail_zero, zero_grads), (rows_in, cots, firsts, states_in, tails), reverse=True)
    g_in_gain, g_gate, g_inner, g_bcoef, g_step, g_conv_w, g_conv_b, g_step_bias, g_decay_log, g_skip, g_norm_gain, g_out = totals
    return (outs.reshape(TOKENS, D), in_grads.reshape(TOKENS, D), g_in_gain, g_gate, g_inner, g_bcoef, g_step, g_conv_w[:, :INNER], g_conv_w[:, INNER:], g_conv_b[:INNER], g_conv_b[INNER:], g_step_bias, g_decay_log, g_skip, g_norm_gain, g_out)
```

```python
import functools

import jax
import jax.numpy as jnp
from jax import lax
from jax.experimental import pallas as pl
from jax.experimental.pallas import tpu as pltpu
from jax.sharding import PartitionSpec as P

Q = 256
EPSILON = 1e-05
F32 = jnp.float32
B16 = jnp.bfloat16


def nn(a, b):
    return lax.dot_general(a, b, (((1,), (0,)), ((), ())), preferred_element_type=F32)


def nt(a, b):
    return lax.dot_general(a, b, (((1,), (1,)), ((), ())), preferred_element_type=F32)


def tn(a, b):
    return lax.dot_general(a, b, (((0,), (0,)), ((), ())), preferred_element_type=F32)


def split(a):
    high = a.astype(B16)
    return high, (a - high.astype(F32))


def exact_dot(ones, a):
    high, rest = split(a)
    mid, rest = split(rest)
    return nn(ones, high) + nn(ones, mid) + nn(ones, rest.astype(B16))


def two_dot(a, ones):
    high, rest = split(a)
    return nn(high, ones) + nn(rest.astype(B16), ones)


def iota(shape, dim):
    return lax.broadcasted_iota(jnp.int32, shape, dim)


def head_map(channels, width):
    return (iota((channels, 128), 0) // width == iota((channels, 128), 1)).astype(F32)


def expand(a, heads):
    low = iota((a.shape[0], 128), 1) < 64
    pieces = [
        jnp.where(low, a[:, 2 * i : 2 * i + 1], a[:, 2 * i + 1 : 2 * i + 2])
        for i in range(heads // 2)
    ]
    return jnp.concatenate(pieces, axis=1)


def softplus(a):
    return jnp.maximum(a, 0.0) + jnp.log1p(jnp.exp(-jnp.abs(a)))


def silu(a):
    return a * jax.nn.sigmoid(a)


def silu_grad(a):
    sig = jax.nn.sigmoid(a)
    return sig * (1.0 + a * (1.0 - sig))


def column(row, hmap):
    return jnp.sum(hmap * row, axis=1, keepdims=True)


def triangle(lower):
    row, col = iota((Q, Q), 0), iota((Q, Q), 1)
    keep = (row >= col) if lower else (col >= row)
    return keep.astype(F32).astype(B16)


def rms_scale(x):
    return lax.rsqrt(jnp.mean(x * x, axis=1, keepdims=True) + EPSILON)


def enter_end(cums, tok):
    last = cums[Q - 1 : Q, :]
    enter = jnp.exp(cums) * tok[:, 3:4]
    end = jnp.exp(last - cums) * tok[:, 4:5]
    carry = jnp.exp(last) * tok[Q - 1 : Q, 3:4]
    return enter, end, carry


def front_kernel(
    heads, x, halo, gain, w_in, w_bt, w_s, taps, hp, tok,
    normed_o, vals_o, pre_o, bc_o, sr_o, cums_o, sent_o, dp_o, fin_o, hv_o,
    ext, state, prod,
):
    c = pl.program_id(0)
    inner = w_in.shape[1]
    full = ext.shape[1]

    def project(values):
        wide = values.astype(F32)
        scale = rms_scale(wide)
        normed = (wide * scale * gain[...]).astype(B16)
        return normed, scale

    @pl.when(c == 0)
    def _():
        hn, _ = project(halo[...])
        ext[0:8, 0:inner] = nn(hn, w_in[...])
        ext[0:8, inner:full] = nt(hn, w_bt[...])
        hv_o[...] = ext[0:8, :]
        state[...] = jnp.zeros_like(state)
        prod[...] = jnp.ones_like(prod)

    @pl.when(c > 0)
    def _():
        ext[0:8, :] = ext[Q : Q + 8, :]

    normed, scale = project(x[...])
    normed_o[...] = normed
    ext[8 : Q + 8, 0:inner] = nn(normed, w_in[...])
    ext[8 : Q + 8, inner:full] = nt(normed, w_bt[...])
    vals_o[...] = ext[8 : Q + 8, :]
    t = tok[...]
    pre = taps[4:5, :] + taps[3:4, :] * ext[8 : Q + 8, :]
    for k in range(3):
        pre = pre + taps[k : k + 1, :] * ext[5 + k : 5 + k + Q, :] * t[:, k : k + 1]
    pre_o[...] = pre
    act = silu(pre)
    bc = act[:, inner:].astype(B16)
    bc_o[...] = bc
    sr = nn(normed, w_s[...]) + hp[0:1, :]
    sr_o[...] = jnp.where(iota((Q, 128), 1) == 127, scale, sr)
    step = softplus(sr)
    cums = exact_dot(triangle(True), -hp[1:2, :] * step)
    cums_o[...] = cums
    _, end, carry = enter_end(cums, t)
    hmap = head_map(inner, inner // heads)
    sent_o[0] = state[...]
    dp_o[0] = prod[...]
    x16 = (expand(step * end, heads) * act[:, :inner]).astype(B16)
    state[...] = column(carry, hmap) * state[...] + tn(x16, bc[:, :128])
    prod[...] = prod[...] * carry
    fin_o[0:inner, :] = state[...]
    fin_o[inner : inner + 8, :] = prod[...]


def causal(tok, docrow):
    return (iota((Q, Q), 0) >= iota((Q, Q), 1)) & (tok[:, 5:6] == docrow[0:1, :])


def intra_kernel(heads, normed, w_gate, pre, bc, sr, cums, tok, docrow, hp, gate_o, y_o):
    gate_o[...] = nn(normed[...], w_gate[...])
    act = silu(pre[...])
    width = act.shape[1] // heads
    scaled = (expand(softplus(sr[...]), heads) * act).astype(B16)
    scores = nt(bc[:, 128:], bc[:, :128])
    mask = causal(tok[...], docrow[...])
    cum = cums[...]
    cum_t = cum.T
    outs = []
    for h in range(heads):
        diff = cum[:, h : h + 1] - cum_t[h : h + 1, :]
        mix = (scores * jnp.where(mask, jnp.exp(diff), 0.0)).astype(B16)
        outs.append(nn(mix, scaled[:, h * width : (h + 1) * width]))
    skip = expand(jnp.broadcast_to(hp[2:3, :], (8, 128)), heads)[0:1, :]
    y_o[...] = jnp.concatenate(outs, axis=1) + skip * act


def join_kernel(
    heads, y, gate, bc, cums, tok, sent, dp, s_in, cot, w_out, ngain,
    ssd_o, inter_o, gn_o, stats_o,
):
    inner = y.shape[1]
    hmap = head_map(inner, inner // heads)
    enter, _, _ = enter_end(cums[...], tok[...])
    entering = sent[0] + column(dp[0, 0:1, :], hmap) * s_in[0:inner, :]
    inter = expand(enter, heads) * nt(bc[:, 128:], entering.astype(B16))
    inter_o[...] = inter
    ssd = y[...] + inter
    ssd_o[...] = ssd
    gated = ssd * silu(gate[...])
    gn = nt(cot[...], w_out[...])
    gn_o[...] = gn
    lane = iota((inner, 128), 1)
    first = (lane == 0).astype(F32).astype(B16)
    second = (lane == 1).astype(F32).astype(B16)
    both = two_dot(gated * gated, first) + two_dot(ngain[...] * gn * gated, second)
    stats_o[...] = both.T[0:8, :]


def gate_kernel(
    heads, width_all, ssd, gate, gn, stats, ngain, pre, bc, cums, tok,
    norm_o, gate_o, gs_o, sums_o, sb_o, db_o, fin_o,
    state, prod,
):
    i = pl.program_id(0)
    inner = ssd.shape[1]
    hmap = head_map(inner, inner // heads)

    @pl.when(i == 0)
    def _():
        state[...] = jnp.zeros_like(state)
        prod[...] = jnp.ones_like(prod)
        sums_o[...] = jnp.zeros_like(sums_o)

    st = stats[...].T
    rms = lax.rsqrt(st[:, 0:1] / width_all + EPSILON)
    pull = rms * rms * rms * st[:, 1:2] / width_all
    g = gate[...]
    sig = jax.nn.sigmoid(g)
    s = ssd[...]
    gated = s * (g * sig)
    norm_o[...] = (gated * rms * ngain[...]).astype(B16)
    gn_ = gn[...]
    grad_gated = rms * (ngain[...] * gn_) - gated * pull
    gs = grad_gated * (g * sig)
    gs_o[...] = gs
    gate_o[...] = (grad_gated * s * (sig * (1.0 + g * (1.0 - sig)))).astype(B16)
    act = silu(pre[...])
    sums_o[0:1, :] += jnp.sum(gn_ * gated * rms, axis=0, keepdims=True)
    sums_o[1:2, :] += jnp.sum(gs * act, axis=0, keepdims=True)
    enter, _, carry = enter_end(cums[...], tok[...])
    back = tn((expand(enter, heads) * gs).astype(B16), bc[:, 128:])
    sb_o[0] = state[...]
    db_o[0] = prod[...]
    state[...] = column(carry, hmap) * state[...] + back
    prod[...] = prod[...] * carry
    fin_o[0:inner, :] = state[...]
    fin_o[inner : inner + 8, :] = prod[...]


def intra_back_kernel(
    heads, gs, pre, bc, sr, cums, tok, docrow, sent, dp, s_in, gsc_o, rc_o, gbc_o
):
    inner = gs.shape[1]
    width = inner // heads
    hmap = head_map(inner, width)
    act = silu(pre[...])
    scaled = (expand(softplus(sr[...]), heads) * act).astype(B16)
    grad = gs[...]
    g16 = grad.astype(B16)
    bmat, cmat = bc[:, :128], bc[:, 128:]
    scores = nt(cmat, bmat)
    mask = causal(tok[...], docrow[...])
    cum = cums[...]
    cum_t = cum.T
    total = jnp.zeros((Q, Q), F32)
    rows, cols, outs = [], [], []
    for h in range(heads):
        part = slice(h * width, (h + 1) * width)
        decay = jnp.where(mask, jnp.exp(cum[:, h : h + 1] - cum_t[h : h + 1, :]), 0.0)
        weighted = decay * nt(g16[:, part], scaled[:, part])
        total = total + weighted
        ws = scores * weighted
        rows.append(jnp.sum(ws, axis=1, keepdims=True))
        cols.append(jnp.sum(ws, axis=0, keepdims=True))
        outs.append(tn((scores * decay).astype(B16), g16[:, part]))
    gsc_o[...] = jnp.concatenate(outs, axis=1)
    cols = jnp.concatenate(cols + [jnp.zeros((8 - heads, Q), F32)], axis=0).T
    lane = iota((Q, 128), 1)
    rc = jnp.zeros((Q, 128), F32)
    for h in range(heads):
        rc = jnp.where(lane == h, rows[h] - cols[:, h : h + 1], rc)
    rc_o[...] = rc
    enter, _, _ = enter_end(cum, tok[...])
    entering = sent[0] + column(dp[0, 0:1, :], hmap) * s_in[0:inner, :]
    t16 = total.astype(B16)
    gbc_o[:, :128] = tn(t16, cmat)
    gbc_o[:, 128:] = nn(t16, bmat) + nn(
        (expand(enter, heads) * grad).astype(B16), entering.astype(B16)
    )


def conv_back(i, count, gp, tok, taps, vals, hv, ext, mext, shift, sums_o, rim_o):
    ch = gp.shape[1]

    @pl.when(i == 0)
    def _():
        ext[Q : Q + 8, :] = jnp.zeros((8, ch), F32)
        mext[Q : Q + 8, :] = jnp.zeros((8, 8), F32)
        sums_o[...] = jnp.zeros_like(sums_o)

    @pl.when(i > 0)
    def _():
        ext[Q : Q + 8, :] = ext[0:8, :]
        mext[Q : Q + 8, :] = mext[0:8, :]

    ext[0:Q, :] = gp
    mext[0:Q, :] = tok
    out = jnp.zeros((Q, ch), F32)
    for k in range(4):
        z = ext[3 - k : 3 - k + Q, :]
        if k < 3:
            z = z * mext[3 - k : 3 - k + Q, k : k + 1]
        out = out + taps[k : k + 1, :] * z
        sums_o[k : k + 1, :] += jnp.sum(vals * z, axis=0, keepdims=True)
    sums_o[4:5, :] += jnp.sum(gp, axis=0, keepdims=True)

    @pl.when(i == count - 1)
    def _():
        rim = jnp.zeros((8, ch), F32)
        shift[0:8, :] = jnp.zeros((8, ch), F32)
        for k in range(3):
            shift[8:16, :] = ext[0:8, :] * mext[0:8, k : k + 1]
            moved = shift[3 - k : 11 - k, :]
            rim = rim + taps[k : k + 1, :] * moved
            sums_o[k : k + 1, :] += jnp.sum(hv * moved, axis=0, keepdims=True)
        rim_o[...] = rim

    return out


def bcoef_back_kernel(
    heads, count, gbc, pre, vals, sr, cums, tok, sb, db, s_after, taps, hv,
    pack_o, rim_o, sums_o, ext, mext, shift,
):
    i = pl.program_id(0)
    inner = pre.shape[1] - 256
    hmap = head_map(inner, inner // heads)
    act = silu(pre[:, :inner])
    _, end, _ = enter_end(cums[...], tok[...])
    after = sb[0] + column(db[0, 0:1, :], hmap) * s_after[0:inner, :]
    x16 = (expand(softplus(sr[...]) * end, heads) * act).astype(B16)
    gbm = gbc[:, :128] + nn(x16, after.astype(B16))
    gp = jnp.concatenate([gbm, gbc[:, 128:]], axis=1) * silu_grad(pre[:, inner:])
    out = conv_back(
        i, count, gp, tok[...], taps[:, inner:], vals[:, inner:], hv[:, inner:],
        ext, mext, shift, sums_o, rim_o,
    ).astype(B16)
    own = pack_o.shape[0]
    span = 256 // own
    half = Q // 2
    for v in range(own):
        piece = out[:, v * span : (v + 1) * span]
        pack_o[v] = jnp.concatenate([piece[:half], piece[half:]], axis=1)


def inner_back_kernel(
    heads, count, gs, gsc, rc, inter, pre, vals, bc, sr, cums, tok, sent, dp, s_in,
    sb, db, s_after, taps, hp, hv,
    gv_o, step_o, rim_o, sums_o, small_o, ext, mext, shift,
):
    i = pl.program_id(0)
    inner = gs.shape[1]
    hmap = head_map(inner, inner // heads)
    hmap16 = hmap.astype(B16)
    cum = cums[...]
    t = tok[...]
    _, end, carry = enter_end(cum, t)
    entering = sent[0] + column(dp[0, 0:1, :], hmap) * s_in[0:inner, :]
    after = sb[0] + column(db[0, 0:1, :], hmap) * s_after[0:inner, :]
    p = pre[...]
    act = silu(p)
    s = sr[...]
    step = softplus(s)
    step_x = expand(step, heads)
    grad = gs[...]
    state_b = nt(bc[:, :128], after.astype(B16))
    gsc_ = gsc[...] + expand(end, heads) * state_b
    end_terms = end * two_dot(step_x * act * state_b, hmap16)
    across = jnp.sum(
        hmap * jnp.sum(after * entering, axis=1, keepdims=True), axis=0, keepdims=True
    )
    closing = jnp.sum(end_terms, axis=0, keepdims=True) + carry * across
    lane_ok = iota((Q, 128), 1) < heads
    grad_cums = rc[...] + two_dot(grad * inter[...], hmap16) - end_terms
    grad_cums = grad_cums + jnp.where(iota((Q, 128), 0) == Q - 1, closing, 0.0)
    grad_cums = jnp.where(lane_ok, grad_cums, 0.0)
    grad_decay = exact_dot(triangle(False), grad_cums)
    rates = hp[1:2, :]
    grad_step = two_dot(gsc_ * act, hmap16) - rates * grad_decay
    raw = grad_step * jax.nn.sigmoid(s)
    step_o[...] = raw.astype(B16)

    @pl.when(i == 0)
    def _():
        small_o[...] = jnp.zeros_like(small_o)

    small_o[0:1, :] += jnp.sum(raw, axis=0, keepdims=True)
    small_o[1:2, :] -= jnp.sum(rates * step * grad_decay, axis=0, keepdims=True)
    skip = expand(jnp.broadcast_to(hp[2:3, :], (8, 128)), heads)[0:1, :]
    gp = (step_x * gsc_ + skip * grad) * silu_grad(p)
    gv_o[...] = conv_back(
        i, count, gp, t, taps[...], vals[...], hv[...], ext, mext, shift, sums_o, rim_o
    )


def mixed_kernel(count, place, gnorm, w_out, cot, normed, gate16, mix_o, grads_o, acc_g, acc_o):
    i = pl.program_id(0)
    inner = gnorm.shape[1]

    @pl.when(i == 0)
    def _():
        acc_g[...] = jnp.zeros_like(acc_g)
        acc_o[...] = jnp.zeros_like(acc_o)

    mix_o[0] = nn(gnorm[...], w_out[...]).astype(B16)
    acc_g[...] += tn(normed[...], gate16[...])
    acc_o[...] += tn(gnorm[...], cot[...])

    @pl.when(i == count - 1)
    def _():
        grads_o[:, 0:inner] = acc_g[...].astype(B16)
        grads_o[0:inner, inner:] = acc_o[:, 0:inner].astype(B16)
        grads_o[inner:, inner:] = acc_o[:, inner:].astype(B16)


def inner_grads_kernel(
    count, gv, rim, gate16, step16, normed, w_in, w_gate, w_s, part_o, grads_o, acc
):
    i = pl.program_id(0)

    @pl.when(i == 0)
    def _():
        acc[...] = jnp.zeros_like(acc)

    v = gv[...]
    tail = jnp.where(i == count - 1, rim[...], 0.0)
    v = jnp.concatenate([v[: Q - 8], v[Q - 8 :] + tail], axis=0)
    v16 = v.astype(B16)
    part_o[...] = nt(v16, w_in[...]) + nt(gate16[...], w_gate[...]) + nt(step16[...], w_s[...])
    acc[...] += tn(normed[...], v16)

    @pl.when(i == count - 1)
    def _():
        grads_o[...] = acc[...].astype(B16)


def bcoef_grads_kernel(
    count, others, place, *refs
):
    packs = refs[: others + 1]
    (rim, part, normed, x, sr, w_bt, step16, part_o, grads_o, gain_o, acc) = refs[
        others + 1 :
    ]
    i = pl.program_id(0)

    @pl.when(i == 0)
    def _():
        acc[...] = jnp.zeros_like(acc)
        gain_o[...] = jnp.zeros_like(gain_o)

    packed = packs[0][...].astype(F32)
    for extra in packs[1:]:
        packed = packed + extra[...].astype(F32)
    span = w_bt.shape[0]
    v = jnp.concatenate([packed[:, :span], packed[:, span:]], axis=0)
    tail = jnp.where(i == count - 1, rim[...], 0.0)
    v = jnp.concatenate([v[: Q - 8], v[Q - 8 :] + tail], axis=0)
    v16 = v.astype(B16)
    total = part[...] + nn(v16, w_bt[...])
    part_o[0] = total.astype(B16)
    wide = x[...].astype(F32)
    gain_o[0:1, :] += jnp.sum(total * wide * sr[:, 127:128], axis=0, keepdims=True)
    acc[...] += tn(normed[...], jnp.concatenate([v16, step16[:, :span]], axis=1))

    @pl.when(i == count - 1)
    def _():
        grads_o[...] = acc[...].astype(B16)


def last_kernel(others, x, cot, gain, *refs):
    parts = refs[: others + 1]
    out = refs[others + 1]
    total = parts[0][...].astype(F32)
    for extra in parts[1:]:
        total = total + extra[...].astype(F32)
    wide = x[...].astype(F32)
    scale = rms_scale(wide)
    scaled = gain[...] * total
    dot = jnp.sum(scaled * wide, axis=1, keepdims=True)
    width = wide.shape[1]
    out[...] = (
        cot[...].astype(F32) + scale * scaled - wide * (scale * scale * scale * dot / width)
    )


def combine_kernel(bits, keep, total, other, keep_o, total_o):
    inner = keep.shape[0] - 8
    hmap = head_map(inner, 64)
    theirs = other[...].astype(F32)
    earlier = bits[0] == 1
    t_own, t_their = total[inner : inner + 1, :], theirs[inner : inner + 1, :]
    t_keep = keep[inner : inner + 1, :]
    keep_o[0:inner, :] = keep[0:inner, :] + jnp.where(
        earlier, column(t_keep, hmap) * theirs[0:inner, :], 0.0
    )
    keep_o[inner:, :] = keep[inner:, :] * jnp.where(earlier, theirs[inner:, :], 1.0)
    total_o[0:inner, :] = jnp.where(
        earlier,
        column(t_own, hmap) * theirs[0:inner, :] + total[0:inner, :],
        column(t_their, hmap) * total[0:inner, :] + theirs[0:inner, :],
    )
    total_o[inner:, :] = total[inner:, :] * theirs[inner:, :]


def shape(dims, dtype=F32):
    return jax.ShapeDtypeStruct(dims, dtype)


def call(kernel, grid, ins, in_specs, outs, out_specs, scratch=(), scalars=(), name=None, flops=0):
    size = sum(a.size * a.dtype.itemsize for a in ins) + sum(
        o.size * o.dtype.itemsize for o in outs
    )
    return pl.pallas_call(
        kernel,
        out_shape=outs,
        grid_spec=pltpu.PrefetchScalarGridSpec(
            num_scalar_prefetch=len(scalars),
            grid=grid,
            in_specs=in_specs,
            out_specs=out_specs,
            scratch_shapes=list(scratch),
        ),
        compiler_params=pltpu.CompilerParams(dimension_semantics=("arbitrary",) * len(grid)),
        cost_estimate=pl.CostEstimate(flops=int(flops), bytes_accessed=size, transcendentals=0),
        name=name,
    )(*scalars, *ins)


def ring(value, axis, distance):
    count = lax.axis_size(axis)
    return lax.ppermute(value, axis, [(i, (i + distance) % count) for i in range(count)])


def swap(value, axis, bit):
    count = lax.axis_size(axis)
    return lax.ppermute(value, axis, [(i, i ^ (1 << bit)) for i in range(count)])


def gathered(value, axis):
    count = lax.axis_size(axis)
    place = lax.axis_index(axis)
    out = jnp.zeros((count,) + value.shape, value.dtype)
    for distance in range(count):
        block = ring(value, axis, distance) if distance else value
        start = (lax.rem(place - distance + count, count),) + (0,) * value.ndim
        out = lax.dynamic_update_slice(out, block[None], start)
    return out


def log2(count):
    return count.bit_length() - 1


def carried_in(fin, reverse):
    rows = fin.shape[0]
    place = lax.axis_index("seq")
    keep = jnp.concatenate([jnp.zeros((rows - 8, 128), F32), jnp.ones((8, 128), F32)], axis=0)
    total = fin
    whole = pl.BlockSpec((rows, 128), lambda i, *_: (0, 0))
    for bit in range(log2(lax.axis_size("seq"))):
        other = swap(total.astype(B16), "seq", bit)
        side = lax.rem(lax.shift_right_logical(place, bit), 2)
        side = 1 - side if reverse else side
        keep, total = call(
            combine_kernel, (1,), [keep, total, other], [whole] * 3,
            [shape((rows, 128))] * 2, [whole] * 2,
            scalars=(side.reshape((1,)).astype(jnp.int32),), name="combine",
        )
    return keep


def summed_wt(value):
    for bit in range(log2(lax.axis_size("wt"))):
        value = value + swap(value, "wt", bit)
    return value


def summed_seq(value):
    for bit in range(log2(lax.axis_size("seq"))):
        value = value + swap(value, "seq", bit)
    return value


def big_sum(value, order):
    place = lax.axis_index("seq")
    for bit in order:
        half = value.shape[0] // 2
        side = lax.rem(lax.shift_right_logical(place, bit), 2)
        send = lax.dynamic_slice_in_dim(value, (1 - side) * half, half, 0)
        own = lax.dynamic_slice_in_dim(value, side * half, half, 0)
        value = (own.astype(F32) + swap(send, "seq", bit).astype(F32)).astype(value.dtype)
    for bit in reversed(order):
        side = lax.rem(lax.shift_right_logical(place, bit), 2)
        other = swap(value, "seq", bit)
        out = jnp.zeros((value.shape[0] * 2,) + value.shape[1:], value.dtype)
        out = lax.dynamic_update_slice(out, value, (side * value.shape[0], 0))
        value = lax.dynamic_update_slice(out, other, ((1 - side) * value.shape[0], 0))
    return value


def doc_index(positions, starts):
    return jnp.sum((starts[None, :] <= positions[:, None]).astype(jnp.int32), axis=1) - 1


def per_device(
    block_in,
    in_gain,
    proj_gate,
    proj_inner,
    proj_bcoef,
    proj_step,
    conv_inner,
    conv_inner_bias,
    conv_bcoef,
    conv_bcoef_bias,
    step_bias,
    decay_log,
    skip_gain,
    norm_gain,
    proj_out,
    out_grad,
    doc_starts,
):
    n_wt, n_seq = lax.axis_size("wt"), lax.axis_size("seq")
    w = lax.axis_index("wt")
    rows_own, d = block_in.shape
    length = rows_own * n_wt
    inner = proj_inner.shape[1]
    heads = step_bias.shape[0]
    span = proj_bcoef.shape[1]
    full = inner + span * n_wt
    width_all = inner * n_wt
    count = length // Q
    place = w.reshape((1,)).astype(jnp.int32)

    rows = gathered(block_in, "wt").reshape(length, d)
    w_bt_own = proj_bcoef.T
    w_bt = gathered(w_bt_own, "wt").reshape(span * n_wt, d)
    small = jnp.zeros((8, 256), F32)
    small = lax.dynamic_update_slice(small, conv_bcoef, (0, 0))
    small = lax.dynamic_update_slice(small, conv_bcoef_bias[None], (4, 0))
    small = lax.dynamic_update_slice(small, in_gain.astype(F32)[None], (5, 0))
    small = gathered(small, "wt")
    gain = small[:, 5, : in_gain.shape[0]].reshape(1, d)
    taps_b = small[:, :, :span].transpose(1, 0, 2).reshape(8, span * n_wt)
    tail = block_in[rows_own - 8 :]
    halo = sum(
        lax.ppermute(
            tail, ("seq", "wt"),
            [((s - 1) * n_wt + n_wt - 1, s * n_wt + v) for s in range(1, n_seq)],
        )
        for v in range(n_wt)
    )
    taps_i = jnp.concatenate([conv_inner, conv_inner_bias[None], jnp.zeros((3, inner), F32)], axis=0)
    taps = jnp.concatenate([taps_i, taps_b], axis=1)
    hp = jnp.pad(
        jnp.stack([step_bias, jnp.exp(decay_log), skip_gain]), ((0, 5), (0, 128 - heads))
    )
    w_s = jnp.pad(proj_step, ((0, 0), (0, 128 - heads)))
    ngain = norm_gain.reshape(1, inner)

    first = lax.axis_index("seq") * length
    positions = first + jnp.arange(length, dtype=jnp.int32)
    docs = doc_index(positions, doc_starts)
    docs_c = docs.reshape(count, Q)
    prior = jnp.concatenate([doc_index(jnp.reshape(first - 1, (1,)), doc_starts), docs_c[:-1, -1]])
    columns = [(doc_index(positions - 3 + k, doc_starts) == docs) for k in range(3)]
    columns.append((docs_c == prior[:, None]).reshape(length))
    columns.append((docs_c == docs_c[:, -1:]).reshape(length))
    columns.append(docs)
    tok = jnp.stack([a.astype(F32) for a in columns] + [jnp.zeros((length,), F32)] * 2, axis=1)
    docrow = jnp.broadcast_to(docs.astype(F32)[None], (8, length))

    grid = (count,)

    def by_rows(width, reverse=False, lanes=0):
        if reverse:
            return pl.BlockSpec((Q, width), lambda i, *_: (count - 1 - i, lanes))
        return pl.BlockSpec((Q, width), lambda i, *_: (i, lanes))

    def whole(*dims):
        return pl.BlockSpec(dims, lambda i, *_: (0,) * len(dims))

    def by_chunk(*dims, reverse=False):
        if reverse:
            return pl.BlockSpec((1,) + dims, lambda i, *_: (count - 1 - i, 0, 0))
        return pl.BlockSpec((1,) + dims, lambda i, *_: (i, 0, 0))

    fin_rows = inner + 8
    normed, vals, pre, bc, sr, cums, sent, dp, fin, hv = call(
        functools.partial(front_kernel, heads), grid,
        [rows, halo, gain, proj_inner, w_bt, w_s, taps, hp, tok],
        [by_rows(d), whole(8, d), whole(1, d), whole(d, inner), whole(span * n_wt, d),
         whole(d, 128), whole(8, full), whole(8, 128), by_rows(8)],
        [shape((length, d), B16), shape((length, full)), shape((length, full)),
         shape((length, 256), B16), shape((length, 128)), shape((length, 128)),
         shape((count, inner, 128)), shape((count, 8, 128)), shape((fin_rows, 128)),
         shape((8, full))],
        [by_rows(d), by_rows(full), by_rows(full), by_rows(256), by_rows(128), by_rows(128),
         by_chunk(inner, 128), by_chunk(8, 128), whole(fin_rows, 128), whole(8, full)],
        scratch=[pltpu.VMEM((Q + 8, full), F32), pltpu.VMEM((inner, 128), F32),
                 pltpu.VMEM((8, 128), F32)],
        name="front", flops=2e9,
    )
    s_in = carried_in(fin, False)
    gate, y = call(
        functools.partial(intra_kernel, heads), grid,
        [normed, proj_gate, pre, bc, sr, cums, tok, docrow, hp],
        [by_rows(d), whole(d, inner), by_rows(inner), by_rows(256), by_rows(128), by_rows(128),
         by_rows(8), pl.BlockSpec((8, Q), lambda i, *_: (0, i)), whole(8, 128)],
        [shape((length, inner)), shape((length, inner))],
        [by_rows(inner), by_rows(inner)], name="intra", flops=2e9,
    )
    cot = gathered(out_grad, "wt").reshape(length, d)
    state_spec = whole(fin_rows, 128)
    ssd, inter, gn, stats = call(
        functools.partial(join_kernel, heads), grid,
        [y, gate, bc, cums, tok, sent, dp, s_in, cot, proj_out, ngain],
        [by_rows(inner), by_rows(inner), by_rows(256), by_rows(128), by_rows(8),
         by_chunk(inner, 128), by_chunk(8, 128), state_spec, by_rows(d), whole(inner, d),
         whole(1, inner)],
        [shape((length, inner))] * 3 + [shape((8, length))],
        [by_rows(inner)] * 3 + [pl.BlockSpec((8, Q), lambda i, *_: (0, i))],
        name="join", flops=2e9,
    )
    stats = summed_wt(stats)
    gnorm, gate16, gs, nsums, sb, db, back_fin = call(
        functools.partial(gate_kernel, heads, width_all), grid,
        [ssd, gate, gn, stats, ngain, pre, bc, cums, tok],
        [by_rows(inner, True)] * 3
        + [pl.BlockSpec((8, Q), lambda i, *_: (0, count - 1 - i)), whole(1, inner),
           by_rows(inner, True), by_rows(256, True), by_rows(128, True), by_rows(8, True)],
        [shape((length, inner), B16), shape((length, inner), B16), shape((length, inner)),
         shape((8, inner)), shape((count, inner, 128)), shape((count, 8, 128)),
         shape((fin_rows, 128))],
        [by_rows(inner, True)] * 3
        + [whole(8, inner), by_chunk(inner, 128, reverse=True), by_chunk(8, 128, reverse=True),
           state_spec],
        scratch=[pltpu.VMEM((inner, 128), F32), pltpu.VMEM((8, 128), F32)],
        name="gates", flops=1e9,
    )
    s_after = carried_in(back_fin, True)
    gsc, rc, gbc = call(
        functools.partial(intra_back_kernel, heads), grid,
        [gs, pre, bc, sr, cums, tok, docrow, sent, dp, s_in],
        [by_rows(inner), by_rows(inner), by_rows(256), by_rows(128), by_rows(128), by_rows(8),
         pl.BlockSpec((8, Q), lambda i, *_: (0, i)), by_chunk(inner, 128), by_chunk(8, 128),
         state_spec],
        [shape((length, inner)), shape((length, 128)), shape((length, 256))],
        [by_rows(inner), by_rows(128), by_rows(256)], name="intra_back", flops=4e9,
    )

    def turned(i, p):
        return (lax.rem(i - p[0] + count, count), 0, 0)

    mix_parts, grads_a = call(
        functools.partial(mixed_kernel, count), grid,
        [gnorm, proj_out, cot, normed, gate16],
        [by_rows(inner), whole(inner, d), by_rows(d), by_rows(d), by_rows(inner)],
        [shape((count, Q, d), B16), shape((d, 2 * inner), B16)],
        [pl.BlockSpec((1, Q, d), turned), whole(d, 2 * inner)],
        scratch=[pltpu.VMEM((d, inner), F32), pltpu.VMEM((inner, d), F32)],
        scalars=(place,), name="mixed", flops=2e9,
    )
    mixed = sum(
        (ring(mix_parts[k], "wt", k) if k else mix_parts[0]).astype(F32) for k in range(n_wt)
    )
    block_out = (block_in.astype(F32) + mixed).astype(B16)

    half = length // 2
    packed, rim_b, csum_b = call(
        functools.partial(bcoef_back_kernel, heads, count), grid,
        [gbc, pre, vals, sr, cums, tok, sb, db, s_after, taps, hv],
        [by_rows(256, True), by_rows(full, True), by_rows(full, True), by_rows(128, True),
         by_rows(128, True), by_rows(8, True), by_chunk(inner, 128, reverse=True),
         by_chunk(8, 128, reverse=True), state_spec, whole(8, full), whole(8, full)],
        [shape((n_wt, half, 128), B16), shape((8, 256)), shape((8, 256))],
        [pl.BlockSpec((n_wt, Q // 2, 128), lambda i, *_: (0, count - 1 - i, 0)), whole(8, 256),
         whole(8, 256)],
        scratch=[pltpu.VMEM((Q + 8, 256), F32), pltpu.VMEM((Q + 8, 8), F32),
                 pltpu.VMEM((16, 256), F32)],
        name="bcoef_back", flops=1e9,
    )
    packs, rims = [], []
    for k in range(n_wt):
        target = lax.rem(w + k, n_wt)
        piece = lax.dynamic_index_in_dim(packed, target, 0, False)
        packs.append(ring(piece, "wt", k) if k else piece)
        edge = lax.dynamic_slice_in_dim(rim_b, target * span, span, 1)
        pairs = [
            (s * n_wt + v, (s - 1) * n_wt + (v + k) % n_wt)
            for s in range(1, n_seq)
            for v in range(n_wt)
        ]
        rims.append(lax.ppermute(edge, ("seq", "wt"), pairs))
    rim_b_in = sum(rims)

    gv, step16, rim_i, csum_i, ssum = call(
        functools.partial(inner_back_kernel, heads, count), grid,
        [gs, gsc, rc, inter, pre, vals, bc, sr, cums, tok, sent, dp, s_in, sb, db, s_after,
         taps, hp, hv],
        [by_rows(inner, True), by_rows(inner, True), by_rows(128, True), by_rows(inner, True),
         by_rows(inner, True), by_rows(inner, True), by_rows(256, True), by_rows(128, True),
         by_rows(128, True), by_rows(8, True), by_chunk(inner, 128, reverse=True),
         by_chunk(8, 128, reverse=True), state_spec, by_chunk(inner, 128, reverse=True),
         by_chunk(8, 128, reverse=True), state_spec, whole(8, inner), whole(8, 128),
         whole(8, inner)],
        [shape((length, inner)), shape((length, 128), B16), shape((8, inner)),
         shape((8, inner)), shape((8, 128))],
        [by_rows(inner, True), by_rows(128, True), whole(8, inner), whole(8, inner),
         whole(8, 128)],
        scratch=[pltpu.VMEM((Q + 8, inner), F32), pltpu.VMEM((Q + 8, 8), F32),
                 pltpu.VMEM((16, inner), F32)],
        name="inner_back", flops=1e9,
    )
    rim_i_in = lax.ppermute(rim_i, "seq", [(s, s - 1) for s in range(1, n_seq)])
    part, grads_i = call(
        functools.partial(inner_grads_kernel, count), grid,
        [gv, rim_i_in, gate16, step16, normed, proj_inner, proj_gate, w_s],
        [by_rows(inner), whole(8, inner), by_rows(inner), by_rows(128), by_rows(d),
         whole(d, inner), whole(d, inner), whole(d, 128)],
        [shape((length, d)), shape((d, inner), B16)],
        [by_rows(d), whole(d, inner)],
        scratch=[pltpu.VMEM((d, inner), F32)], name="inner_grads", flops=2e9,
    )
    pack_spec = pl.BlockSpec((Q // 2, 128), lambda i, *_: (i, 0))
    parts, grads_b, gain_sum = call(
        functools.partial(bcoef_grads_kernel, count, n_wt - 1), grid,
        [*packs, rim_b_in, part, normed, rows, sr, w_bt_own, step16],
        [pack_spec] * n_wt
        + [whole(8, span), by_rows(d), by_rows(d), by_rows(d), by_rows(128), whole(span, d),
           by_rows(128)],
        [shape((count, Q, d), B16), shape((d, 2 * span), B16), shape((8, d))],
        [pl.BlockSpec((1, Q, d), turned), whole(d, 2 * span), whole(8, d)],
        scratch=[pltpu.VMEM((d, 2 * span), F32)],
        scalars=(place,), name="bcoef_grads", flops=1e9,
    )
    own_parts = [ring(parts[k], "wt", k) if k else parts[0] for k in range(n_wt)]
    (input_grad,) = call(
        functools.partial(last_kernel, n_wt - 1), (1,),
        [block_in, out_grad, gain, *own_parts],
        [whole(rows_own, d)] * 2 + [whole(1, d)] + [whole(rows_own, d)] * n_wt,
        [shape((rows_own, d))], [whole(rows_own, d)], name="last",
    )

    bits = log2(n_seq)
    total_a = big_sum(grads_a, list(range(bits)))
    total_i = big_sum(
        jnp.concatenate([grads_i, grads_b], axis=1),
        [0] + list(range(bits - 1, 0, -1)),
    )
    g_gate = total_a[:, :inner].astype(F32)
    g_out = jnp.concatenate([total_a[:inner, inner:], total_a[inner:, inner:]], axis=1).astype(F32)
    g_inner = total_i[:, :inner].astype(F32)
    g_bcoef = total_i[:, inner : inner + span].astype(F32)
    g_step = total_i[:, inner + span : inner + span + heads].astype(F32)
    shared = jnp.concatenate([gain_sum, jnp.pad(csum_b, ((0, 0), (0, d - 256)))], axis=0)
    local = jnp.concatenate(
        [jnp.concatenate([csum_i, jnp.pad(ssum, ((0, 0), (0, inner - 128)))], axis=1),
         jnp.pad(nsums, ((0, 0), (0, d - inner)))], axis=0)
    both = summed_seq(jnp.concatenate([shared, local], axis=0))
    shared = summed_wt(both[:16])
    g_gain = lax.dynamic_slice_in_dim(shared[0], w * in_gain.shape[0], in_gain.shape[0], 0)
    g_cb = lax.dynamic_slice_in_dim(shared[8:16], w * span, span, 1)
    g_ci, g_small, g_norm = both[16:24, :inner], both[16:24, inner:], both[24:32]
    g_skip = jnp.sum(g_norm[1, :inner].reshape(heads, inner // heads), axis=1)
    return (
        block_out,
        input_grad,
        g_gain,
        g_gate,
        g_inner,
        g_bcoef,
        g_step,
        g_ci[:4],
        g_cb[:4],
        g_ci[4],
        g_cb[4],
        g_small[0, :heads],
        g_small[1, :heads],
        g_skip,
        g_norm[0, :inner],
        g_out,
    )


def solution(mesh):
    tokens = P(("seq", "wt"), None)
    cols, vec = P(None, "wt"), P("wt")
    return jax.shard_map(
        per_device,
        mesh=mesh,
        in_specs=(
            tokens, vec, cols, cols, cols, cols, cols, vec, cols, vec, vec, vec, vec, vec,
            P("wt", None), tokens, P(),
        ),
        out_specs=(
            tokens, tokens, vec, cols, cols, cols, cols, cols, cols, vec, vec, vec, vec, vec,
            vec, P("wt", None),
        ),
        check_vma=False,
    )
```

```python
import functools

import jax
import jax.numpy as jnp
import numpy as np
from jax import lax
from jax.experimental import pallas as pl
from jax.experimental.pallas import tpu as pltpu
from jax.sharding import PartitionSpec as P

VMEM = pl.BlockSpec(memory_space=pltpu.VMEM)
LIMIT = 16 << 20
Q = 256
HALF = Q // 2
STEP, ENTER, END, CUMS, SIG = 0, 1, 2, 4, 5
EPSILON = 1e-05
F32 = jnp.float32
B16 = jnp.bfloat16


def nn(a, b):
    return lax.dot_general(a, b, (((1,), (0,)), ((), ())), preferred_element_type=F32)


def nt(a, b):
    return lax.dot_general(a, b, (((1,), (1,)), ((), ())), preferred_element_type=F32)


def tn(a, b):
    return lax.dot_general(a, b, (((0,), (0,)), ((), ())), preferred_element_type=F32)


def split(a):
    high = a.astype(B16)
    return high, (a - high.astype(F32))


def exact_dot(ones, a):
    high, rest = split(a)
    mid, rest = split(rest)
    return nn(ones, high) + nn(ones, mid) + nn(ones, rest.astype(B16))


def two_dot(a, ones):
    high, rest = split(a)
    return nn(high, ones) + nn(rest.astype(B16), ones)


def iota(shape, dim):
    return lax.broadcasted_iota(jnp.int32, shape, dim)


def softplus(a):
    return jnp.maximum(a, 0.0) + jnp.log1p(jnp.exp(-jnp.abs(a)))


def three(a, b):
    ah, al = split(a)
    bh, bl = split(b)
    return nt(ah, bh) + nt(al.astype(B16), bh) + nt(ah, bl.astype(B16))


def silu(a):
    return a * jax.nn.sigmoid(a)


def silu_grad(a):
    sig = jax.nn.sigmoid(a)
    return sig * (1.0 + a * (1.0 - sig))


def rms_scale(x):
    return lax.rsqrt(jnp.mean(x * x, axis=1, keepdims=True) + EPSILON)


def total(refs):
    out = refs[0][...].astype(F32)
    for extra in refs[1:]:
        out = out + extra[...].astype(F32)
    return out


def boundary(starts, base):
    found = False
    for k in range(starts.shape[0]):
        at = starts[k]
        found = found | ((at > 0) & (at > base - 3) & (at < base + Q + 3))
    return found


def prep_kernel(place, w_bt, conv, bias, gain, out):
    span, d = w_bt.shape
    quarter = span // 4
    side = lax.rem(lax.div(place[1], 2), 4)
    out[0:quarter, :] = w_bt[pl.ds(pl.multiple_of(side * quarter, quarter), quarter), :]
    rows = jnp.concatenate([conv[...], bias[...].reshape(1, span), jnp.zeros((11, span), F32)], axis=0)
    high, rest = split(rows)
    mid, rest = split(rest)
    wide = jnp.concatenate(
        [high.astype(F32), mid.astype(F32), rest, jnp.zeros((16, d - 3 * span), F32)], axis=1
    )
    row = jnp.concatenate(
        [gain[...].astype(F32).reshape(1, gain.shape[0]), jnp.zeros((1, d - gain.shape[0]), F32)],
        axis=1,
    )
    wide = jnp.where(iota((16, d), 0) == 5, row, wide)
    out[quarter:, :] = wide.astype(B16)


def stack_kernel(*refs):
    *ins, out = refs
    rows = out.shape[0] // len(ins)
    for k, ref in enumerate(ins):
        out[k * rows : (k + 1) * rows, :] = ref[0:rows, :]


def front_kernel(heads, n, place, starts, *refs):
    xs, halos, earlies = refs[:n], refs[n : 2 * n], refs[2 * n : 3 * n]
    bts = refs[3 * n : 3 * n + 4]
    (
        w_in, w_step, conv_i, bias_i, sbias, dlog, skips, ngain, tri, e_step, e_enter, e_end,
        normed_o, vals_o, bvals_o, pre_o, bpre_o, bc_o, pk_o, pk2_o, cumt_o, scaled_o, sent_o,
        dp_o, fin_o, hv_o, hn_o, tok_o, docrow_o, taps, gain, hp, w_s, vec,
        ext, state, prod, w_bt, x,
    ) = refs[3 * n + 4 :]
    c = pl.program_id(0)
    inner = w_in.shape[1]
    full = ext.shape[1]
    span = w_bt.shape[0] // n
    quarter = span // 4
    gain_own = gain.shape[1] // n
    w = place[0]
    side = lax.rem(lax.div(place[1], 2), 4)

    def project(values):
        wide = values.astype(F32)
        return (wide * rms_scale(wide) * gain[0:1, :]).astype(B16)

    @pl.when(c == 0)
    def _():
        taps[0:4, 0:inner] = conv_i[...]
        taps[4:5, 0:inner] = bias_i[...].reshape(1, inner)
        taps[5:8, :] = jnp.zeros((3, full), F32)
        hp[...] = jnp.zeros_like(hp)
        for g in range(16):
            lanes = slice(8 * g, 8 * g + heads)
            hp[0:1, lanes] = sbias[...].reshape(1, heads)
            hp[1:2, lanes] = jnp.exp(dlog[...].reshape(1, heads))
        low = iota((1, 128), 1) < 64
        for p in range(heads // 2):
            one, two = (jnp.broadcast_to(skips[...].reshape(1, heads)[:, h : h + 1], (1, 128)) for h in (2 * p, 2 * p + 1))
            vec[0:1, p * 128 : (p + 1) * 128] = jnp.where(low, one, two)
        vec[1:2, :] = ngain[...].reshape(1, inner)
        copies = (iota((heads, 128), 0) == lax.rem(iota((heads, 128), 1), 8)).astype(F32)
        w_s[...] = nn(w_step[...], copies.astype(B16)).astype(B16)
        for k in range(n):
            v = lax.rem(w - k + n, n)
            for q in range(4):
                at = v * span + (side ^ q) * quarter
                w_bt[pl.ds(pl.multiple_of(at, quarter), quarter), :] = bts[q][
                    k * quarter : (k + 1) * quarter, :
                ]
        for v in range(n):
            for k in range(n):

                @pl.when(lax.rem(w - v + n, n) == k)
                def _(v=v, k=k):
                    low = inner + v * span
                    small = earlies[k][quarter:, :].astype(F32)
                    taps[0:5, low : low + span] = (
                        small[0:5, 0:span] + small[0:5, span : 2 * span]
                    ) + small[0:5, 2 * span : 3 * span]
                    gain[0:1, v * gain_own : (v + 1) * gain_own] = small[5:6, 0:gain_own]

        hn = project(total(halos))
        hn_o[...] = hn
        ext[0:8, 0:inner] = nn(hn, w_in[...])
        ext[0:8, inner:full] = nt(hn, w_bt[...])
        hv_o[...] = ext[0:8, :]
        state[...] = jnp.zeros_like(state)
        prod[...] = jnp.ones_like(prod)

    @pl.when(c > 0)
    def _():
        ext[0:8, :] = ext[Q : Q + 8, :]

    for k in range(n):

        @pl.when(lax.rem(w - c + n, n) == k)
        def _(k=k):
            x[...] = xs[k][...]

    def docs_at(positions):
        found = jnp.zeros(positions.shape, jnp.int32)
        for k in range(starts.shape[0]):
            found = found + (starts[k] <= positions).astype(jnp.int32)
        return found - 1

    base = (place[1] * pl.num_programs(0) + c) * Q
    here = base + iota((Q, 8), 0)
    lane = iota((Q, 8), 1)
    other = jnp.where(lane < 3, here - 3 + lane, jnp.where(lane == 3, base - 1, base + Q - 1))
    docs = docs_at(here)
    tok = jnp.where(lane == 5, docs, (docs_at(other) == docs).astype(jnp.int32)).astype(F32)
    tok_o[...] = tok
    docrow_o[...] = docs_at(base + iota((8, Q), 1)).astype(F32)

    normed = project(x[...])
    normed_o[...] = normed
    ext[8 : Q + 8, 0:inner] = nn(normed, w_in[...])
    ext[8 : Q + 8, inner:full] = nt(normed, w_bt[...])
    vals_o[...] = ext[8 : Q + 8, 0:inner].astype(B16)
    bvals_o[...] = ext[8 : Q + 8, inner:full].astype(B16)
    pre = taps[4:5, :] + taps[3:4, :] * ext[8 : Q + 8, :]
    for k in range(3):
        pre = pre + taps[k : k + 1, :] * ext[5 + k : 5 + k + Q, :]
    pre_o[...] = pre[:, :inner]
    bpre_o[...] = pre[:, inner:]

    @pl.when(boundary(starts, base))
    def _():
        again = taps[4:5, :] + taps[3:4, :] * ext[8 : Q + 8, :]
        for k in range(3):
            again = again + taps[k : k + 1, :] * ext[5 + k : 5 + k + Q, :] * tok_o[:, k : k + 1]
        pre_o[...] = again[:, :inner]
        bpre_o[...] = again[:, inner:]

    act = silu(pre_o[...])
    bc = silu(bpre_o[...]).astype(B16)
    bc_o[...] = bc
    sr = nn(normed, w_s[...]) + hp[0:1, :]
    step = softplus(sr)
    cums = exact_dot(tri[...], -hp[1:2, :] * step)
    enter = jnp.exp(cums) * tok[:, 3:4]
    end = jnp.exp(cums[Q - 1 : Q, :] - cums) * tok[:, 4:5]
    lane = iota((Q, 128), 1)
    group = lax.rem(lane, 64) // 8
    pk = jnp.where(
        group == STEP, step,
        jnp.where(
            group == ENTER, enter,
            jnp.where(group == END, end, jnp.where(group == SIG, jax.nn.sigmoid(sr), cums)),
        ),
    )
    pk_o[...] = pk
    high, low = split(pk)
    pk2 = jnp.where(lane < 64, high.astype(F32), low).astype(B16)
    pk2_o[...] = pk2
    cumt_o[...] = cums.T[0:8, :]
    scaled = nn(pk2, e_step[...]) * act
    scaled_o[...] = scaled.astype(B16)
    x16, x_lo = split(nn(pk2, e_end[...]) * scaled)
    x_lo = x_lo.astype(B16)
    carry = nn(pk2[Q - 16 :], e_enter[...])[15:16, :]
    sent_o[0] = state[...]
    dp_o[0] = prod[...]
    state[...] = carry * state[...] + tn(bc[:, :128], x16) + tn(bc[:, :128], x_lo)
    prod[...] = prod[...] * carry
    fin_o[0:128, :] = state[...].astype(B16)
    fin_o[128:144, :] = jnp.concatenate([prod[...], prod[...]], axis=0).astype(B16)


def intra_kernel(heads, normed, w_gate, pre, bc, pk, cumt, scaled, tok, docrow, vec, gate_o, y_o):
    gate_o[...] = nn(normed[...], w_gate[...])
    low = iota((HALF, 128), 1) < 64
    for block in range(2):
        rows = slice(block * HALF, (block + 1) * HALF)
        wide = (block + 1) * HALF
        scores = nt(bc[rows, 128:], bc[:wide, :128])
        mask = (block * HALF + iota((HALF, wide), 0) >= iota((HALF, wide), 1)) & (
            tok[rows, 5:6] == docrow[0:1, :wide]
        )
        for pair in range(heads // 2):
            cols = slice(pair * 128, (pair + 1) * 128)
            values = scaled[:wide, cols]
            outs = []
            for h in (2 * pair, 2 * pair + 1):
                diff = pk[rows, 8 * CUMS + h : 8 * CUMS + h + 1] - cumt[h : h + 1, :wide]
                mix = scores * jnp.where(mask, jnp.exp(diff), 0.0)
                outs.append(nn(mix.astype(B16), values))
            y_o[rows, cols] = jnp.where(low, *outs) + vec[0:1, cols] * silu(pre[rows, cols])


def fold_states(keep, others, out):
    state = jnp.zeros(out.shape, F32)
    for ref in reversed(others):
        state = ref[128:129, :].astype(F32) * state + ref[0:128, :].astype(F32)
    out[...] = keep[128:129, :] * state + keep[0:128, :]


def pair_kernel(reverse, place, own, other, keep_o, total_o):
    mine, theirs = own[...].astype(F32), other[...].astype(F32)
    earlier = lax.rem(place[1], 2) == (0 if reverse else 1)
    keep_o[0:128, :] = jnp.where(earlier, theirs[0:128, :], 0.0)
    keep_o[128:, :] = jnp.where(earlier, theirs[128:136, :], 1.0)
    total_o[0:128, :] = jnp.where(
        earlier,
        mine[128:129, :] * theirs[0:128, :] + mine[0:128, :],
        theirs[128:129, :] * mine[0:128, :] + theirs[0:128, :],
    ).astype(B16)
    total_o[128:, :] = (mine[128:, :] * theirs[128:, :]).astype(B16)


def join_kernel(n, m, place, y, gate, bc, pk2, sent, dp, keep, *refs):
    others, cots = refs[:m], refs[m : m + n]
    (w_out, vec, e_enter, ssd_o, inter_o, gn_o, stats_o, s_in, cot_o) = refs[m + n :]
    c = pl.program_id(0)
    inner = y.shape[1]

    @pl.when(c == 0)
    def _():
        fold_states(keep, others, s_in)

    for k in range(n):

        @pl.when(lax.rem(place[0] - c + n, n) == k)
        def _(k=k):
            cot_o[...] = cots[k][...]

    entering = sent[0] + dp[0, 0:1, :] * s_in[...]
    inter = nn(pk2[...], e_enter[...]) * nn(bc[:, 128:], entering.astype(B16))
    inter_o[...] = inter
    ssd = y[...] + inter
    ssd_o[...] = ssd
    gated = ssd * silu(gate[...])
    gn = nt(cot_o[...], w_out[...])
    gn_o[...] = gn
    lane = iota((inner, 128), 1)
    first = (lane == 0).astype(F32).astype(B16)
    second = (lane == 1).astype(F32).astype(B16)
    both = two_dot(gated * gated, first)
    both = both + two_dot(vec[1:2, :] * gn * gated, second)
    stats_o[...] = both.T[0:8, :]


def gate_kernel(n, width_all, ssd, gate, gn, vec, pre, bc, pk2, e_enter, *refs):
    stats = refs[:n]
    norm_o, gate_o, gs_o, sums_o, sb_o, db_o, fin_o, state, prod = refs[n:]
    i = pl.program_id(0)

    @pl.when(i == 0)
    def _():
        state[...] = jnp.zeros_like(state)
        prod[...] = jnp.ones_like(prod)
        sums_o[...] = jnp.zeros_like(sums_o)

    st = total(stats)
    rms = lax.rsqrt(st[0:1, :] / width_all + EPSILON)
    pull = rms * rms * rms * st[1:2, :] / width_all
    st = jnp.concatenate([rms, pull, jnp.zeros((126, Q), F32)], axis=0).T
    rms, pull = st[:, 0:1], st[:, 1:2]
    g = gate[...]
    sig = jax.nn.sigmoid(g)
    s = ssd[...]
    act_g = g * sig
    gated = s * act_g
    scaled = gated * rms
    ngain = vec[1:2, :]
    norm_o[...] = (scaled * ngain).astype(B16)
    gn_ = gn[...]
    grad_gated = rms * (ngain * gn_) - gated * pull
    gs = grad_gated * act_g
    gs_o[...] = gs
    gate_o[...] = (grad_gated * s * (sig * (1.0 + g * (1.0 - sig)))).astype(B16)
    sums_o[0:1, :] += jnp.sum(gn_ * scaled, axis=0, keepdims=True)
    sums_o[1:2, :] += jnp.sum(gs * silu(pre[...]), axis=0, keepdims=True)
    enter = nn(pk2[...], e_enter[...])
    carry = enter[Q - 1 : Q, :]
    sb_o[0] = state[...]
    db_o[0] = prod[...]
    state[...] = carry * state[...] + tn(bc[:, 128:], (enter * gs).astype(B16)) + tn(bc[:, 128:], split(enter * gs)[1].astype(B16))
    prod[...] = prod[...] * carry
    fin_o[0:128, :] = state[...].astype(B16)
    fin_o[128:144, :] = jnp.concatenate([prod[...], prod[...]], axis=0).astype(B16)


def intra_back_kernel(
    heads, gs, bc, pk, pk2, cumt, scaled, tok, docrow, sent, dp, s_in, e_enter,
    gsc_o, rc_o, gbc_o, tot, plus, minus,
):
    low = iota((HALF, 128), 1) < 64
    g16 = gs[...].astype(B16)
    plus[...] = jnp.zeros_like(plus)
    for block in range(2):
        rows = slice(block * HALF, (block + 1) * HALF)
        wide = slice(block * HALF, Q)
        width = Q - block * HALF
        scores = nt(bc[rows, :128], bc[wide, 128:])
        mask = (iota((HALF, width), 0) <= iota((HALF, width), 1)) & (
            tok[rows, 5:6] == docrow[0:1, wide]
        )
        sums = jnp.zeros((HALF, width), F32)
        lane = iota((HALF, 128), 1)
        minus_acc = jnp.zeros((HALF, 128), F32)
        for pair in range(heads // 2):
            cols = slice(pair * 128, (pair + 1) * 128)
            mine = scaled[rows, cols]
            grads = g16[wide, cols]
            outs = []
            for h in (2 * pair, 2 * pair + 1):
                diff = cumt[h : h + 1, wide] - pk[rows, 8 * CUMS + h : 8 * CUMS + h + 1]
                decay = jnp.where(mask, jnp.exp(diff), 0.0)
                keep = low if h % 2 == 0 else ~low
                masked = jnp.where(keep, mine.astype(F32), 0.0).astype(B16)
                weighted = decay * nt(masked, grads)
                sums = sums + weighted
                ws = scores * weighted
                plus[h : h + 1, wide] += jnp.sum(ws, axis=0, keepdims=True)
                minus_acc = jnp.where(
                    lax.rem(lane, 8) == h, jnp.sum(ws, axis=1, keepdims=True), minus_acc
                )
                outs.append(nn((scores * decay).astype(B16), grads))
            gsc_o[rows, cols] = jnp.where(low, *outs)
        minus[rows, :] = minus_acc
        tot[rows, wide] = sums.astype(B16)
    tot[HALF:, :HALF] = jnp.zeros((HALF, HALF), B16)
    rc_o[...] = jnp.concatenate([plus[...]] * 16, axis=0).T - minus[...]
    entering = sent[0] + dp[0, 0:1, :] * s_in[...]
    t16 = tot[...]
    enter = nn(pk2[...], e_enter[...]) * gs[...]
    gbc_o[:, :128] = nn(t16, bc[:, 128:])
    gbc_o[:, 128:] = tn(t16, bc[:, :128]) + three(enter, entering)


def conv_back(i, count, masked, gp, tok, taps, vals, hv, ext, mext, shift, out, sums_o, rim_o):
    ch = gp.shape[1]

    @pl.when(i == 0)
    def _():
        ext[Q : Q + 8, :] = jnp.zeros((8, ch), F32)
        mext[Q : Q + 8, :] = jnp.zeros((8, 8), F32)
        sums_o[...] = jnp.zeros_like(sums_o)

    @pl.when(i > 0)
    def _():
        ext[Q : Q + 8, :] = ext[0:8, :]
        mext[Q : Q + 8, :] = mext[0:8, :]

    ext[0:Q, :] = gp
    mext[0:Q, :] = tok
    sums_o[4:5, :] += jnp.sum(gp, axis=0, keepdims=True)

    def sweep(use_mask):
        vals_ = vals.astype(F32)
        acc = jnp.zeros((Q, ch), F32)
        for k in range(4):
            z = ext[3 - k : 3 - k + Q, :]
            if k < 3 and use_mask:
                z = z * mext[3 - k : 3 - k + Q, k : k + 1]
            acc = acc + taps[k : k + 1, :] * z
            sums_o[k : k + 1, :] += jnp.sum(vals_ * z, axis=0, keepdims=True)
        out[...] = acc.astype(B16)

    @pl.when(masked)
    def _():
        sweep(True)

    @pl.when(jnp.logical_not(masked))
    def _():
        sweep(False)

    @pl.when(i == count - 1)
    def _():
        rim = jnp.zeros((8, ch), F32)
        shift[0:8, :] = jnp.zeros((8, ch), F32)
        for k in range(3):
            shift[8:16, :] = ext[0:8, :] * mext[0:8, k : k + 1]
            moved = shift[3 - k : 11 - k, :]
            rim = rim + taps[k : k + 1, :] * moved
            sums_o[k : k + 1, :] += jnp.sum(hv * moved, axis=0, keepdims=True)
        rim_o[...] = rim


def chunk_base(place, count, i):
    return (place[1] * count + (count - 1 - i)) * Q


def bcoef_back_kernel(
    count, n, m, place, starts, gbc, pre, vals, pk2, scaled, tok, sb, db, taps, hv, e_end,
    keep, *refs
):
    others, packs = refs[:m], refs[m : m + n]
    sums_o, s_after, ext, mext, shift, rim_o, out, pieces = refs[m + n :]
    i = pl.program_id(0)
    inner = scaled.shape[1]

    @pl.when(i == 0)
    def _():
        fold_states(keep, others, s_after)

    after_ = sb[0] + db[0, 0:1, :] * s_after[...]
    x16 = nn(pk2[...], e_end[...]) * scaled[...].astype(F32)
    gbm = gbc[:, :128] + three(x16, after_)
    gp = jnp.concatenate([gbm, gbc[:, 128:]], axis=1) * silu_grad(pre[...])
    conv_back(
        i, count, boundary(starts, chunk_base(place, count, i)), gp, tok[...],
        taps[:, inner:], vals[...], hv[:, inner:], ext, mext, shift, out, sums_o, rim_o,
    )
    span = 256 // n
    row = pl.multiple_of((count - 1 - i) * HALF, HALF)
    for v in range(n):
        piece = out[:, v * span : (v + 1) * span]
        pieces[v] = jnp.concatenate([piece[:HALF], piece[HALF:]], axis=1)
    for k in range(n):
        packs[k][pl.ds(row, HALF), :] = pieces[lax.rem(place[0] + k, n)]

    @pl.when(i == count - 1)
    def _():
        for v in range(n):
            edge = rim_o[:, v * span : (v + 1) * span]
            pieces[v, 0:16, 0:span] = jnp.concatenate([edge, edge], axis=0).astype(B16)
        for k in range(n):
            packs[k][count * HALF :, :] = pieces[lax.rem(place[0] + k, n), 0:16, :]


def inner_back_kernel(
    count, place, starts, gs, gsc, rc, inter, pre, vals, bc, pk, pk2, scaled, tok, sent,
    dp, s_in, sb, db, s_after, taps, hp, hv, vec, tri, e_step, e_enter, e_end, hmap,
    gv_o, step_o, rim_o, sums_o, small_o, ext, mext, shift,
):
    i = pl.program_id(0)
    entering = sent[0] + dp[0, 0:1, :] * s_in[...]
    after_ = sb[0] + db[0, 0:1, :] * s_after[...]
    p = pre[...]
    sig_p = jax.nn.sigmoid(p)
    act = p * sig_p
    weights = pk2[...]
    end_state = nn(weights, e_end[...]) * nn(bc[:, :128], after_.astype(B16))
    gsc_ = gsc[...] + end_state
    grad = gs[...]
    end_terms = scaled[...].astype(F32) * end_state
    carry = nn(weights[Q - 16 :], e_enter[...])[15:16, :]
    closing = jnp.sum(end_terms, axis=0, keepdims=True) + carry * jnp.sum(
        after_ * entering, axis=0, keepdims=True
    )
    closing = two_dot(jnp.broadcast_to(closing, (8, closing.shape[1])), hmap[...])[0:1, :]
    grad_cums = rc[...] + two_dot(grad * inter[...] - end_terms, hmap[...])
    grad_cums = grad_cums + jnp.where(iota((Q, 128), 0) == Q - 1, closing, 0.0)
    high, low = split(grad_cums)
    grad_decay = tn(tri[...], high) + tn(tri[...], low.astype(B16))
    drive = hp[1:2, :] * grad_decay
    raw = (nn((gsc_ * act).astype(B16), hmap[...]) - drive) * pk[...]
    lane = iota((Q, 128), 1)
    step_o[...] = jnp.where(lane // 8 == SIG, raw, 0.0).astype(B16)

    @pl.when(i == 0)
    def _():
        small_o[...] = jnp.zeros_like(small_o)

    small_o[0:1, :] += jnp.sum(raw, axis=0, keepdims=True)
    small_o[1:2, :] -= jnp.sum(drive * pk[...], axis=0, keepdims=True)
    gp = (nn(weights, e_step[...]) * gsc_ + vec[0:1, :] * grad) * (
        sig_p * (1.0 + p * (1.0 - sig_p))
    )
    conv_back(
        i, count, boundary(starts, chunk_base(place, count, i)), gp, tok[...], taps[...],
        vals[...], hv[...], ext, mext, shift, gv_o, sums_o, rim_o,
    )


def mix_kernel(n, gnorm, w_out, *mixes):
    mixed = nn(gnorm[...], w_out[...]).astype(B16)
    for k in range(n):

        @pl.when(pl.program_id(0) == k)
        def _(k=k):
            mixes[k][...] = mixed


def gate_grads_kernel(place, gnorm, normed, gate16, cot, keep_o, send_o):
    r = pl.program_id(0)
    core = lax.rem(place[1], 2)
    inner = gate16.shape[1]
    left = tn(normed[...], gate16[...]).astype(B16)
    right = tn(gnorm[...], cot[...]).astype(B16)

    @pl.when(r == core)
    def _():
        keep_o[:, 0:inner] = left
        keep_o[:, inner:] = right

    @pl.when(r != core)
    def _():
        send_o[:, 0:inner] = left
        send_o[:, inner:] = right


def inner_grads_kernel(
    place, gv, gv_all, rim, hn, gate16, step16, normed, w_in, w_gate, w_s, part_o, keep_o, send_o
):
    r = pl.program_id(0)
    core = lax.rem(place[1], 2)
    part_o[...] = nt(gv[...], w_in[...]) + nt(gate16[...], w_gate[...]) + nt(step16[...], w_s[...])
    grads = (tn(normed[...], gv_all[...]) + tn(hn[...], rim[...].astype(B16))).astype(B16)

    @pl.when(r == core)
    def _():
        keep_o[...] = grads

    @pl.when(r != core)
    def _():
        send_o[...] = grads


def bcoef_grads_kernel(count, n, pack_view, tail_view, place, *refs):
    packs = [pack_view(ref, pl.program_id(0), (place,)) for ref in refs[:n]]
    tails = [tail_view(ref, 0, (place,)) for ref in refs[:n]]
    (
        rim_i, hn, part, normed, w_bt, w_in, step16, gain, csum_b, csum_i, ssum, nsums,
    ) = refs[n : n + 12]
    parts = refs[n + 12 : 2 * n + 12]
    keep_o, send_o, small_o, local_o, acc, gsum = refs[2 * n + 12 :]
    i = pl.program_id(0)
    span, d = w_bt.shape
    inner = w_in.shape[1]

    @pl.when(i == 0)
    def _():
        rim16 = total(tails)[0:8, :span].astype(B16)
        edge = nn(rim16, w_bt[...]) + nt(rim_i[...].astype(B16), w_in[...])
        small_o[3:8, :] = edge[3:8, :]
        gsum[...] = jnp.sum(edge * hn[...].astype(F32), axis=0, keepdims=True)
        acc[...] = tn(jnp.concatenate([rim16, jnp.zeros((8, span), B16)], axis=1), hn[...])

    packed = total(packs)
    v16 = jnp.concatenate([packed[:, :span], packed[:, span:]], axis=0).astype(B16)
    sums = part[...] + nn(v16, w_bt[...])
    for k in range(n):

        @pl.when(i == k)
        def _(k=k):
            parts[k][...] = sums.astype(B16)

    x16 = normed[...]
    gsum[...] += jnp.sum(sums * x16.astype(F32), axis=0, keepdims=True)
    acc[...] += tn(jnp.concatenate([v16, step16[:, :span]], axis=1), x16)

    @pl.when(i == count - 1)
    def _():
        turned = acc[...].T.astype(B16)
        core = lax.rem(place[1], 2)
        half = d // 2

        @pl.when(core == 0)
        def _():
            keep_o[...] = turned[:half]
            send_o[...] = turned[half:]

        @pl.when(core == 1)
        def _():
            keep_o[...] = turned[half:]
            send_o[...] = turned[:half]

        small_o[0:1, :] = gsum[...] / gain[0:1, :]
        for k in range(3):
            small_o[1:2, k * 256 : (k + 1) * 256] = csum_b[k : k + 1, :]
            local_o[3 + k : 4 + k, 0:inner] = csum_i[2 * k : 2 * k + 1, :]
        for k in range(2):
            small_o[2:3, k * 256 : (k + 1) * 256] = csum_b[3 + k : 4 + k, :]
            local_o[3 + k : 4 + k, inner:] = csum_i[2 * k + 1 : 2 * k + 2, :]
        local_o[5:6, inner:] = nsums[1:2, :]
        local_o[6:7, 0:inner] = nsums[0:1, :]
        local_o[6:7, inner : inner + 128] = ssum[0:1, :]
        local_o[6:7, inner + 128 : inner + 256] = ssum[1:2, :]


def small_kernel(local, *refs):
    *ins, small_o, edge_o = refs
    both = total(ins)
    small_o[0:3, :] = both[0:3, :]
    small_o[3:8, :] = local[3:8, :]
    edge_o[0:3, :] = jnp.zeros((3, both.shape[1]), F32)
    edge_o[3:8, :] = both[3:8, :]


def last_kernel(n, x, cot, gain, edge, *refs):
    parts, mixes, (grad_o, block_o) = refs[:n], refs[n : 2 * n], refs[2 * n :]
    sums = total(parts)
    rows = sums.shape[0]
    sums = jnp.concatenate([sums[: rows - 8], sums[rows - 8 :] + edge[...]], axis=0)
    wide = x[...].astype(F32)
    block_o[...] = (wide + total(mixes)).astype(B16)
    scale = rms_scale(wide)
    scaled = gain[0:1, :] * sums
    dot = jnp.sum(scaled * wide, axis=1, keepdims=True)
    width = wide.shape[1]
    grad_o[...] = (
        cot[...].astype(F32) + scale * scaled - wide * (scale * scale * scale * dot / width)
    )


def add_kernel(a, b, out):
    out[...] = a[...] + b[...]


def ends_kernel(n, heads, place, *refs):
    smalls = refs[:n]
    gain_o, taps_i_o, taps_b_o, bias_i_o, bias_b_o, sbias_o, dlog_o, skip_o, ngain_o = refs[n:]
    sums = total(smalls)
    inner, span = ngain_o.shape[0], bias_b_o.shape[0]
    count, own = 256 // span, gain_o.shape[0]
    for v in range(count):

        @pl.when(place[0] == v)
        def _(v=v):
            gain_o[...] = sums[0:1, v * own : (v + 1) * own].reshape(own)
            low = v * span
            for k in range(4):
                row, at = (1, 256 * k) if k < 3 else (2, 0)
                taps_b_o[k : k + 1, :] = sums[row : row + 1, at + low : at + low + span]
            bias_b_o[...] = sums[2:3, 256 + low : 256 + low + span].reshape(span)

    taps_i_o[0:1, :] = sums[3:4, :inner]
    taps_i_o[1:2, :] = sums[3:4, inner:]
    taps_i_o[2:3, :] = sums[4:5, :inner]
    taps_i_o[3:4, :] = sums[4:5, inner:]
    bias_i_o[...] = sums[5:6, :inner].reshape(inner)
    ngain_o[...] = sums[6:7, :inner].reshape(inner)
    raw_at, decay_at = inner + 8 * SIG, inner + 128 + 8 * STEP
    sbias_o[...] = sums[6:7, raw_at : raw_at + heads].reshape(heads)
    dlog_o[...] = sums[6:7, decay_at : decay_at + heads].reshape(heads)
    hit = iota((8, inner), 1) // (inner // heads) == iota((8, inner), 0)
    rows = jnp.where(hit, sums[5:6, inner:], 0.0)
    column = jnp.sum(rows, axis=1, keepdims=True)
    skip_o[...] = jnp.broadcast_to(column, (8, 128)).T[0:1, 0:heads].reshape(heads)


def halves_kernel(n, place, *refs):
    ins, outs = refs[:6], refs[6:]
    rows = outs[0].shape[0]
    for k in range(n):
        piece = pl.ds(pl.multiple_of(lax.rem(lax.div(place[1], 2) + k, n) * rows, rows), rows)
        at = 0
        for j in range(3):
            mine, theirs = ins[2 * j], ins[2 * j + 1]
            cols = slice(at, at + mine.shape[1])
            at += mine.shape[1]
            outs[k][:, cols] = (
                mine[piece, :].astype(F32) + theirs[piece, :].astype(F32)
            ).astype(B16)


def pieces_kernel(*refs):
    refs[-1][...] = total(refs[:-1]).astype(B16)


def unpack_kernel(n, place, *refs):
    pieces = refs[: 2 * n]
    gate_o, inner_o, bcoef_o, step_o, out_o, late = refs[2 * n :]
    rows = pieces[0].shape[0]
    inner = gate_o.shape[1]
    span = bcoef_o.shape[0]
    heads = step_o.shape[0]
    for side in range(2):
        for k in range(n):
            piece = pieces[side * n + k][...].astype(F32)
            whole_half = lax.rem(lax.div(place[1], 2) - k + n, n)
            core = lax.rem(place[1] + side, 2)
            at = pl.multiple_of(core * (n * rows) + whole_half * rows, rows)
            dst = pl.ds(at, rows)
            gate_o[dst, :] = piece[:, 0:inner]
            inner_o[dst, :] = piece[:, 2 * inner : 3 * inner]
            late[dst, :] = piece[:, 3 * inner :]
            low = pl.ds(pl.multiple_of(whole_half * rows, rows), rows)

            @pl.when(core == 0)
            def _():
                out_o[low, 0:inner] = piece[:, inner : 2 * inner]

            @pl.when(core == 1)
            def _():
                out_o[low, inner:] = piece[:, inner : 2 * inner]

    turned = late[...].T
    bcoef_o[...] = turned[:span, :]
    step_o[...] = turned[span + 8 * SIG : span + 8 * SIG + heads, :]


def shape(dims, dtype=F32):
    return jax.ShapeDtypeStruct(dims, dtype)


def call(kernel, grid, ins, in_specs, outs, out_specs, scratch=(), scalars=(), flops=0):
    size = sum(a.size * a.dtype.itemsize for a in ins) + sum(
        o.size * o.dtype.itemsize for o in outs
    )
    views = list(in_specs) + list(out_specs)

    def body(*refs):
        first = len(scalars)
        step = pl.program_id(0) if grid else 0
        seen = [
            view(ref, step, refs[:first]) if view else ref
            for view, ref in zip(views, refs[first:])
        ]
        kernel(*refs[:first], *seen, *refs[first + len(views) :])

    return pl.pallas_call(
        body,
        out_shape=outs,
        grid_spec=pltpu.PrefetchScalarGridSpec(
            num_scalar_prefetch=len(scalars),
            grid=grid,
            in_specs=[VMEM] * len(ins),
            out_specs=[VMEM] * len(outs),
            scratch_shapes=list(scratch),
        ),
        compiler_params=pltpu.CompilerParams(
            dimension_semantics=("arbitrary",) * len(grid) or None,
            vmem_limit_bytes=LIMIT,
        ),
        cost_estimate=pl.CostEstimate(
            flops=int(flops), bytes_accessed=size, transcendentals=0
        ),
    )(*scalars, *ins)


def ring(value, axis, distance):
    count = lax.axis_size(axis)
    return lax.ppermute(value, axis, [(i, (i + distance) % count) for i in range(count)])


def swap(value, axis, bit):
    count = lax.axis_size(axis)
    return lax.ppermute(value, axis, [(i, i ^ (1 << bit)) for i in range(count)])


def spread(value, axis):
    count = lax.axis_size(axis)
    return [value] + [ring(value, axis, k) for k in range(1, count)]


def reduce_parts(parts, axis):
    return [ring(p, axis, k) if k else p for k, p in enumerate(parts)]


def states(fin, place, reverse):
    rows, inner = fin.shape
    count = lax.axis_size("seq")
    other = swap(fin, "seq", 0)
    keep, both = call(
        functools.partial(pair_kernel, reverse), (), [fin, other], [None] * 2,
        [shape((rows - 8, inner)), shape((rows, inner), B16)], [None] * 2,
        scalars=(place,),
    )
    got = []
    for k in range(1, count // 2):
        if reverse:
            pairs = [(i + 2 * k, i) for i in range(count - 2 * k)]
        else:
            pairs = [(i, i + 2 * k) for i in range(count - 2 * k)]
        got.append(lax.ppermute(both, "seq", pairs))
    return keep, got


def per_device(
    block_in,
    in_gain,
    proj_gate,
    proj_inner,
    proj_bcoef,
    proj_step,
    conv_inner,
    conv_inner_bias,
    conv_bcoef,
    conv_bcoef_bias,
    step_bias,
    decay_log,
    skip_gain,
    norm_gain,
    proj_out,
    out_grad,
    doc_starts,
):
    n_wt, n_seq = lax.axis_size("wt"), lax.axis_size("seq")
    w, seq = lax.axis_index("wt"), lax.axis_index("seq")
    rows_own, d = block_in.shape
    length = rows_own * n_wt
    inner = proj_inner.shape[1]
    heads = step_bias.shape[0]
    span = proj_bcoef.shape[1]
    full = inner + span * n_wt
    width_all = inner * n_wt
    count = length // Q
    pairs = n_seq // 2
    place = jnp.stack([w, seq]).astype(jnp.int32)
    scalars = (place, doc_starts)

    w_bt_own = proj_bcoef.T
    quarter = span // 4
    (early,) = call(
        prep_kernel, (), [w_bt_own, conv_bcoef, conv_bcoef_bias, in_gain], [None] * 4,
        [shape((quarter + 16, d), B16)], [None], scalars=(place,),
    )
    earlies = spread(early, "wt")
    rows = spread(block_in, "wt")
    (bts,) = call(
        stack_kernel, (), earlies, [None] * n_wt, [shape((quarter * n_wt, d), B16)], [None],
    )
    bts_x = swap(bts, "seq", 1)
    bts_y = [swap(b, "seq", 2) for b in (bts, bts_x)]
    tail = block_in[rows_own - 8 :]
    halos = []
    for v in range(n_wt):
        halos.append(
            lax.ppermute(
                tail, ("seq", "wt"),
                [((s - 1) * n_wt + n_wt - 1, s * n_wt + v) for s in range(1, n_seq)],
            )
        )
    cots = spread(out_grad, "wt")

    lanes, chans = np.arange(128), np.arange(inner) // (inner // heads)

    def one_hot(group):
        hit = ((lanes % 64) // 8 == group)[:, None] & ((lanes % 8)[:, None] == chans[None, :])
        return jnp.asarray(hit.astype(np.float32), B16)

    e_step, e_enter, e_end = one_hot(STEP), one_hot(ENTER), one_hot(END)
    hmap = jnp.asarray((chans[:, None] == (lanes % 8)[None, :]).astype(np.float32), B16)
    tri = jnp.asarray((np.arange(Q)[:, None] >= np.arange(Q)[None, :]).astype(np.float32), B16)

    grid = (count,)

    def at_rows(ref, index, rows=Q):
        return ref.at[pl.ds(pl.multiple_of(index * rows, rows), rows), :]

    def by_rows(reverse=False):
        if reverse:
            return lambda ref, i, p: at_rows(ref, count - 1 - i)
        return lambda ref, i, p: at_rows(ref, i)

    def by_turn():
        return lambda ref, i, p: at_rows(ref, lax.rem(i + p[0][0], count))

    def whole(*dims):
        return None

    def by_chunk(*dims, reverse=False):
        if reverse:
            return lambda ref, i, p: ref.at[pl.ds(count - 1 - i, 1)]
        return lambda ref, i, p: ref.at[pl.ds(i, 1)]

    def by_lanes(width, reverse=False):
        def view(ref, i, p):
            index = count - 1 - i if reverse else i
            return ref.at[:, pl.ds(pl.multiple_of(index * width, width), width)]

        return view

    def lead(ref, i, p):
        return ref.at[:, :inner]

    by_cols = by_lanes(Q)
    by_cols_back = by_lanes(Q, True)
    fin_spec, state_spec = whole(144, inner), whole(128, inner)
    e_spec = whole(128, inner)
    states_out = [shape((count, 128, inner)), shape((count, 8, inner)), shape((144, inner), B16)]
    (normed, vals, bvals, pre, bpre, bc, pk, pk2, cumt, scaled, sent, dp, fin, hv, hn, tok,
     docrow, taps, gain, hp, w_s, vec) = call(
        functools.partial(front_kernel, heads, n_wt), grid,
        [*rows, *halos, *earlies, bts, bts_x, *bts_y, proj_inner, proj_step, conv_inner,
         conv_inner_bias, step_bias, decay_log, skip_gain, norm_gain, tri, e_step, e_enter,
         e_end],
        [None] * (3 * n_wt + 16),
        [shape((length, d), B16), shape((length, inner), B16), shape((length, 256), B16),
         shape((length, inner)), shape((length, 256)),
         shape((length, 256), B16), shape((length, 128)), shape((length, 128), B16),
         shape((8, length)), shape((length, inner), B16), *states_out,
         shape((8, full)), shape((8, d), B16), shape((length, 8)), shape((8, length)),
         shape((8, full)), shape((8, d)), shape((8, 128)), shape((d, 128), B16),
         shape((8, inner))],
        [by_rows(), by_rows(), by_rows(), by_rows(), by_rows(), by_rows(),
         by_rows(), by_rows(),
         by_cols, by_rows(), by_chunk(128, inner), by_chunk(8, inner), fin_spec,
         whole(8, full), whole(8, d), by_rows(), by_cols, whole(8, full), whole(8, d),
         None, None, None],
        scratch=[pltpu.VMEM((Q + 8, full), F32), pltpu.VMEM((128, inner), F32),
                 pltpu.VMEM((8, inner), F32), pltpu.VMEM((span * n_wt, d), B16),
                 pltpu.VMEM((Q, d), B16)],
        scalars=scalars, flops=2e9,
    )
    keep, got = states(fin, place, False)
    gate, y = call(
        functools.partial(intra_kernel, heads), grid,
        [normed, proj_gate, pre, bc, pk, cumt, scaled, tok, docrow, vec],
        [by_rows(), whole(d, inner), by_rows(), by_rows(), by_rows(), by_cols,
         by_rows(), by_rows(), by_cols, whole(1, inner)],
        [shape((length, inner)), shape((length, inner))],
        [by_rows(), by_rows()], flops=2e9,
    )
    got_spec = [whole(136, inner)] + [fin_spec] * (pairs - 1)
    ssd, inter, gn, stats, s_in, cot = call(
        functools.partial(join_kernel, n_wt, pairs - 1), grid,
        [y, gate, bc, pk2, sent, dp, keep, *got, *cots, proj_out, vec, e_enter],
        [by_rows(), by_rows(), by_rows(), by_rows(),
         by_chunk(128, inner), by_chunk(8, inner), *got_spec]
        + [whole(Q, d)] * n_wt + [whole(inner, d), whole(1, inner), e_spec],
        [shape((length, inner))] * 3
        + [shape((8, length)), shape((128, inner)), shape((length, d), B16)],
        [by_rows()] * 3 + [by_cols, state_spec, by_rows()],
        scalars=(place,), flops=2e9,
    )
    gnorm, gate16, gs, nsums, sb, db, back_fin = call(
        functools.partial(gate_kernel, n_wt, width_all), grid,
        [ssd, gate, gn, vec, pre, bc, pk2, e_enter, *spread(stats, "wt")],
        [by_rows(True)] * 3
        + [whole(1, inner), by_rows(True), by_rows(True), by_rows(True), e_spec]
        + [by_cols_back] * n_wt,
        [shape((length, inner), B16), shape((length, inner), B16), shape((length, inner)),
         shape((8, inner)), *states_out],
        [by_rows(True)] * 3
        + [whole(8, inner), by_chunk(128, inner, reverse=True), by_chunk(8, inner, reverse=True),
           fin_spec],
        scratch=[pltpu.VMEM((128, inner), F32), pltpu.VMEM((8, inner), F32)],
        flops=1e9,
    )
    keep_b, got_b = states(back_fin, place, True)
    gsc, rc, gbc = call(
        functools.partial(intra_back_kernel, heads), grid,
        [gs, bc, pk, pk2, cumt, scaled, tok, docrow, sent, dp, s_in, e_enter],
        [by_rows(), by_rows(), by_rows(), by_rows(), by_cols, by_rows(),
         by_rows(), by_cols, by_chunk(128, inner), by_chunk(8, inner), state_spec, e_spec],
        [shape((length, inner)), shape((length, 128)), shape((length, 256))],
        [by_rows(), by_rows(), by_rows()],
        scratch=[pltpu.VMEM((Q, Q), B16), pltpu.VMEM((8, Q), F32), pltpu.VMEM((Q, 128), F32)],
        flops=4e9,
    )

    half = d // 2
    d_half = by_lanes(half)
    mixes = call(
        lambda p, *refs: mix_kernel(n_wt, *refs), grid, [gnorm, proj_out],
        [by_turn(), whole(inner, d)], [shape((Q, d), B16)] * n_wt, [whole(Q, d)] * n_wt,
        scalars=(place,), flops=1e9,
    )
    keep_a, send_a = call(
        gate_grads_kernel, (2,), [gnorm, normed, gate16, cot],
        [whole(length, inner), d_half, whole(length, inner), d_half],
        [shape((half, 2 * inner), B16)] * 2, [whole(half, 2 * inner)] * 2,
        scalars=(place,), flops=2e9,
    )
    got_a = swap(send_a, "seq", 0)
    mixes = reduce_parts(mixes, "wt")

    rows_pack = length // 2 + 16
    *packs, csum_b, s_after = call(
        functools.partial(bcoef_back_kernel, count, n_wt, pairs - 1), grid,
        [gbc, bpre, bvals, pk2, scaled, tok, sb, db, taps, hv, e_end,
         keep_b, *got_b],
        [by_rows(True), by_rows(True), by_rows(True), by_rows(True),
         by_rows(True), by_rows(True), by_chunk(128, inner, reverse=True),
         by_chunk(8, inner, reverse=True), whole(8, full), whole(8, full), e_spec, *got_spec],
        [shape((rows_pack, 128), B16)] * n_wt + [shape((8, 256)), shape((128, inner))],
        [whole(rows_pack, 128)] * n_wt + [whole(8, 256), state_spec],
        scratch=[pltpu.VMEM((Q + 8, 256), F32), pltpu.VMEM((Q + 8, 8), F32),
                 pltpu.VMEM((16, 256), F32), pltpu.VMEM((8, 256), F32),
                 pltpu.VMEM((Q, 256), B16), pltpu.VMEM((n_wt, HALF, 128), B16)],
        scalars=scalars, flops=1e9,
    )
    packs = reduce_parts(packs, "wt")
    gv, step16, rim_i, csum_i, ssum = call(
        functools.partial(inner_back_kernel, count), grid,
        [gs, gsc, rc, inter, pre, vals, bc, pk, pk2, scaled, tok, sent, dp, s_in, sb, db,
         s_after, taps, hp, hv, vec, tri, e_step, e_enter, e_end, hmap],
        [by_rows(True), by_rows(True), by_rows(True), by_rows(True),
         by_rows(True), by_rows(True), by_rows(True), by_rows(True),
         by_rows(True), by_rows(True), by_rows(True),
         by_chunk(128, inner, reverse=True), by_chunk(8, inner, reverse=True), state_spec,
         by_chunk(128, inner, reverse=True), by_chunk(8, inner, reverse=True), state_spec,
         lead, whole(8, 128), lead, whole(1, inner), whole(Q, Q), e_spec,
         e_spec, e_spec, whole(inner, 128)],
        [shape((length, inner), B16), shape((length, 128), B16), shape((8, inner)),
         shape((8, inner)), shape((8, 128))],
        [by_rows(True), by_rows(True), whole(8, inner), whole(8, inner),
         whole(8, 128)],
        scratch=[pltpu.VMEM((Q + 8, inner), F32), pltpu.VMEM((Q + 8, 8), F32),
                 pltpu.VMEM((16, inner), F32)],
        scalars=scalars, flops=1e9,
    )
    t_half = lambda: lambda ref, r, p: at_rows(ref, r, length // 2)
    part, keep_i, send_i = call(
        inner_grads_kernel, (2,),
        [gv, gv, rim_i, hn, gate16, step16, normed, proj_inner, proj_gate, w_s],
        [t_half(), whole(length, inner), whole(8, inner),
         d_half, t_half(), t_half(), d_half,
         whole(d, inner), whole(d, inner), whole(d, 128)],
        [shape((length, d)), shape((half, inner), B16), shape((half, inner), B16)],
        [t_half(), whole(half, inner), whole(half, inner)],
        scalars=(place,), flops=2e9,
    )
    got_i = swap(send_i, "seq", 0)
    pack_spec = lambda ref, i, p: at_rows(ref, lax.rem(i + p[0][0], count), HALF)
    tail_spec = lambda ref, i, p: ref.at[length // 2 : length // 2 + 16, :]
    *parts, keep_p, send_p, small, local = call(
        functools.partial(bcoef_grads_kernel, count, n_wt, pack_spec, tail_spec), grid,
        [*packs, rim_i, hn, part, normed, w_bt_own, proj_inner, step16, gain, csum_b,
         csum_i, ssum, nsums],
        [None] * n_wt
        + [whole(8, inner), whole(8, d), by_turn(), by_turn(), whole(span, d),
           whole(d, inner), by_turn(), whole(8, d), whole(8, 256), whole(8, inner),
           whole(8, 128), whole(8, inner)],
        [shape((Q, d), B16)] * n_wt
        + [shape((half, 2 * span), B16)] * 2 + [shape((8, d))] * 2,
        [whole(Q, d)] * n_wt + [whole(half, 2 * span)] * 2 + [whole(8, d)] * 2,
        scratch=[pltpu.VMEM((2 * span, d), F32), pltpu.VMEM((1, d), F32)],
        scalars=(place,), flops=1e9,
    )
    parts = reduce_parts(parts, "wt")
    got_p = swap(send_p, "seq", 0)
    small, edge = call(
        small_kernel, (), [local, *spread(small, "wt")], [None] * (n_wt + 1),
        [shape((8, d))] * 2, [None] * 2,
    )
    edge = lax.ppermute(
        edge, ("seq", "wt"),
        [(s * n_wt + n_wt - 1, (s - 1) * n_wt + n_wt - 1) for s in range(1, n_seq)],
    )
    input_grad, block_out = call(
        functools.partial(last_kernel, n_wt), (),
        [block_in, out_grad, gain, edge, *parts, *mixes], [None] * (4 + 2 * n_wt),
        [shape((rows_own, d)), shape((rows_own, d), B16)], [None] * 2,
    )

    def pair_ring(value, k):
        return lax.ppermute(
            value, "seq", [(i, (i + 2 * k) % n_seq) for i in range(n_seq)]
        )

    wide = 3 * inner + 2 * span
    piece_rows = half // pairs
    pieces = call(
        functools.partial(halves_kernel, pairs), (),
        [keep_a, got_a, keep_i, got_i, keep_p, got_p], [None] * 6,
        [shape((piece_rows, wide), B16)] * pairs, [None] * pairs,
        scalars=(place,),
    )
    pieces = [pair_ring(p, k) if k else p for k, p in enumerate(pieces)]
    (piece,) = call(
        pieces_kernel, (), pieces, [None] * pairs, [shape((piece_rows, wide), B16)], [None],
    )
    own = [pair_ring(piece, k) if k else piece for k in range(pairs)]
    theirs = [swap(p, "seq", 0) for p in own]
    g_gate, g_inner, g_bcoef, g_step, g_out = call(
        functools.partial(unpack_kernel, pairs), (1,), [*own, *theirs],
        [whole(piece_rows, wide)] * (2 * pairs),
        [shape((d, inner)), shape((d, inner)), shape((span, d)), shape((heads, d)),
         shape((inner, d))],
        [whole(d, inner), whole(d, inner), whole(span, d), whole(heads, d), whole(inner, d)],
        scratch=[pltpu.VMEM((d, 2 * span), F32)], scalars=(place,),
    )
    (small,) = call(
        add_kernel, (), [small, swap(small, "seq", 0)], [None] * 2,
        [shape((8, d))], [None],
    )
    smalls = [pair_ring(small, k) if k else small for k in range(pairs)]
    (g_gain, g_ci, g_cb, g_cib, g_cbb, g_sbias, g_dlog, g_skip, g_norm) = call(
        functools.partial(ends_kernel, pairs, heads), (), smalls, [None] * pairs,
        [shape((in_gain.shape[0],)), shape((4, inner)), shape((4, span)), shape((inner,)),
         shape((span,)), shape((heads,)), shape((heads,)), shape((heads,)), shape((inner,))],
        [None] * 9, scalars=(place,),
    )
    return (
        block_out,
        input_grad,
        g_gain,
        g_gate,
        g_inner,
        g_bcoef.T,
        g_step.T,
        g_ci,
        g_cb,
        g_cib,
        g_cbb,
        g_sbias,
        g_dlog,
        g_skip,
        g_norm,
        g_out,
    )


def solution(mesh):
    tokens = P(("seq", "wt"), None)
    cols, vec = P(None, "wt"), P("wt")
    return jax.shard_map(
        per_device,
        mesh=mesh,
        in_specs=(
            tokens, vec, cols, cols, cols, cols, cols, vec, cols, vec, vec, vec, vec, vec,
            P("wt", None), tokens, P(),
        ),
        out_specs=(
            tokens, tokens, vec, cols, cols, cols, cols, cols, cols, vec, vec, vec, vec, vec,
            vec, P("wt", None),
        ),
        check_vma=False,
    )
```

```python
import functools

import jax
import jax.numpy as jnp
import numpy as np
from jax import lax
from jax.experimental import pallas as pl
from jax.experimental.pallas import tpu as pltpu
from jax.sharding import PartitionSpec as P

VMEM = pl.BlockSpec(memory_space=pltpu.VMEM)
HBM = pl.BlockSpec(memory_space=pltpu.HBM)
LIMIT = 16 << 20
Q = 256
HALF = Q // 2
STEP, ENTER, END, CUMS, SIG = 0, 1, 2, 4, 5
EPSILON = 1e-05
F32 = jnp.float32
B16 = jnp.bfloat16


def nn(a, b):
    return lax.dot_general(a, b, (((1,), (0,)), ((), ())), preferred_element_type=F32)


def nt(a, b):
    return lax.dot_general(a, b, (((1,), (1,)), ((), ())), preferred_element_type=F32)


def tn(a, b):
    return lax.dot_general(a, b, (((0,), (0,)), ((), ())), preferred_element_type=F32)


def split(a):
    high = a.astype(B16)
    return high, (a - high.astype(F32))


def exact_dot(ones, a):
    high, rest = split(a)
    mid, rest = split(rest)
    return nn(ones, high) + nn(ones, mid) + nn(ones, rest.astype(B16))


def two_dot(a, ones):
    high, rest = split(a)
    return nn(high, ones) + nn(rest.astype(B16), ones)


def iota(shape, dim):
    return lax.broadcasted_iota(jnp.int32, shape, dim)


def softplus(a):
    return jnp.maximum(a, 0.0) + jnp.log1p(jnp.exp(-jnp.abs(a)))


def three(a, b):
    ah, al = split(a)
    bh, bl = split(b)
    return nt(ah, bh) + nt(al.astype(B16), bh) + nt(ah, bl.astype(B16))


def silu(a):
    return a * jax.nn.sigmoid(a)


def silu_grad(a):
    sig = jax.nn.sigmoid(a)
    return sig * (1.0 + a * (1.0 - sig))


def rms_scale(x):
    return lax.rsqrt(jnp.mean(x * x, axis=1, keepdims=True) + EPSILON)


def total(refs):
    out = refs[0][...].astype(F32)
    for extra in refs[1:]:
        out = out + extra[...].astype(F32)
    return out


def boundary(starts, base):
    found = False
    for k in range(starts.shape[0]):
        at = starts[k]
        found = found | ((at > 0) & (at > base - 3) & (at < base + Q + 3))
    return found


def prep_kernel(place, w_bt, conv, bias, gain, out):
    span, d = w_bt.shape
    quarter = span // 4
    side = lax.rem(lax.div(place[1], 2), 4)
    out[0:quarter, :] = w_bt[pl.ds(pl.multiple_of(side * quarter, quarter), quarter), :]
    rows = jnp.concatenate([conv[...], bias[...].reshape(1, span), jnp.zeros((11, span), F32)], axis=0)
    high, rest = split(rows)
    mid, rest = split(rest)
    wide = jnp.concatenate(
        [high.astype(F32), mid.astype(F32), rest, jnp.zeros((16, d - 3 * span), F32)], axis=1
    )
    row = jnp.concatenate(
        [gain[...].astype(F32).reshape(1, gain.shape[0]), jnp.zeros((1, d - gain.shape[0]), F32)],
        axis=1,
    )
    wide = jnp.where(iota((16, d), 0) == 5, row, wide)
    out[quarter:, :] = wide.astype(B16)


def stack_kernel(*refs):
    *ins, out = refs
    rows = out.shape[0] // len(ins)
    for k, ref in enumerate(ins):
        out[k * rows : (k + 1) * rows, :] = ref[0:rows, :]


def front_kernel(heads, n, place, starts, *refs):
    xs, halos, earlies = refs[:n], refs[n : 2 * n], refs[2 * n : 3 * n]
    bts = refs[3 * n : 3 * n + 4]
    (
        w_in, w_step, conv_i, bias_i, sbias, dlog, skips, ngain, tri, e_step, e_enter, e_end,
        normed_o, vals_o, bvals_o, pre_o, bpre_o, bc_o, pk_o, pk2_o, cumt_o, scaled_o, sent_o,
        dp_o, fin_o, hv_o, hn_o, tok_o, docrow_o, taps, gain, hp, w_s, vec,
        ext, state, prod, w_bt, x,
    ) = refs[3 * n + 4 :]
    c = pl.program_id(0)
    inner = w_in.shape[1]
    full = ext.shape[1]
    span = w_bt.shape[0] // n
    quarter = span // 4
    gain_own = gain.shape[1] // n
    w = place[0]
    side = lax.rem(lax.div(place[1], 2), 4)

    def project(values):
        wide = values.astype(F32)
        return (wide * rms_scale(wide) * gain[0:1, :]).astype(B16)

    @pl.when(c == 0)
    def _():
        taps[0:4, 0:inner] = conv_i[...]
        taps[4:5, 0:inner] = bias_i[...].reshape(1, inner)
        taps[5:8, :] = jnp.zeros((3, full), F32)
        hp[...] = jnp.zeros_like(hp)
        for g in range(16):
            lanes = slice(8 * g, 8 * g + heads)
            hp[0:1, lanes] = sbias[...].reshape(1, heads)
            hp[1:2, lanes] = jnp.exp(dlog[...].reshape(1, heads))
        low = iota((1, 128), 1) < 64
        for p in range(heads // 2):
            one, two = (jnp.broadcast_to(skips[...].reshape(1, heads)[:, h : h + 1], (1, 128)) for h in (2 * p, 2 * p + 1))
            vec[0:1, p * 128 : (p + 1) * 128] = jnp.where(low, one, two)
        vec[1:2, :] = ngain[...].reshape(1, inner)
        copies = (iota((heads, 128), 0) == lax.rem(iota((heads, 128), 1), 8)).astype(F32)
        w_s[...] = nn(w_step[...], copies.astype(B16)).astype(B16)
        for k in range(n):
            v = lax.rem(w - k + n, n)
            for q in range(4):
                at = v * span + (side ^ q) * quarter
                w_bt[pl.ds(pl.multiple_of(at, quarter), quarter), :] = bts[q][
                    k * quarter : (k + 1) * quarter, :
                ]
        for v in range(n):
            for k in range(n):

                @pl.when(lax.rem(w - v + n, n) == k)
                def _(v=v, k=k):
                    low = inner + v * span
                    small = earlies[k][quarter:, :].astype(F32)
                    taps[0:5, low : low + span] = (
                        small[0:5, 0:span] + small[0:5, span : 2 * span]
                    ) + small[0:5, 2 * span : 3 * span]
                    gain[0:1, v * gain_own : (v + 1) * gain_own] = small[5:6, 0:gain_own]

        hn = project(total(halos))
        hn_o[...] = hn
        ext[0:8, 0:inner] = nn(hn, w_in[...])
        ext[0:8, inner:full] = nt(hn, w_bt[...])
        hv_o[...] = ext[0:8, :]
        state[...] = jnp.zeros_like(state)
        prod[...] = jnp.ones_like(prod)

    @pl.when(c > 0)
    def _():
        ext[0:8, :] = ext[Q : Q + 8, :]

    for k in range(n):

        @pl.when(lax.rem(w - c + n, n) == k)
        def _(k=k):
            x[...] = xs[k][...]

    def docs_at(positions):
        found = jnp.zeros(positions.shape, jnp.int32)
        for k in range(starts.shape[0]):
            found = found + (starts[k] <= positions).astype(jnp.int32)
        return found - 1

    base = (place[1] * pl.num_programs(0) + c) * Q
    here = base + iota((Q, 8), 0)
    lane = iota((Q, 8), 1)
    other = jnp.where(lane < 3, here - 3 + lane, jnp.where(lane == 3, base - 1, base + Q - 1))
    docs = docs_at(here)
    tok = jnp.where(lane == 5, docs, (docs_at(other) == docs).astype(jnp.int32)).astype(F32)
    tok_o[...] = tok
    docrow_o[...] = docs_at(base + iota((8, Q), 1)).astype(F32)

    normed = project(x[...])
    normed_o[...] = normed
    ext[8 : Q + 8, 0:inner] = nn(normed, w_in[...])
    ext[8 : Q + 8, inner:full] = nt(normed, w_bt[...])
    vals_o[...] = ext[8 : Q + 8, 0:inner].astype(B16)
    bvals_o[...] = ext[8 : Q + 8, inner:full].astype(B16)
    pre = taps[4:5, :] + taps[3:4, :] * ext[8 : Q + 8, :]
    for k in range(3):
        pre = pre + taps[k : k + 1, :] * ext[5 + k : 5 + k + Q, :]
    pre_o[...] = pre[:, :inner]
    bpre_o[...] = pre[:, inner:]

    @pl.when(boundary(starts, base))
    def _():
        again = taps[4:5, :] + taps[3:4, :] * ext[8 : Q + 8, :]
        for k in range(3):
            again = again + taps[k : k + 1, :] * ext[5 + k : 5 + k + Q, :] * tok_o[:, k : k + 1]
        pre_o[...] = again[:, :inner]
        bpre_o[...] = again[:, inner:]

    act = silu(pre_o[...])
    bc = silu(bpre_o[...]).astype(B16)
    bc_o[...] = bc
    sr = nn(normed, w_s[...]) + hp[0:1, :]
    step = softplus(sr)
    cums = exact_dot(tri[...], -hp[1:2, :] * step)
    enter = jnp.exp(cums) * tok[:, 3:4]
    end = jnp.exp(cums[Q - 1 : Q, :] - cums) * tok[:, 4:5]
    lane = iota((Q, 128), 1)
    group = lax.rem(lane, 64) // 8
    pk = jnp.where(
        group == STEP, step,
        jnp.where(
            group == ENTER, enter,
            jnp.where(group == END, end, jnp.where(group == SIG, jax.nn.sigmoid(sr), cums)),
        ),
    )
    pk_o[...] = pk
    high, low = split(pk)
    pk2 = jnp.where(lane < 64, high.astype(F32), low).astype(B16)
    pk2_o[...] = pk2
    cumt_o[...] = cums.T[0:8, :]
    scaled = nn(pk2, e_step[...]) * act
    scaled_o[...] = scaled.astype(B16)
    x16, x_lo = split(nn(pk2, e_end[...]) * scaled)
    x_lo = x_lo.astype(B16)
    carry = nn(pk2[Q - 16 :], e_enter[...])[15:16, :]
    sent_o[0] = state[...]
    dp_o[0] = prod[...]
    state[...] = carry * state[...] + tn(bc[:, :128], x16) + tn(bc[:, :128], x_lo)
    prod[...] = prod[...] * carry
    fin_o[0:128, :] = state[...].astype(B16)
    fin_o[128:144, :] = jnp.concatenate([prod[...], prod[...]], axis=0).astype(B16)


def intra_kernel(heads, normed, w_gate, pre, bc, pk, cumt, scaled, tok, docrow, vec, gate_o, y_o):
    gate_o[...] = nn(normed[...], w_gate[...])
    low = iota((HALF, 128), 1) < 64
    for block in range(2):
        rows = slice(block * HALF, (block + 1) * HALF)
        wide = (block + 1) * HALF
        scores = nt(bc[rows, 128:], bc[:wide, :128])
        mask = (block * HALF + iota((HALF, wide), 0) >= iota((HALF, wide), 1)) & (
            tok[rows, 5:6] == docrow[0:1, :wide]
        )
        for pair in range(heads // 2):
            cols = slice(pair * 128, (pair + 1) * 128)
            values = scaled[:wide, cols]
            outs = []
            for h in (2 * pair, 2 * pair + 1):
                diff = pk[rows, 8 * CUMS + h : 8 * CUMS + h + 1] - cumt[h : h + 1, :wide]
                mix = scores * jnp.where(mask, jnp.exp(diff), 0.0)
                outs.append(nn(mix.astype(B16), values))
            y_o[rows, cols] = jnp.where(low, *outs) + vec[0:1, cols] * silu(pre[rows, cols])


def fold_states(keep, others, out):
    state = jnp.zeros(out.shape, F32)
    for ref in reversed(others):
        state = ref[128:129, :].astype(F32) * state + ref[0:128, :].astype(F32)
    out[...] = keep[128:129, :] * state + keep[0:128, :]


def pair_kernel(reverse, place, own, other, keep_o, total_o):
    mine, theirs = own[...].astype(F32), other[...].astype(F32)
    earlier = lax.rem(place[1], 2) == (0 if reverse else 1)
    keep_o[0:128, :] = jnp.where(earlier, theirs[0:128, :], 0.0)
    keep_o[128:, :] = jnp.where(earlier, theirs[128:136, :], 1.0)
    total_o[0:128, :] = jnp.where(
        earlier,
        mine[128:129, :] * theirs[0:128, :] + mine[0:128, :],
        theirs[128:129, :] * mine[0:128, :] + theirs[0:128, :],
    ).astype(B16)
    total_o[128:, :] = (mine[128:, :] * theirs[128:, :]).astype(B16)


def join_kernel(n, m, place, y, gate, bc, pk2, sent, dp, keep, *refs):
    others, cots = refs[:m], refs[m : m + n]
    w_out, vec, e_enter, ssd_o, inter_o, gn_o, stats_o, s_in, cot_o = refs[m + n : m + n + 9]
    mixes = refs[m + n + 9 :]
    c = pl.program_id(0)
    inner = y.shape[1]

    @pl.when(c == 0)
    def _():
        fold_states(keep, others, s_in)

    for k in range(n):

        @pl.when(lax.rem(place[0] - c + n, n) == k)
        def _(k=k):
            cot_o[...] = cots[k][...]

    entering = sent[0] + dp[0, 0:1, :] * s_in[...]
    inter = nn(pk2[...], e_enter[...]) * nn(bc[:, 128:], entering.astype(B16))
    inter_o[...] = inter
    ssd = y[...] + inter
    ssd_o[...] = ssd
    gated = ssd * silu(gate[...])
    mixed = nn((gated * vec[1:2, :]).astype(B16), w_out[...]).astype(B16)
    for k in range(n):

        @pl.when(lax.rem(c - place[0] + n, n) == k)
        def _(k=k):
            mixes[k][...] = mixed

    gn = nt(cot_o[...], w_out[...])
    gn_o[...] = gn
    lane = iota((inner, 128), 1)
    first = (lane == 0).astype(F32).astype(B16)
    second = (lane == 1).astype(F32).astype(B16)
    both = two_dot(gated * gated, first)
    both = both + two_dot(vec[1:2, :] * gn * gated, second)
    stats_o[...] = both.T[0:8, :]


def gate_kernel(n, width_all, ssd, gate, gn, vec, pre, bc, pk2, e_enter, *refs):
    stats = refs[:n]
    norm_o, gate_o, gs_o, sums_o, sb_o, db_o, fin_o, rms_o, state, prod = refs[n:]
    i = pl.program_id(0)

    @pl.when(i == 0)
    def _():
        state[...] = jnp.zeros_like(state)
        prod[...] = jnp.ones_like(prod)
        sums_o[...] = jnp.zeros_like(sums_o)

    st = total(stats)
    rms = lax.rsqrt(st[0:1, :] / width_all + EPSILON)
    pull = rms * rms * rms * st[1:2, :] / width_all
    st = jnp.concatenate([rms, pull, jnp.zeros((126, Q), F32)], axis=0).T
    rms, pull = st[:, 0:1], st[:, 1:2]
    rms_o[...] = st[:, 0:8]
    g = gate[...]
    sig = jax.nn.sigmoid(g)
    s = ssd[...]
    act_g = g * sig
    gated = s * act_g
    scaled = gated * rms
    ngain = vec[1:2, :]
    norm_o[...] = (scaled * ngain).astype(B16)
    gn_ = gn[...]
    grad_gated = rms * (ngain * gn_) - gated * pull
    gs = grad_gated * act_g
    gs_o[...] = gs
    gate_o[...] = (grad_gated * s * (sig * (1.0 + g * (1.0 - sig)))).astype(B16)
    sums_o[0:1, :] += jnp.sum(gn_ * scaled, axis=0, keepdims=True)
    sums_o[1:2, :] += jnp.sum(gs * silu(pre[...]), axis=0, keepdims=True)
    enter = nn(pk2[...], e_enter[...])
    carry = enter[Q - 1 : Q, :]
    sb_o[0] = state[...]
    db_o[0] = prod[...]
    state[...] = carry * state[...] + tn(bc[:, 128:], (enter * gs).astype(B16)) + tn(bc[:, 128:], split(enter * gs)[1].astype(B16))
    prod[...] = prod[...] * carry
    fin_o[0:128, :] = state[...].astype(B16)
    fin_o[128:144, :] = jnp.concatenate([prod[...], prod[...]], axis=0).astype(B16)


def intra_back_kernel(
    heads, gs, bc, pk, pk2, cumt, scaled, tok, docrow, sent, dp, s_in, e_enter,
    gsc_o, rc_o, gbc_o, tot, plus, minus,
):
    low = iota((HALF, 128), 1) < 64
    g16 = gs[...].astype(B16)
    plus[...] = jnp.zeros_like(plus)
    for block in range(2):
        rows = slice(block * HALF, (block + 1) * HALF)
        wide = slice(block * HALF, Q)
        width = Q - block * HALF
        scores = nt(bc[rows, :128], bc[wide, 128:])
        mask = (iota((HALF, width), 0) <= iota((HALF, width), 1)) & (
            tok[rows, 5:6] == docrow[0:1, wide]
        )
        sums = jnp.zeros((HALF, width), F32)
        lane = iota((HALF, 128), 1)
        minus_acc = jnp.zeros((HALF, 128), F32)
        for pair in range(heads // 2):
            cols = slice(pair * 128, (pair + 1) * 128)
            mine = scaled[rows, cols]
            grads = g16[wide, cols]
            outs = []
            for h in (2 * pair, 2 * pair + 1):
                diff = cumt[h : h + 1, wide] - pk[rows, 8 * CUMS + h : 8 * CUMS + h + 1]
                decay = jnp.where(mask, jnp.exp(diff), 0.0)
                keep = low if h % 2 == 0 else ~low
                masked = jnp.where(keep, mine.astype(F32), 0.0).astype(B16)
                weighted = decay * nt(masked, grads)
                sums = sums + weighted
                ws = scores * weighted
                plus[h : h + 1, wide] += jnp.sum(ws, axis=0, keepdims=True)
                minus_acc = jnp.where(
                    lax.rem(lane, 8) == h, jnp.sum(ws, axis=1, keepdims=True), minus_acc
                )
                outs.append(nn((scores * decay).astype(B16), grads))
            gsc_o[rows, cols] = jnp.where(low, *outs)
        minus[rows, :] = minus_acc
        tot[rows, wide] = sums.astype(B16)
    tot[HALF:, :HALF] = jnp.zeros((HALF, HALF), B16)
    rc_o[...] = jnp.concatenate([plus[...]] * 16, axis=0).T - minus[...]
    entering = sent[0] + dp[0, 0:1, :] * s_in[...]
    t16 = tot[...]
    enter = nn(pk2[...], e_enter[...]) * gs[...]
    gbc_o[:, :128] = nn(t16, bc[:, 128:])
    gbc_o[:, 128:] = tn(t16, bc[:, :128]) + three(enter, entering)


def conv_back(i, count, masked, gp, tok, taps, vals, hv, ext, mext, shift, out, sums_o, rim_o):
    ch = gp.shape[1]

    @pl.when(i == 0)
    def _():
        ext[Q : Q + 8, :] = jnp.zeros((8, ch), F32)
        mext[Q : Q + 8, :] = jnp.zeros((8, 8), F32)
        sums_o[...] = jnp.zeros_like(sums_o)

    @pl.when(i > 0)
    def _():
        ext[Q : Q + 8, :] = ext[0:8, :]
        mext[Q : Q + 8, :] = mext[0:8, :]

    ext[0:Q, :] = gp
    mext[0:Q, :] = tok
    sums_o[4:5, :] += jnp.sum(gp, axis=0, keepdims=True)

    def sweep(use_mask):
        vals_ = vals.astype(F32)
        acc = jnp.zeros((Q, ch), F32)
        for k in range(4):
            z = ext[3 - k : 3 - k + Q, :]
            if k < 3 and use_mask:
                z = z * mext[3 - k : 3 - k + Q, k : k + 1]
            acc = acc + taps[k : k + 1, :] * z
            sums_o[k : k + 1, :] += jnp.sum(vals_ * z, axis=0, keepdims=True)
        out[...] = acc.astype(B16)

    @pl.when(masked)
    def _():
        sweep(True)

    @pl.when(jnp.logical_not(masked))
    def _():
        sweep(False)

    @pl.when(i == count - 1)
    def _():
        rim = jnp.zeros((8, ch), F32)
        shift[0:8, :] = jnp.zeros((8, ch), F32)
        for k in range(3):
            shift[8:16, :] = ext[0:8, :] * mext[0:8, k : k + 1]
            moved = shift[3 - k : 11 - k, :]
            rim = rim + taps[k : k + 1, :] * moved
            sums_o[k : k + 1, :] += jnp.sum(hv * moved, axis=0, keepdims=True)
        rim_o[...] = rim


def chunk_base(place, count, i):
    return (place[1] * count + (count - 1 - i)) * Q


def bcoef_back_kernel(
    count, n, m, place, starts, gbc, pre, vals, pk2, scaled, tok, sb, db, taps, hv, e_end,
    keep, *refs
):
    others, packs = refs[:m], refs[m : m + n]
    sums_o, s_after, ext, mext, shift, rim_o, out, pieces = refs[m + n :]
    i = pl.program_id(0)
    inner = scaled.shape[1]

    @pl.when(i == 0)
    def _():
        fold_states(keep, others, s_after)

    after_ = sb[0] + db[0, 0:1, :] * s_after[...]
    x16 = nn(pk2[...], e_end[...]) * scaled[...].astype(F32)
    gbm = gbc[:, :128] + three(x16, after_)
    gp = jnp.concatenate([gbm, gbc[:, 128:]], axis=1) * silu_grad(pre[...])
    conv_back(
        i, count, boundary(starts, chunk_base(place, count, i)), gp, tok[...],
        taps[:, inner:], vals[...], hv[:, inner:], ext, mext, shift, out, sums_o, rim_o,
    )
    span = 256 // n
    row = pl.multiple_of((count - 1 - i) * HALF, HALF)
    for v in range(n):
        piece = out[:, v * span : (v + 1) * span]
        pieces[v] = jnp.concatenate([piece[:HALF], piece[HALF:]], axis=1)
    for k in range(n):
        packs[k][pl.ds(row, HALF), :] = pieces[lax.rem(place[0] + k, n)]

    @pl.when(i == count - 1)
    def _():
        for v in range(n):
            edge = rim_o[:, v * span : (v + 1) * span]
            pieces[v, 0:16, 0:span] = jnp.concatenate([edge, edge], axis=0).astype(B16)
        for k in range(n):
            packs[k][count * HALF :, :] = pieces[lax.rem(place[0] + k, n), 0:16, :]


def inner_back_kernel(
    count, place, starts, gs, gsc, rc, inter, pre, vals, bc, pk, pk2, scaled, tok, sent,
    dp, s_in, sb, db, s_after, taps, hp, hv, vec, tri, e_step, e_enter, e_end, hmap,
    gv_o, step_o, rim_o, sums_o, small_o, ext, mext, shift,
):
    i = pl.program_id(0)
    entering = sent[0] + dp[0, 0:1, :] * s_in[...]
    after_ = sb[0] + db[0, 0:1, :] * s_after[...]
    p = pre[...]
    sig_p = jax.nn.sigmoid(p)
    act = p * sig_p
    weights = pk2[...]
    end_state = nn(weights, e_end[...]) * nn(bc[:, :128], after_.astype(B16))
    gsc_ = gsc[...] + end_state
    grad = gs[...]
    end_terms = scaled[...].astype(F32) * end_state
    carry = nn(weights[Q - 16 :], e_enter[...])[15:16, :]
    closing = jnp.sum(end_terms, axis=0, keepdims=True) + carry * jnp.sum(
        after_ * entering, axis=0, keepdims=True
    )
    closing = two_dot(jnp.broadcast_to(closing, (8, closing.shape[1])), hmap[...])[0:1, :]
    grad_cums = rc[...] + two_dot(grad * inter[...] - end_terms, hmap[...])
    grad_cums = grad_cums + jnp.where(iota((Q, 128), 0) == Q - 1, closing, 0.0)
    high, low = split(grad_cums)
    grad_decay = tn(tri[...], high) + tn(tri[...], low.astype(B16))
    drive = hp[1:2, :] * grad_decay
    raw = (nn((gsc_ * act).astype(B16), hmap[...]) - drive) * pk[...]
    lane = iota((Q, 128), 1)
    step_o[...] = jnp.where(lane // 8 == SIG, raw, 0.0).astype(B16)

    @pl.when(i == 0)
    def _():
        small_o[...] = jnp.zeros_like(small_o)

    small_o[0:1, :] += jnp.sum(raw, axis=0, keepdims=True)
    small_o[1:2, :] -= jnp.sum(drive * pk[...], axis=0, keepdims=True)
    gp = (nn(weights, e_step[...]) * gsc_ + vec[0:1, :] * grad) * (
        sig_p * (1.0 + p * (1.0 - sig_p))
    )
    conv_back(
        i, count, boundary(starts, chunk_base(place, count, i)), gp, tok[...], taps[...],
        vals[...], hv[...], ext, mext, shift, gv_o, sums_o, rim_o,
    )


def gate_grads_kernel(place, gnorm, normed, gate16, cot, keep_o, send_o):
    r = pl.program_id(0)
    core = lax.rem(place[1], 2)
    inner = gate16.shape[1]
    left = tn(normed[...], gate16[...]).astype(B16)
    right = tn(gnorm[...], cot[...]).astype(B16)

    @pl.when(r == core)
    def _():
        keep_o[:, 0:inner] = left
        keep_o[:, inner:] = right

    @pl.when(r != core)
    def _():
        send_o[:, 0:inner] = left
        send_o[:, inner:] = right


def inner_grads_kernel(
    place, gv, gv_all, rim, hn, gate16, step16, normed, w_in, w_gate, w_s, part_o, keep_o, send_o
):
    r = pl.program_id(0)
    core = lax.rem(place[1], 2)
    part_o[...] = nt(gv[...], w_in[...]) + nt(gate16[...], w_gate[...]) + nt(step16[...], w_s[...])
    grads = (tn(normed[...], gv_all[...]) + tn(hn[...], rim[...].astype(B16))).astype(B16)

    @pl.when(r == core)
    def _():
        keep_o[...] = grads

    @pl.when(r != core)
    def _():
        send_o[...] = grads


def bcoef_grads_kernel(count, n, pack_view, tail_view, place, *refs):
    packs = [pack_view(ref, pl.program_id(0), (place,)) for ref in refs[:n]]
    tails = [tail_view(ref, 0, (place,)) for ref in refs[:n]]
    (
        rim_i, hn, part, normed, w_bt, w_in, step16, gain, csum_b, csum_i, ssum, nsums,
    ) = refs[n : n + 12]
    parts = refs[n + 12 : 2 * n + 12]
    keep_o, send_o, small_o, local_o, acc, gsum = refs[2 * n + 12 :]
    i = pl.program_id(0)
    span, d = w_bt.shape
    inner = w_in.shape[1]

    @pl.when(i == 0)
    def _():
        rim16 = total(tails)[0:8, :span].astype(B16)
        edge = nn(rim16, w_bt[...]) + nt(rim_i[...].astype(B16), w_in[...])
        small_o[3:8, :] = edge[3:8, :]
        gsum[...] = jnp.sum(edge * hn[...].astype(F32), axis=0, keepdims=True)
        acc[...] = tn(jnp.concatenate([rim16, jnp.zeros((8, span), B16)], axis=1), hn[...])

    packed = total(packs)
    v16 = jnp.concatenate([packed[:, :span], packed[:, span:]], axis=0).astype(B16)
    sums = part[...] + nn(v16, w_bt[...])
    for k in range(n):

        @pl.when(i == k)
        def _(k=k):
            parts[k][...] = sums.astype(B16)

    x16 = normed[...]
    gsum[...] += jnp.sum(sums * x16.astype(F32), axis=0, keepdims=True)
    acc[...] += tn(jnp.concatenate([v16, step16[:, :span]], axis=1), x16)

    @pl.when(i == count - 1)
    def _():
        turned = acc[...].T.astype(B16)
        core = lax.rem(place[1], 2)
        half = d // 2

        @pl.when(core == 0)
        def _():
            keep_o[...] = turned[:half]
            send_o[...] = turned[half:]

        @pl.when(core == 1)
        def _():
            keep_o[...] = turned[half:]
            send_o[...] = turned[:half]

        small_o[0:1, :] = gsum[...] / gain[0:1, :]
        for k in range(3):
            small_o[1:2, k * 256 : (k + 1) * 256] = csum_b[k : k + 1, :]
            local_o[3 + k : 4 + k, 0:inner] = csum_i[2 * k : 2 * k + 1, :]
        for k in range(2):
            small_o[2:3, k * 256 : (k + 1) * 256] = csum_b[3 + k : 4 + k, :]
            local_o[3 + k : 4 + k, inner:] = csum_i[2 * k + 1 : 2 * k + 2, :]
        local_o[5:6, inner:] = nsums[1:2, :]
        local_o[6:7, 0:inner] = nsums[0:1, :]
        local_o[6:7, inner : inner + 128] = ssum[0:1, :]
        local_o[6:7, inner + 128 : inner + 256] = ssum[1:2, :]


def small_kernel(local, *refs):
    *ins, small_o, edge_o = refs
    both = total(ins)
    small_o[0:3, :] = both[0:3, :]
    small_o[3:8, :] = local[3:8, :]
    edge_o[0:3, :] = jnp.zeros((3, both.shape[1]), F32)
    edge_o[3:8, :] = both[3:8, :]


def last_kernel(n, place, x, cot, gain, edge, rms, *refs):
    parts, mixes, (grad_o, block_o) = refs[:n], refs[n : 2 * n], refs[2 * n :]
    sums = total(parts)
    rows = sums.shape[0]
    sums = jnp.concatenate([sums[: rows - 8], sums[rows - 8 :] + edge[...]], axis=0)
    wide = x[...].astype(F32)
    own = rms[pl.ds(pl.multiple_of(place[0] * rows, rows), rows), 0:1]
    block_o[...] = (wide + own * total(mixes)).astype(B16)
    scale = rms_scale(wide)
    scaled = gain[0:1, :] * sums
    dot = jnp.sum(scaled * wide, axis=1, keepdims=True)
    width = wide.shape[1]
    grad_o[...] = (
        cot[...].astype(F32) + scale * scaled - wide * (scale * scale * scale * dot / width)
    )


def add_kernel(a, b, out):
    out[...] = a[...] + b[...]


def ends_kernel(n, heads, place, *refs):
    smalls = refs[:n]
    gain_o, taps_i_o, taps_b_o, bias_i_o, bias_b_o, sbias_o, dlog_o, skip_o, ngain_o = refs[n:]
    sums = total(smalls)
    inner, span = ngain_o.shape[0], bias_b_o.shape[0]
    count, own = 256 // span, gain_o.shape[0]
    for v in range(count):

        @pl.when(place[0] == v)
        def _(v=v):
            gain_o[...] = sums[0:1, v * own : (v + 1) * own].reshape(own)
            low = v * span
            for k in range(4):
                row, at = (1, 256 * k) if k < 3 else (2, 0)
                taps_b_o[k : k + 1, :] = sums[row : row + 1, at + low : at + low + span]
            bias_b_o[...] = sums[2:3, 256 + low : 256 + low + span].reshape(span)

    taps_i_o[0:1, :] = sums[3:4, :inner]
    taps_i_o[1:2, :] = sums[3:4, inner:]
    taps_i_o[2:3, :] = sums[4:5, :inner]
    taps_i_o[3:4, :] = sums[4:5, inner:]
    bias_i_o[...] = sums[5:6, :inner].reshape(inner)
    ngain_o[...] = sums[6:7, :inner].reshape(inner)
    raw_at, decay_at = inner + 8 * SIG, inner + 128 + 8 * STEP
    sbias_o[...] = sums[6:7, raw_at : raw_at + heads].reshape(heads)
    dlog_o[...] = sums[6:7, decay_at : decay_at + heads].reshape(heads)
    hit = iota((8, inner), 1) // (inner // heads) == iota((8, inner), 0)
    rows = jnp.where(hit, sums[5:6, inner:], 0.0)
    column = jnp.sum(rows, axis=1, keepdims=True)
    skip_o[...] = jnp.broadcast_to(column, (8, 128)).T[0:1, 0:heads].reshape(heads)


def halves_kernel(n, place, *refs):
    ins, outs = refs[:6], refs[6:]
    rows = outs[0].shape[0]
    for k in range(n):
        piece = pl.ds(pl.multiple_of(lax.rem(lax.div(place[1], 2) + k, n) * rows, rows), rows)
        at = 0
        for j in range(3):
            mine, theirs = ins[2 * j], ins[2 * j + 1]
            cols = slice(at, at + mine.shape[1])
            at += mine.shape[1]
            outs[k][:, cols] = (
                mine[piece, :].astype(F32) + theirs[piece, :].astype(F32)
            ).astype(B16)


def pieces_kernel(*refs):
    refs[-1][...] = total(refs[:-1]).astype(B16)


def unpack_kernel(n, place, *refs):
    pieces = refs[: 2 * n]
    gate_o, inner_o, bcoef_o, step_o, out_o, late = refs[2 * n :]
    rows = pieces[0].shape[0]
    inner = gate_o.shape[1]
    span = bcoef_o.shape[0]
    heads = step_o.shape[0]
    for side in range(2):
        for k in range(n):
            piece = pieces[side * n + k][...].astype(F32)
            whole_half = lax.rem(lax.div(place[1], 2) - k + n, n)
            core = lax.rem(place[1] + side, 2)
            at = pl.multiple_of(core * (n * rows) + whole_half * rows, rows)
            dst = pl.ds(at, rows)
            gate_o[dst, :] = piece[:, 0:inner]
            inner_o[dst, :] = piece[:, 2 * inner : 3 * inner]
            late[dst, :] = piece[:, 3 * inner :]
            low = pl.ds(pl.multiple_of(whole_half * rows, rows), rows)

            @pl.when(core == 0)
            def _():
                out_o[low, 0:inner] = piece[:, inner : 2 * inner]

            @pl.when(core == 1)
            def _():
                out_o[low, inner:] = piece[:, inner : 2 * inner]

    turned = late[...].T
    bcoef_o[...] = turned[:span, :]
    step_o[...] = turned[span + 8 * SIG : span + 8 * SIG + heads, :]


def shape(dims, dtype=F32):
    return jax.ShapeDtypeStruct(dims, dtype)


def call(
    kernel, grid, ins, in_specs, outs, out_specs, scratch=(), scalars=(), flops=0,
    fetch=(),
):
    size = sum(a.size * a.dtype.itemsize for a in ins) + sum(
        o.size * o.dtype.itemsize for o in outs
    )
    views = list(in_specs) + list(out_specs)
    ins = [
        pltpu.with_memory_space_constraint(a, pltpu.HBM) if k in fetch else a
        for k, a in enumerate(ins)
    ]

    landing = [pltpu.VMEM(ins[k].shape, ins[k].dtype) for k in fetch]
    landing += [pltpu.SemaphoreType.DMA((len(fetch),))] if fetch else []

    def body(*refs):
        first = len(scalars)
        step = pl.program_id(0) if grid else 0
        if fetch:
            refs, local, sems = list(refs[: -len(landing)]), refs[-len(landing) : -1], refs[-1]

            sources = [refs[first + k] for k in fetch]

            def copies():
                return [
                    pltpu.make_async_copy(source, local[j], sems.at[j])
                    for j, source in enumerate(sources)
                ]

            def bring():
                for copy in copies():
                    copy.start()
                for copy in copies():
                    copy.wait()

            if grid:
                pl.when(step == 0)(bring)
            else:
                bring()
            for j, k in enumerate(fetch):
                refs[first + k] = local[j]
        seen = [
            view(ref, step, refs[:first]) if view else ref
            for view, ref in zip(views, refs[first:])
        ]
        kernel(*refs[:first], *seen, *refs[first + len(views) :])

    return pl.pallas_call(
        body,
        out_shape=outs,
        grid_spec=pltpu.PrefetchScalarGridSpec(
            num_scalar_prefetch=len(scalars),
            grid=grid,
            in_specs=[HBM if k in fetch else VMEM for k in range(len(ins))],
            out_specs=[VMEM] * len(outs),
            scratch_shapes=list(scratch) + landing,
        ),
        compiler_params=pltpu.CompilerParams(
            dimension_semantics=("arbitrary",) * len(grid) or None,
            vmem_limit_bytes=LIMIT,
        ),
        cost_estimate=pl.CostEstimate(
            flops=int(flops), bytes_accessed=size, transcendentals=0
        ),
    )(*scalars, *ins)


def ring(value, axis, distance):
    count = lax.axis_size(axis)
    return lax.ppermute(value, axis, [(i, (i + distance) % count) for i in range(count)])


def swap(value, axis, bit):
    count = lax.axis_size(axis)
    return lax.ppermute(value, axis, [(i, i ^ (1 << bit)) for i in range(count)])


def spread(value, axis):
    count = lax.axis_size(axis)
    return [value] + [ring(value, axis, k) for k in range(1, count)]


def reduce_parts(parts, axis):
    return [ring(p, axis, k) if k else p for k, p in enumerate(parts)]


def states(fin, place, reverse):
    rows, inner = fin.shape
    count = lax.axis_size("seq")
    other = swap(fin, "seq", 0)
    keep, both = call(
        functools.partial(pair_kernel, reverse), (), [fin, other], [None] * 2,
        [shape((rows - 8, inner)), shape((rows, inner), B16)], [None] * 2,
        scalars=(place,),
    )
    got = []
    for k in range(1, count // 2):
        if reverse:
            pairs = [(i + 2 * k, i) for i in range(count - 2 * k)]
        else:
            pairs = [(i, i + 2 * k) for i in range(count - 2 * k)]
        got.append(lax.ppermute(both, "seq", pairs))
    return keep, got


def per_device(
    block_in,
    in_gain,
    proj_gate,
    proj_inner,
    proj_bcoef,
    proj_step,
    conv_inner,
    conv_inner_bias,
    conv_bcoef,
    conv_bcoef_bias,
    step_bias,
    decay_log,
    skip_gain,
    norm_gain,
    proj_out,
    out_grad,
    doc_starts,
):
    n_wt, n_seq = lax.axis_size("wt"), lax.axis_size("seq")
    w, seq = lax.axis_index("wt"), lax.axis_index("seq")
    rows_own, d = block_in.shape
    length = rows_own * n_wt
    inner = proj_inner.shape[1]
    heads = step_bias.shape[0]
    span = proj_bcoef.shape[1]
    full = inner + span * n_wt
    width_all = inner * n_wt
    count = length // Q
    pairs = n_seq // 2
    place = jnp.stack([w, seq]).astype(jnp.int32)
    scalars = (place, doc_starts)

    w_bt_own = proj_bcoef.T
    quarter = span // 4
    (early,) = call(
        prep_kernel, (), [w_bt_own, conv_bcoef, conv_bcoef_bias, in_gain], [None] * 4,
        [shape((quarter + 16, d), B16)], [None], scalars=(place,),
        fetch=tuple(range(4)),
    )
    earlies = spread(early, "wt")
    rows = spread(block_in, "wt")
    (bts,) = call(
        stack_kernel, (), earlies, [None] * n_wt, [shape((quarter * n_wt, d), B16)], [None],
    )
    bts_x = swap(bts, "seq", 1)
    bts_y = [swap(b, "seq", 2) for b in (bts, bts_x)]
    tail = block_in[rows_own - 8 :]
    halos = []
    for v in range(n_wt):
        halos.append(
            lax.ppermute(
                tail, ("seq", "wt"),
                [((s - 1) * n_wt + n_wt - 1, s * n_wt + v) for s in range(1, n_seq)],
            )
        )
    cots = spread(out_grad, "wt")

    lanes, chans = np.arange(128), np.arange(inner) // (inner // heads)

    def one_hot(group):
        hit = ((lanes % 64) // 8 == group)[:, None] & ((lanes % 8)[:, None] == chans[None, :])
        return jnp.asarray(hit.astype(np.float32), B16)

    e_step, e_enter, e_end = one_hot(STEP), one_hot(ENTER), one_hot(END)
    hmap = jnp.asarray((chans[:, None] == (lanes % 8)[None, :]).astype(np.float32), B16)
    tri = jnp.asarray((np.arange(Q)[:, None] >= np.arange(Q)[None, :]).astype(np.float32), B16)

    grid = (count,)

    def at_rows(ref, index, rows=Q):
        return ref.at[pl.ds(pl.multiple_of(index * rows, rows), rows), :]

    def by_rows(reverse=False):
        if reverse:
            return lambda ref, i, p: at_rows(ref, count - 1 - i)
        return lambda ref, i, p: at_rows(ref, i)

    def by_turn():
        return lambda ref, i, p: at_rows(ref, lax.rem(i + p[0][0], count))

    def whole(*dims):
        return None

    def by_chunk(*dims, reverse=False):
        if reverse:
            return lambda ref, i, p: ref.at[pl.ds(count - 1 - i, 1)]
        return lambda ref, i, p: ref.at[pl.ds(i, 1)]

    def by_lanes(width, reverse=False):
        def view(ref, i, p):
            index = count - 1 - i if reverse else i
            return ref.at[:, pl.ds(pl.multiple_of(index * width, width), width)]

        return view

    def lead(ref, i, p):
        return ref.at[:, :inner]

    by_cols = by_lanes(Q)
    by_cols_back = by_lanes(Q, True)
    fin_spec, state_spec = whole(144, inner), whole(128, inner)
    e_spec = whole(128, inner)
    states_out = [shape((count, 128, inner)), shape((count, 8, inner)), shape((144, inner), B16)]
    (normed, vals, bvals, pre, bpre, bc, pk, pk2, cumt, scaled, sent, dp, fin, hv, hn, tok,
     docrow, taps, gain, hp, w_s, vec) = call(
        functools.partial(front_kernel, heads, n_wt), grid,
        [*rows, *halos, *earlies, bts, bts_x, *bts_y, proj_inner, proj_step, conv_inner,
         conv_inner_bias, step_bias, decay_log, skip_gain, norm_gain, tri, e_step, e_enter,
         e_end],
        [None] * (3 * n_wt + 16),
        [shape((length, d), B16), shape((length, inner), B16), shape((length, 256), B16),
         shape((length, inner)), shape((length, 256)),
         shape((length, 256), B16), shape((length, 128)), shape((length, 128), B16),
         shape((8, length)), shape((length, inner), B16), *states_out,
         shape((8, full)), shape((8, d), B16), shape((length, 8)), shape((8, length)),
         shape((8, full)), shape((8, d)), shape((8, 128)), shape((d, 128), B16),
         shape((8, inner))],
        [by_rows(), by_rows(), by_rows(), by_rows(), by_rows(), by_rows(),
         by_rows(), by_rows(),
         by_cols, by_rows(), by_chunk(128, inner), by_chunk(8, inner), fin_spec,
         whole(8, full), whole(8, d), by_rows(), by_cols, whole(8, full), whole(8, d),
         None, None, None],
        scratch=[pltpu.VMEM((Q + 8, full), F32), pltpu.VMEM((128, inner), F32),
                 pltpu.VMEM((8, inner), F32), pltpu.VMEM((span * n_wt, d), B16),
                 pltpu.VMEM((Q, d), B16)],
        scalars=scalars, flops=2e9,
        fetch=(0, *range(3 * n_wt + 4, 3 * n_wt + 16)),
    )
    keep, got = states(fin, place, False)
    gate, y = call(
        functools.partial(intra_kernel, heads), grid,
        [normed, proj_gate, pre, bc, pk, cumt, scaled, tok, docrow, vec],
        [by_rows(), whole(d, inner), by_rows(), by_rows(), by_rows(), by_cols,
         by_rows(), by_rows(), by_cols, whole(1, inner)],
        [shape((length, inner)), shape((length, inner))],
        [by_rows(), by_rows()], flops=2e9,
    )
    got_spec = [whole(136, inner)] + [fin_spec] * (pairs - 1)
    ssd, inter, gn, stats, s_in, cot, *mixes = call(
        functools.partial(join_kernel, n_wt, pairs - 1), grid,
        [y, gate, bc, pk2, sent, dp, keep, *got, *cots, proj_out, vec, e_enter],
        [by_rows(), by_rows(), by_rows(), by_rows(),
         by_chunk(128, inner), by_chunk(8, inner), *got_spec]
        + [whole(Q, d)] * n_wt + [whole(inner, d), whole(1, inner), e_spec],
        [shape((length, inner))] * 3
        + [shape((8, length)), shape((128, inner)), shape((length, d), B16)]
        + [shape((Q, d), B16)] * n_wt,
        [by_rows()] * 3 + [by_cols, state_spec, by_rows()] + [None] * n_wt,
        scalars=(place,), flops=2e9,
    )
    gnorm, gate16, gs, nsums, sb, db, back_fin, rms = call(
        functools.partial(gate_kernel, n_wt, width_all), grid,
        [ssd, gate, gn, vec, pre, bc, pk2, e_enter, *spread(stats, "wt")],
        [by_rows(True)] * 3
        + [whole(1, inner), by_rows(True), by_rows(True), by_rows(True), e_spec]
        + [by_cols_back] * n_wt,
        [shape((length, inner), B16), shape((length, inner), B16), shape((length, inner)),
         shape((8, inner)), *states_out, shape((length, 8))],
        [by_rows(True)] * 3
        + [whole(8, inner), by_chunk(128, inner, reverse=True), by_chunk(8, inner, reverse=True),
           fin_spec, by_rows(True)],
        scratch=[pltpu.VMEM((128, inner), F32), pltpu.VMEM((8, inner), F32)],
        flops=1e9,
    )
    keep_b, got_b = states(back_fin, place, True)
    gsc, rc, gbc = call(
        functools.partial(intra_back_kernel, heads), grid,
        [gs, bc, pk, pk2, cumt, scaled, tok, docrow, sent, dp, s_in, e_enter],
        [by_rows(), by_rows(), by_rows(), by_rows(), by_cols, by_rows(),
         by_rows(), by_cols, by_chunk(128, inner), by_chunk(8, inner), state_spec, e_spec],
        [shape((length, inner)), shape((length, 128)), shape((length, 256))],
        [by_rows(), by_rows(), by_rows()],
        scratch=[pltpu.VMEM((Q, Q), B16), pltpu.VMEM((8, Q), F32), pltpu.VMEM((Q, 128), F32)],
        flops=4e9,
    )

    half = d // 2
    d_half = by_lanes(half)
    keep_a, send_a = call(
        gate_grads_kernel, (2,), [gnorm, normed, gate16, cot],
        [whole(length, inner), d_half, whole(length, inner), d_half],
        [shape((half, 2 * inner), B16)] * 2, [whole(half, 2 * inner)] * 2,
        scalars=(place,), flops=2e9,
    )
    got_a = swap(send_a, "seq", 0)
    mixes = reduce_parts(mixes, "wt")

    rows_pack = length // 2 + 16
    *packs, csum_b, s_after = call(
        functools.partial(bcoef_back_kernel, count, n_wt, pairs - 1), grid,
        [gbc, bpre, bvals, pk2, scaled, tok, sb, db, taps, hv, e_end,
         keep_b, *got_b],
        [by_rows(True), by_rows(True), by_rows(True), by_rows(True),
         by_rows(True), by_rows(True), by_chunk(128, inner, reverse=True),
         by_chunk(8, inner, reverse=True), whole(8, full), whole(8, full), e_spec, *got_spec],
        [shape((rows_pack, 128), B16)] * n_wt + [shape((8, 256)), shape((128, inner))],
        [whole(rows_pack, 128)] * n_wt + [whole(8, 256), state_spec],
        scratch=[pltpu.VMEM((Q + 8, 256), F32), pltpu.VMEM((Q + 8, 8), F32),
                 pltpu.VMEM((16, 256), F32), pltpu.VMEM((8, 256), F32),
                 pltpu.VMEM((Q, 256), B16), pltpu.VMEM((n_wt, HALF, 128), B16)],
        scalars=scalars, flops=1e9,
    )
    packs = reduce_parts(packs, "wt")
    gv, step16, rim_i, csum_i, ssum = call(
        functools.partial(inner_back_kernel, count), grid,
        [gs, gsc, rc, inter, pre, vals, bc, pk, pk2, scaled, tok, sent, dp, s_in, sb, db,
         s_after, taps, hp, hv, vec, tri, e_step, e_enter, e_end, hmap],
        [by_rows(True), by_rows(True), by_rows(True), by_rows(True),
         by_rows(True), by_rows(True), by_rows(True), by_rows(True),
         by_rows(True), by_rows(True), by_rows(True),
         by_chunk(128, inner, reverse=True), by_chunk(8, inner, reverse=True), state_spec,
         by_chunk(128, inner, reverse=True), by_chunk(8, inner, reverse=True), state_spec,
         lead, whole(8, 128), lead, whole(1, inner), whole(Q, Q), e_spec,
         e_spec, e_spec, whole(inner, 128)],
        [shape((length, inner), B16), shape((length, 128), B16), shape((8, inner)),
         shape((8, inner)), shape((8, 128))],
        [by_rows(True), by_rows(True), whole(8, inner), whole(8, inner),
         whole(8, 128)],
        scratch=[pltpu.VMEM((Q + 8, inner), F32), pltpu.VMEM((Q + 8, 8), F32),
                 pltpu.VMEM((16, inner), F32)],
        scalars=scalars, flops=1e9,
    )
    t_half = lambda: lambda ref, r, p: at_rows(ref, r, length // 2)
    part, keep_i, send_i = call(
        inner_grads_kernel, (2,),
        [gv, gv, rim_i, hn, gate16, step16, normed, proj_inner, proj_gate, w_s],
        [t_half(), whole(length, inner), whole(8, inner),
         d_half, t_half(), t_half(), d_half,
         whole(d, inner), whole(d, inner), whole(d, 128)],
        [shape((length, d)), shape((half, inner), B16), shape((half, inner), B16)],
        [t_half(), whole(half, inner), whole(half, inner)],
        scalars=(place,), flops=2e9,
    )
    got_i = swap(send_i, "seq", 0)
    pack_spec = lambda ref, i, p: at_rows(ref, lax.rem(i + p[0][0], count), HALF)
    tail_spec = lambda ref, i, p: ref.at[length // 2 : length // 2 + 16, :]
    *parts, keep_p, send_p, small, local = call(
        functools.partial(bcoef_grads_kernel, count, n_wt, pack_spec, tail_spec), grid,
        [*packs, rim_i, hn, part, normed, w_bt_own, proj_inner, step16, gain, csum_b,
         csum_i, ssum, nsums],
        [None] * n_wt
        + [whole(8, inner), whole(8, d), by_turn(), by_turn(), whole(span, d),
           whole(d, inner), by_turn(), whole(8, d), whole(8, 256), whole(8, inner),
           whole(8, 128), whole(8, inner)],
        [shape((Q, d), B16)] * n_wt
        + [shape((half, 2 * span), B16)] * 2 + [shape((8, d))] * 2,
        [whole(Q, d)] * n_wt + [whole(half, 2 * span)] * 2 + [whole(8, d)] * 2,
        scratch=[pltpu.VMEM((2 * span, d), F32), pltpu.VMEM((1, d), F32)],
        scalars=(place,), flops=1e9,
    )
    parts = reduce_parts(parts, "wt")
    got_p = swap(send_p, "seq", 0)
    small, edge = call(
        small_kernel, (), [local, *spread(small, "wt")], [None] * (n_wt + 1),
        [shape((8, d))] * 2, [None] * 2,
    )
    edge = lax.ppermute(
        edge, ("seq", "wt"),
        [(s * n_wt + n_wt - 1, (s - 1) * n_wt + n_wt - 1) for s in range(1, n_seq)],
    )
    input_grad, block_out = call(
        functools.partial(last_kernel, n_wt), (),
        [block_in, out_grad, gain, edge, rms, *parts, *mixes], [None] * (5 + 2 * n_wt),
        [shape((rows_own, d)), shape((rows_own, d), B16)], [None] * 2, scalars=(place,),
    )

    def pair_ring(value, k):
        return lax.ppermute(
            value, "seq", [(i, (i + 2 * k) % n_seq) for i in range(n_seq)]
        )

    wide = 3 * inner + 2 * span
    piece_rows = half // pairs
    pieces = call(
        functools.partial(halves_kernel, pairs), (),
        [keep_a, got_a, keep_i, got_i, keep_p, got_p], [None] * 6,
        [shape((piece_rows, wide), B16)] * pairs, [None] * pairs,
        scalars=(place,),
    )
    pieces = [pair_ring(p, k) if k else p for k, p in enumerate(pieces)]
    (piece,) = call(
        pieces_kernel, (), pieces, [None] * pairs, [shape((piece_rows, wide), B16)], [None],
    )
    own = [pair_ring(piece, k) if k else piece for k in range(pairs)]
    theirs = [swap(p, "seq", 0) for p in own]
    g_gate, g_inner, g_bcoef, g_step, g_out = call(
        functools.partial(unpack_kernel, pairs), (1,), [*own, *theirs],
        [whole(piece_rows, wide)] * (2 * pairs),
        [shape((d, inner)), shape((d, inner)), shape((span, d)), shape((heads, d)),
         shape((inner, d))],
        [whole(d, inner), whole(d, inner), whole(span, d), whole(heads, d), whole(inner, d)],
        scratch=[pltpu.VMEM((d, 2 * span), F32)], scalars=(place,),
    )
    (small,) = call(
        add_kernel, (), [small, swap(small, "seq", 0)], [None] * 2,
        [shape((8, d))], [None],
    )
    smalls = [pair_ring(small, k) if k else small for k in range(pairs)]
    (g_gain, g_ci, g_cb, g_cib, g_cbb, g_sbias, g_dlog, g_skip, g_norm) = call(
        functools.partial(ends_kernel, pairs, heads), (), smalls, [None] * pairs,
        [shape((in_gain.shape[0],)), shape((4, inner)), shape((4, span)), shape((inner,)),
         shape((span,)), shape((heads,)), shape((heads,)), shape((heads,)), shape((inner,))],
        [None] * 9, scalars=(place,),
    )
    return (
        block_out,
        input_grad,
        g_gain,
        g_gate,
        g_inner,
        g_bcoef.T,
        g_step.T,
        g_ci,
        g_cb,
        g_cib,
        g_cbb,
        g_sbias,
        g_dlog,
        g_skip,
        g_norm,
        g_out,
    )


def solution(mesh):
    tokens = P(("seq", "wt"), None)
    cols, vec = P(None, "wt"), P("wt")
    return jax.shard_map(
        per_device,
        mesh=mesh,
        in_specs=(
            tokens, vec, cols, cols, cols, cols, cols, vec, cols, vec, vec, vec, vec, vec,
            P("wt", None), tokens, P(),
        ),
        out_specs=(
            tokens, tokens, vec, cols, cols, cols, cols, cols, cols, vec, vec, vec, vec, vec,
            vec, P("wt", None),
        ),
        check_vma=False,
    )
```

```python
import functools

import jax
import jax.numpy as jnp
import numpy as np
from jax import lax
from jax.experimental import pallas as pl
from jax.experimental.pallas import tpu as pltpu
from jax.sharding import PartitionSpec as P

VMEM = pl.BlockSpec(memory_space=pltpu.VMEM)
HBM = pl.BlockSpec(memory_space=pltpu.HBM)
LIMIT = 16 << 20
Q = 256
HALF = Q // 2
STEP, ENTER, END, CUMS, SIG = 0, 1, 2, 4, 5
EPSILON = 1e-05
F32 = jnp.float32
B16 = jnp.bfloat16


def nn(a, b):
    return lax.dot_general(a, b, (((1,), (0,)), ((), ())), preferred_element_type=F32)


def nt(a, b):
    return lax.dot_general(a, b, (((1,), (1,)), ((), ())), preferred_element_type=F32)


def tn(a, b):
    return lax.dot_general(a, b, (((0,), (0,)), ((), ())), preferred_element_type=F32)


def split(a):
    high = a.astype(B16)
    return high, (a - high.astype(F32))


def exact_dot(ones, a):
    high, rest = split(a)
    mid, rest = split(rest)
    return nn(ones, high) + nn(ones, mid) + nn(ones, rest.astype(B16))


def two_dot(a, ones):
    high, rest = split(a)
    return nn(high, ones) + nn(rest.astype(B16), ones)


def iota(shape, dim):
    return lax.broadcasted_iota(jnp.int32, shape, dim)


def softplus(a):
    return jnp.maximum(a, 0.0) + jnp.log1p(jnp.exp(-jnp.abs(a)))


def three(a, b):
    ah, al = split(a)
    bh, bl = split(b)
    return nt(ah, bh) + nt(al.astype(B16), bh) + nt(ah, bl.astype(B16))


def silu(a):
    return a * jax.nn.sigmoid(a)


def silu_grad(a):
    sig = jax.nn.sigmoid(a)
    return sig * (1.0 + a * (1.0 - sig))


def rms_scale(x):
    return lax.rsqrt(jnp.mean(x * x, axis=1, keepdims=True) + EPSILON)


def total(refs):
    out = refs[0][...].astype(F32)
    for extra in refs[1:]:
        out = out + extra[...].astype(F32)
    return out


def boundary(starts, base):
    found = False
    for k in range(starts.shape[0]):
        at = starts[k]
        found = found | ((at > 0) & (at > base - 3) & (at < base + Q + 3))
    return found


def prep_kernel(place, w_bt, conv, bias, gain, out):
    span, d = w_bt.shape
    quarter = span // 4
    side = lax.rem(lax.div(place[1], 2), 4)
    out[0:quarter, :] = w_bt[pl.ds(pl.multiple_of(side * quarter, quarter), quarter), :]
    rows = jnp.concatenate([conv[...], bias[...].reshape(1, span), jnp.zeros((11, span), F32)], axis=0)
    high, rest = split(rows)
    mid, rest = split(rest)
    wide = jnp.concatenate(
        [high.astype(F32), mid.astype(F32), rest, jnp.zeros((16, d - 3 * span), F32)], axis=1
    )
    row = jnp.concatenate(
        [gain[...].astype(F32).reshape(1, gain.shape[0]), jnp.zeros((1, d - gain.shape[0]), F32)],
        axis=1,
    )
    wide = jnp.where(iota((16, d), 0) == 5, row, wide)
    out[quarter:, :] = wide.astype(B16)


def stack_kernel(*refs):
    *ins, out = refs
    rows = out.shape[0] // len(ins)
    for k, ref in enumerate(ins):
        out[k * rows : (k + 1) * rows, :] = ref[0:rows, :]


def setup_kernel(heads, n, place, *refs):
    earlies, bts = refs[:n], refs[n : n + 4]
    (
        w_step, conv_i, bias_i, sbias, dlog, skips, ngain, w_bt, taps, gain, hp, w_s, vec,
    ) = refs[n + 4 :]
    inner = conv_i.shape[1]
    full = taps.shape[1]
    span = w_bt.shape[0] // n
    quarter = span // 4
    gain_own = gain.shape[1] // n
    w = place[0]
    side = lax.rem(lax.div(place[1], 2), 4)
    taps[0:4, 0:inner] = conv_i[...]
    taps[4:5, 0:inner] = bias_i[...].reshape(1, inner)
    taps[5:8, :] = jnp.zeros((3, full), F32)
    hp[...] = jnp.zeros_like(hp)
    for g in range(16):
        lanes = slice(8 * g, 8 * g + heads)
        hp[0:1, lanes] = sbias[...].reshape(1, heads)
        hp[1:2, lanes] = jnp.exp(dlog[...].reshape(1, heads))
    low = iota((1, 128), 1) < 64
    for p in range(heads // 2):
        one, two = (jnp.broadcast_to(skips[...].reshape(1, heads)[:, h : h + 1], (1, 128)) for h in (2 * p, 2 * p + 1))
        vec[0:1, p * 128 : (p + 1) * 128] = jnp.where(low, one, two)
    vec[1:2, :] = ngain[...].reshape(1, inner)
    copies = (iota((heads, 128), 0) == lax.rem(iota((heads, 128), 1), 8)).astype(F32)
    w_s[...] = nn(w_step[...], copies.astype(B16)).astype(B16)
    for k in range(n):
        v = lax.rem(w - k + n, n)
        for q in range(4):
            at = v * span + (side ^ q) * quarter
            w_bt[pl.ds(pl.multiple_of(at, quarter), quarter), :] = bts[q][
                k * quarter : (k + 1) * quarter, :
            ]
    for v in range(n):
        for k in range(n):

            @pl.when(lax.rem(w - v + n, n) == k)
            def _(v=v, k=k):
                low = inner + v * span
                small = earlies[k][quarter:, :].astype(F32)
                taps[0:5, low : low + span] = (
                    small[0:5, 0:span] + small[0:5, span : 2 * span]
                ) + small[0:5, 2 * span : 3 * span]
                gain[0:1, v * gain_own : (v + 1) * gain_own] = small[5:6, 0:gain_own]


def front_kernel(n, place, starts, *refs):
    xs, halos = refs[:n], refs[n : 2 * n]
    (
        w_bt, taps, gain, hp, w_s, w_in, tri, e_step, e_enter, e_end,
        normed_o, vals_o, bvals_o, pre_o, bpre_o, bc_o, pk_o, pk2_o, cumt_o, scaled_o, sent_o,
        dp_o, fin_o, hv_o, hn_o, tok_o, docrow_o,
        ext, state, prod, x,
    ) = refs[2 * n :]
    c = pl.program_id(0)
    inner = w_in.shape[1]
    full = ext.shape[1]
    w = place[0]

    def project(values):
        wide = values.astype(F32)
        return (wide * rms_scale(wide) * gain[0:1, :]).astype(B16)

    @pl.when(c == 0)
    def _():
        hn = project(total(halos))
        hn_o[...] = hn
        ext[0:8, 0:inner] = nn(hn, w_in[...])
        ext[0:8, inner:full] = nt(hn, w_bt[...])
        hv_o[...] = ext[0:8, :]
        state[...] = jnp.zeros_like(state)
        prod[...] = jnp.ones_like(prod)

    @pl.when(c > 0)
    def _():
        ext[0:8, :] = ext[Q : Q + 8, :]

    for k in range(n):

        @pl.when(lax.rem(w - c + n, n) == k)
        def _(k=k):
            x[...] = xs[k][...]

    def docs_at(positions):
        found = jnp.zeros(positions.shape, jnp.int32)
        for k in range(starts.shape[0]):
            found = found + (starts[k] <= positions).astype(jnp.int32)
        return found - 1

    base = (place[1] * pl.num_programs(0) + c) * Q
    here = base + iota((Q, 8), 0)
    lane = iota((Q, 8), 1)
    other = jnp.where(lane < 3, here - 3 + lane, jnp.where(lane == 3, base - 1, base + Q - 1))
    docs = docs_at(here)
    tok = jnp.where(lane == 5, docs, (docs_at(other) == docs).astype(jnp.int32)).astype(F32)
    tok_o[...] = tok
    docrow_o[...] = docs_at(base + iota((8, Q), 1)).astype(F32)

    normed = project(x[...])
    normed_o[...] = normed
    ext[8 : Q + 8, 0:inner] = nn(normed, w_in[...])
    ext[8 : Q + 8, inner:full] = nt(normed, w_bt[...])
    vals_o[...] = ext[8 : Q + 8, 0:inner].astype(B16)
    bvals_o[...] = ext[8 : Q + 8, inner:full].astype(B16)
    pre = taps[4:5, :] + taps[3:4, :] * ext[8 : Q + 8, :]
    for k in range(3):
        pre = pre + taps[k : k + 1, :] * ext[5 + k : 5 + k + Q, :]
    pre_o[...] = pre[:, :inner]
    bpre_o[...] = pre[:, inner:]

    @pl.when(boundary(starts, base))
    def _():
        again = taps[4:5, :] + taps[3:4, :] * ext[8 : Q + 8, :]
        for k in range(3):
            again = again + taps[k : k + 1, :] * ext[5 + k : 5 + k + Q, :] * tok_o[:, k : k + 1]
        pre_o[...] = again[:, :inner]
        bpre_o[...] = again[:, inner:]

    act = silu(pre_o[...])
    bc = silu(bpre_o[...]).astype(B16)
    bc_o[...] = bc
    sr = nn(normed, w_s[...]) + hp[0:1, :]
    step = softplus(sr)
    cums = exact_dot(tri[...], -hp[1:2, :] * step)
    enter = jnp.exp(cums) * tok[:, 3:4]
    end = jnp.exp(cums[Q - 1 : Q, :] - cums) * tok[:, 4:5]
    lane = iota((Q, 128), 1)
    group = lax.rem(lane, 64) // 8
    pk = jnp.where(
        group == STEP, step,
        jnp.where(
            group == ENTER, enter,
            jnp.where(group == END, end, jnp.where(group == SIG, jax.nn.sigmoid(sr), cums)),
        ),
    )
    pk_o[...] = pk
    high, low = split(pk)
    pk2 = jnp.where(lane < 64, high.astype(F32), low).astype(B16)
    pk2_o[...] = pk2
    cumt_o[...] = cums.T[0:8, :]
    scaled = nn(pk2, e_step[...]) * act
    scaled_o[...] = scaled.astype(B16)
    x16, x_lo = split(nn(pk2, e_end[...]) * scaled)
    x_lo = x_lo.astype(B16)
    carry = nn(pk2[Q - 16 :], e_enter[...])[15:16, :]
    sent_o[0] = state[...]
    dp_o[0] = prod[...]
    state[...] = carry * state[...] + tn(bc[:, :128], x16) + tn(bc[:, :128], x_lo)
    prod[...] = prod[...] * carry
    fin_o[0:128, :] = state[...].astype(B16)
    fin_o[128:144, :] = jnp.concatenate([prod[...], prod[...]], axis=0).astype(B16)


def intra_kernel(heads, normed, w_gate, pre, bc, pk, cumt, scaled, tok, docrow, vec, gate_o, y_o):
    gate_o[...] = nn(normed[...], w_gate[...])
    low = iota((HALF, 128), 1) < 64
    for block in range(2):
        rows = slice(block * HALF, (block + 1) * HALF)
        wide = (block + 1) * HALF
        scores = nt(bc[rows, 128:], bc[:wide, :128])
        mask = (block * HALF + iota((HALF, wide), 0) >= iota((HALF, wide), 1)) & (
            tok[rows, 5:6] == docrow[0:1, :wide]
        )
        for pair in range(heads // 2):
            cols = slice(pair * 128, (pair + 1) * 128)
            values = scaled[:wide, cols]
            outs = []
            for h in (2 * pair, 2 * pair + 1):
                diff = pk[rows, 8 * CUMS + h : 8 * CUMS + h + 1] - cumt[h : h + 1, :wide]
                mix = scores * jnp.where(mask, jnp.exp(diff), 0.0)
                outs.append(nn(mix.astype(B16), values))
            y_o[rows, cols] = jnp.where(low, *outs) + vec[0:1, cols] * silu(pre[rows, cols])


def fold_states(keep, others, out):
    state = jnp.zeros(out.shape, F32)
    for ref in reversed(others):
        state = ref[128:129, :].astype(F32) * state + ref[0:128, :].astype(F32)
    out[...] = keep[128:129, :] * state + keep[0:128, :]


def pair_kernel(reverse, place, own, other, keep_o, total_o):
    mine, theirs = own[...].astype(F32), other[...].astype(F32)
    earlier = lax.rem(place[1], 2) == (0 if reverse else 1)
    keep_o[0:128, :] = jnp.where(earlier, theirs[0:128, :], 0.0)
    keep_o[128:, :] = jnp.where(earlier, theirs[128:136, :], 1.0)
    total_o[0:128, :] = jnp.where(
        earlier,
        mine[128:129, :] * theirs[0:128, :] + mine[0:128, :],
        theirs[128:129, :] * mine[0:128, :] + theirs[0:128, :],
    ).astype(B16)
    total_o[128:, :] = (mine[128:, :] * theirs[128:, :]).astype(B16)


def join_kernel(n, m, place, y, gate, bc, pk2, sent, dp, keep, *refs):
    others = refs[:m]
    w_out, vec, e_enter, ssd_o, inter_o, gated_o, squares_o, s_in = refs[m : m + 8]
    mixes = refs[m + 8 :]
    c = pl.program_id(0)
    inner = y.shape[1]

    @pl.when(c == 0)
    def _():
        fold_states(keep, others, s_in)

    entering = sent[0] + dp[0, 0:1, :] * s_in[...]
    inter = nn(pk2[...], e_enter[...]) * nn(bc[:, 128:], entering.astype(B16))
    inter_o[...] = inter
    ssd = y[...] + inter
    ssd_o[...] = ssd
    gated = ssd * silu(gate[...])
    gated_o[...] = gated
    mixed = nn((gated * vec[1:2, :]).astype(B16), w_out[...]).astype(B16)
    for k in range(n):

        @pl.when(lax.rem(c - place[0] + n, n) == k)
        def _(k=k):
            mixes[k][...] = mixed

    first = (iota((inner, 128), 1) == 0).astype(F32).astype(B16)
    squares_o[...] = two_dot(gated * gated, first).T[0:8, :]


def dots_kernel(n, place, gated, squares, *refs):
    cots = refs[:n]
    w_out, vec, gn_o, stats_o, cot_o = refs[n:]
    c = pl.program_id(0)
    inner = gated.shape[1]
    for k in range(n):

        @pl.when(lax.rem(place[0] - c + n, n) == k)
        def _(k=k):
            cot_o[...] = cots[k][...]

    gn = nt(cot_o[...], w_out[...])
    gn_o[...] = gn
    second = (iota((inner, 128), 1) == 1).astype(F32).astype(B16)
    stats_o[...] = squares[...] + two_dot(vec[1:2, :] * gn * gated[...], second).T[0:8, :]


def gate_kernel(n, width_all, ssd, gate, gn, vec, pre, bc, pk2, e_enter, *refs):
    stats = refs[:n]
    norm_o, gate_o, gs_o, sums_o, sb_o, db_o, fin_o, rms_o, state, prod = refs[n:]
    i = pl.program_id(0)

    @pl.when(i == 0)
    def _():
        state[...] = jnp.zeros_like(state)
        prod[...] = jnp.ones_like(prod)
        sums_o[...] = jnp.zeros_like(sums_o)

    st = total(stats)
    rms = lax.rsqrt(st[0:1, :] / width_all + EPSILON)
    pull = rms * rms * rms * st[1:2, :] / width_all
    st = jnp.concatenate([rms, pull, jnp.zeros((126, Q), F32)], axis=0).T
    rms, pull = st[:, 0:1], st[:, 1:2]
    rms_o[...] = st[:, 0:8]
    g = gate[...]
    sig = jax.nn.sigmoid(g)
    s = ssd[...]
    act_g = g * sig
    gated = s * act_g
    scaled = gated * rms
    ngain = vec[1:2, :]
    norm_o[...] = (scaled * ngain).astype(B16)
    gn_ = gn[...]
    grad_gated = rms * (ngain * gn_) - gated * pull
    gs = grad_gated * act_g
    gs_o[...] = gs
    gate_o[...] = (grad_gated * s * (sig * (1.0 + g * (1.0 - sig)))).astype(B16)
    sums_o[0:1, :] += jnp.sum(gn_ * scaled, axis=0, keepdims=True)
    sums_o[1:2, :] += jnp.sum(gs * silu(pre[...]), axis=0, keepdims=True)
    enter = nn(pk2[...], e_enter[...])
    carry = enter[Q - 1 : Q, :]
    sb_o[0] = state[...]
    db_o[0] = prod[...]
    state[...] = carry * state[...] + tn(bc[:, 128:], (enter * gs).astype(B16)) + tn(bc[:, 128:], split(enter * gs)[1].astype(B16))
    prod[...] = prod[...] * carry
    fin_o[0:128, :] = state[...].astype(B16)
    fin_o[128:144, :] = jnp.concatenate([prod[...], prod[...]], axis=0).astype(B16)


def intra_back_kernel(
    heads, gs, bc, pk, pk2, cumt, scaled, tok, docrow, sent, dp, s_in, e_enter,
    gsc_o, rc_o, gbc_o, tot, plus, minus,
):
    low = iota((HALF, 128), 1) < 64
    g16 = gs[...].astype(B16)
    plus[...] = jnp.zeros_like(plus)
    for block in range(2):
        rows = slice(block * HALF, (block + 1) * HALF)
        wide = slice(block * HALF, Q)
        width = Q - block * HALF
        scores = nt(bc[rows, :128], bc[wide, 128:])
        mask = (iota((HALF, width), 0) <= iota((HALF, width), 1)) & (
            tok[rows, 5:6] == docrow[0:1, wide]
        )
        sums = jnp.zeros((HALF, width), F32)
        lane = iota((HALF, 128), 1)
        minus_acc = jnp.zeros((HALF, 128), F32)
        for pair in range(heads // 2):
            cols = slice(pair * 128, (pair + 1) * 128)
            mine = scaled[rows, cols]
            grads = g16[wide, cols]
            outs = []
            for h in (2 * pair, 2 * pair + 1):
                diff = cumt[h : h + 1, wide] - pk[rows, 8 * CUMS + h : 8 * CUMS + h + 1]
                decay = jnp.where(mask, jnp.exp(diff), 0.0)
                keep = low if h % 2 == 0 else ~low
                masked = jnp.where(keep, mine.astype(F32), 0.0).astype(B16)
                weighted = decay * nt(masked, grads)
                sums = sums + weighted
                ws = scores * weighted
                plus[h : h + 1, wide] += jnp.sum(ws, axis=0, keepdims=True)
                minus_acc = jnp.where(
                    lax.rem(lane, 8) == h, jnp.sum(ws, axis=1, keepdims=True), minus_acc
                )
                outs.append(nn((scores * decay).astype(B16), grads))
            gsc_o[rows, cols] = jnp.where(low, *outs)
        minus[rows, :] = minus_acc
        tot[rows, wide] = sums.astype(B16)
    tot[HALF:, :HALF] = jnp.zeros((HALF, HALF), B16)
    rc_o[...] = jnp.concatenate([plus[...]] * 16, axis=0).T - minus[...]
    entering = sent[0] + dp[0, 0:1, :] * s_in[...]
    t16 = tot[...]
    enter = nn(pk2[...], e_enter[...]) * gs[...]
    gbc_o[:, :128] = nn(t16, bc[:, 128:])
    gbc_o[:, 128:] = tn(t16, bc[:, :128]) + three(enter, entering)


def conv_back(i, count, masked, gp, tok, taps, vals, hv, ext, mext, shift, out, sums_o, rim_o):
    ch = gp.shape[1]

    @pl.when(i == 0)
    def _():
        ext[Q : Q + 8, :] = jnp.zeros((8, ch), F32)
        mext[Q : Q + 8, :] = jnp.zeros((8, 8), F32)
        sums_o[...] = jnp.zeros_like(sums_o)

    @pl.when(i > 0)
    def _():
        ext[Q : Q + 8, :] = ext[0:8, :]
        mext[Q : Q + 8, :] = mext[0:8, :]

    ext[0:Q, :] = gp
    mext[0:Q, :] = tok
    sums_o[4:5, :] += jnp.sum(gp, axis=0, keepdims=True)

    def sweep(use_mask):
        vals_ = vals.astype(F32)
        acc = jnp.zeros((Q, ch), F32)
        for k in range(4):
            z = ext[3 - k : 3 - k + Q, :]
            if k < 3 and use_mask:
                z = z * mext[3 - k : 3 - k + Q, k : k + 1]
            acc = acc + taps[k : k + 1, :] * z
            sums_o[k : k + 1, :] += jnp.sum(vals_ * z, axis=0, keepdims=True)
        out[...] = acc.astype(B16)

    @pl.when(masked)
    def _():
        sweep(True)

    @pl.when(jnp.logical_not(masked))
    def _():
        sweep(False)

    @pl.when(i == count - 1)
    def _():
        rim = jnp.zeros((8, ch), F32)
        shift[0:8, :] = jnp.zeros((8, ch), F32)
        for k in range(3):
            shift[8:16, :] = ext[0:8, :] * mext[0:8, k : k + 1]
            moved = shift[3 - k : 11 - k, :]
            rim = rim + taps[k : k + 1, :] * moved
            sums_o[k : k + 1, :] += jnp.sum(hv * moved, axis=0, keepdims=True)
        rim_o[...] = rim


def chunk_base(place, count, i):
    return (place[1] * count + (count - 1 - i)) * Q


def bcoef_back_kernel(
    count, n, m, place, starts, gbc, pre, vals, pk2, scaled, tok, sb, db, taps, hv, e_end,
    keep, *refs
):
    others, packs = refs[:m], refs[m : m + n]
    sums_o, s_after, ext, mext, shift, rim_o, out, pieces = refs[m + n :]
    i = pl.program_id(0)
    inner = scaled.shape[1]

    @pl.when(i == 0)
    def _():
        fold_states(keep, others, s_after)

    after_ = sb[0] + db[0, 0:1, :] * s_after[...]
    x16 = nn(pk2[...], e_end[...]) * scaled[...].astype(F32)
    gbm = gbc[:, :128] + three(x16, after_)
    gp = jnp.concatenate([gbm, gbc[:, 128:]], axis=1) * silu_grad(pre[...])
    conv_back(
        i, count, boundary(starts, chunk_base(place, count, i)), gp, tok[...],
        taps[:, inner:], vals[...], hv[:, inner:], ext, mext, shift, out, sums_o, rim_o,
    )
    span = 256 // n
    row = pl.multiple_of((count - 1 - i) * HALF, HALF)
    for v in range(n):
        piece = out[:, v * span : (v + 1) * span]
        pieces[v] = jnp.concatenate([piece[:HALF], piece[HALF:]], axis=1)
    for k in range(n):
        packs[k][pl.ds(row, HALF), :] = pieces[lax.rem(place[0] + k, n)]

    @pl.when(i == count - 1)
    def _():
        for v in range(n):
            edge = rim_o[:, v * span : (v + 1) * span]
            pieces[v, 0:16, 0:span] = jnp.concatenate([edge, edge], axis=0).astype(B16)
        for k in range(n):
            packs[k][count * HALF :, :] = pieces[lax.rem(place[0] + k, n), 0:16, :]


def inner_back_kernel(
    count, place, starts, gs, gsc, rc, inter, pre, vals, bc, pk, pk2, scaled, tok, sent,
    dp, s_in, sb, db, s_after, taps, hp, hv, vec, tri, e_step, e_enter, e_end, hmap,
    gv_o, step_o, rim_o, sums_o, small_o, ext, mext, shift,
):
    i = pl.program_id(0)
    entering = sent[0] + dp[0, 0:1, :] * s_in[...]
    after_ = sb[0] + db[0, 0:1, :] * s_after[...]
    p = pre[...]
    sig_p = jax.nn.sigmoid(p)
    act = p * sig_p
    weights = pk2[...]
    end_state = nn(weights, e_end[...]) * nn(bc[:, :128], after_.astype(B16))
    gsc_ = gsc[...] + end_state
    grad = gs[...]
    end_terms = scaled[...].astype(F32) * end_state
    carry = nn(weights[Q - 16 :], e_enter[...])[15:16, :]
    closing = jnp.sum(end_terms, axis=0, keepdims=True) + carry * jnp.sum(
        after_ * entering, axis=0, keepdims=True
    )
    closing = two_dot(jnp.broadcast_to(closing, (8, closing.shape[1])), hmap[...])[0:1, :]
    grad_cums = rc[...] + two_dot(grad * inter[...] - end_terms, hmap[...])
    grad_cums = grad_cums + jnp.where(iota((Q, 128), 0) == Q - 1, closing, 0.0)
    high, low = split(grad_cums)
    grad_decay = tn(tri[...], high) + tn(tri[...], low.astype(B16))
    drive = hp[1:2, :] * grad_decay
    raw = (nn((gsc_ * act).astype(B16), hmap[...]) - drive) * pk[...]
    lane = iota((Q, 128), 1)
    step_o[...] = jnp.where(lane // 8 == SIG, raw, 0.0).astype(B16)

    @pl.when(i == 0)
    def _():
        small_o[...] = jnp.zeros_like(small_o)

    small_o[0:1, :] += jnp.sum(raw, axis=0, keepdims=True)
    small_o[1:2, :] -= jnp.sum(drive * pk[...], axis=0, keepdims=True)
    gp = (nn(weights, e_step[...]) * gsc_ + vec[0:1, :] * grad) * (
        sig_p * (1.0 + p * (1.0 - sig_p))
    )
    conv_back(
        i, count, boundary(starts, chunk_base(place, count, i)), gp, tok[...], taps[...],
        vals[...], hv[...], ext, mext, shift, gv_o, sums_o, rim_o,
    )


def gate_grads_kernel(place, gnorm, normed, gate16, cot, keep_o, send_o):
    r = pl.program_id(0)
    core = lax.rem(place[1], 2)
    inner = gate16.shape[1]
    left = tn(normed[...], gate16[...]).astype(B16)
    right = tn(gnorm[...], cot[...]).astype(B16)

    @pl.when(r == core)
    def _():
        keep_o[:, 0:inner] = left
        keep_o[:, inner:] = right

    @pl.when(r != core)
    def _():
        send_o[:, 0:inner] = left
        send_o[:, inner:] = right


def inner_grads_kernel(
    place, gv, gv_all, rim, hn, gate16, step16, normed, w_in, w_gate, w_s, part_o, keep_o, send_o
):
    r = pl.program_id(0)
    core = lax.rem(place[1], 2)
    part_o[...] = nt(gv[...], w_in[...]) + nt(gate16[...], w_gate[...]) + nt(step16[...], w_s[...])
    grads = (tn(normed[...], gv_all[...]) + tn(hn[...], rim[...].astype(B16))).astype(B16)

    @pl.when(r == core)
    def _():
        keep_o[...] = grads

    @pl.when(r != core)
    def _():
        send_o[...] = grads


def bcoef_grads_kernel(count, n, pack_view, tail_view, place, *refs):
    packs = [pack_view(ref, pl.program_id(0), (place,)) for ref in refs[:n]]
    tails = [tail_view(ref, 0, (place,)) for ref in refs[:n]]
    (
        rim_i, hn, part, normed, w_bt, w_in, step16, gain, csum_b, csum_i, ssum, nsums,
    ) = refs[n : n + 12]
    parts = refs[n + 12 : 2 * n + 12]
    keep_o, send_o, small_o, local_o, acc, gsum = refs[2 * n + 12 :]
    i = pl.program_id(0)
    span, d = w_bt.shape
    inner = w_in.shape[1]

    @pl.when(i == 0)
    def _():
        rim16 = total(tails)[0:8, :span].astype(B16)
        edge = nn(rim16, w_bt[...]) + nt(rim_i[...].astype(B16), w_in[...])
        small_o[3:8, :] = edge[3:8, :]
        gsum[...] = jnp.sum(edge * hn[...].astype(F32), axis=0, keepdims=True)
        acc[...] = tn(jnp.concatenate([rim16, jnp.zeros((8, span), B16)], axis=1), hn[...])

    packed = total(packs)
    v16 = jnp.concatenate([packed[:, :span], packed[:, span:]], axis=0).astype(B16)
    sums = part[...] + nn(v16, w_bt[...])
    for k in range(n):

        @pl.when(i == k)
        def _(k=k):
            parts[k][...] = sums.astype(B16)

    x16 = normed[...]
    gsum[...] += jnp.sum(sums * x16.astype(F32), axis=0, keepdims=True)
    acc[...] += tn(jnp.concatenate([v16, step16[:, :span]], axis=1), x16)

    @pl.when(i == count - 1)
    def _():
        turned = acc[...].T.astype(B16)
        core = lax.rem(place[1], 2)
        half = d // 2

        @pl.when(core == 0)
        def _():
            keep_o[...] = turned[:half]
            send_o[...] = turned[half:]

        @pl.when(core == 1)
        def _():
            keep_o[...] = turned[half:]
            send_o[...] = turned[:half]

        small_o[0:1, :] = gsum[...] / gain[0:1, :]
        for k in range(3):
            small_o[1:2, k * 256 : (k + 1) * 256] = csum_b[k : k + 1, :]
            local_o[3 + k : 4 + k, 0:inner] = csum_i[2 * k : 2 * k + 1, :]
        for k in range(2):
            small_o[2:3, k * 256 : (k + 1) * 256] = csum_b[3 + k : 4 + k, :]
            local_o[3 + k : 4 + k, inner:] = csum_i[2 * k + 1 : 2 * k + 2, :]
        local_o[5:6, inner:] = nsums[1:2, :]
        local_o[6:7, 0:inner] = nsums[0:1, :]
        local_o[6:7, inner : inner + 128] = ssum[0:1, :]
        local_o[6:7, inner + 128 : inner + 256] = ssum[1:2, :]


def small_kernel(local, *refs):
    *ins, small_o, edge_o = refs
    both = total(ins)
    small_o[0:3, :] = both[0:3, :]
    small_o[3:8, :] = local[3:8, :]
    edge_o[0:3, :] = jnp.zeros((3, both.shape[1]), F32)
    edge_o[3:8, :] = both[3:8, :]


def last_kernel(n, place, x, cot, gain, edge, rms, *refs):
    parts, mixes, (grad_o, block_o) = refs[:n], refs[n : 2 * n], refs[2 * n :]
    sums = total(parts)
    rows = sums.shape[0]
    sums = jnp.concatenate([sums[: rows - 8], sums[rows - 8 :] + edge[...]], axis=0)
    wide = x[...].astype(F32)
    own = rms[pl.ds(pl.multiple_of(place[0] * rows, rows), rows), 0:1]
    block_o[...] = (wide + own * total(mixes)).astype(B16)
    scale = rms_scale(wide)
    scaled = gain[0:1, :] * sums
    dot = jnp.sum(scaled * wide, axis=1, keepdims=True)
    width = wide.shape[1]
    grad_o[...] = (
        cot[...].astype(F32) + scale * scaled - wide * (scale * scale * scale * dot / width)
    )


def add_kernel(a, b, out):
    out[...] = a[...] + b[...]


def ends_kernel(n, heads, place, *refs):
    smalls = refs[:n]
    gain_o, taps_i_o, taps_b_o, bias_i_o, bias_b_o, sbias_o, dlog_o, skip_o, ngain_o = refs[n:]
    sums = total(smalls)
    inner, span = ngain_o.shape[0], bias_b_o.shape[0]
    count, own = 256 // span, gain_o.shape[0]
    for v in range(count):

        @pl.when(place[0] == v)
        def _(v=v):
            gain_o[...] = sums[0:1, v * own : (v + 1) * own].reshape(own)
            low = v * span
            for k in range(4):
                row, at = (1, 256 * k) if k < 3 else (2, 0)
                taps_b_o[k : k + 1, :] = sums[row : row + 1, at + low : at + low + span]
            bias_b_o[...] = sums[2:3, 256 + low : 256 + low + span].reshape(span)

    taps_i_o[0:1, :] = sums[3:4, :inner]
    taps_i_o[1:2, :] = sums[3:4, inner:]
    taps_i_o[2:3, :] = sums[4:5, :inner]
    taps_i_o[3:4, :] = sums[4:5, inner:]
    bias_i_o[...] = sums[5:6, :inner].reshape(inner)
    ngain_o[...] = sums[6:7, :inner].reshape(inner)
    raw_at, decay_at = inner + 8 * SIG, inner + 128 + 8 * STEP
    sbias_o[...] = sums[6:7, raw_at : raw_at + heads].reshape(heads)
    dlog_o[...] = sums[6:7, decay_at : decay_at + heads].reshape(heads)
    hit = iota((8, inner), 1) // (inner // heads) == iota((8, inner), 0)
    rows = jnp.where(hit, sums[5:6, inner:], 0.0)
    column = jnp.sum(rows, axis=1, keepdims=True)
    skip_o[...] = jnp.broadcast_to(column, (8, 128)).T[0:1, 0:heads].reshape(heads)


def halves_kernel(n, place, *refs):
    ins, outs = refs[:6], refs[6:]
    rows = outs[0].shape[0]
    for k in range(n):
        piece = pl.ds(pl.multiple_of(lax.rem(lax.div(place[1], 2) + k, n) * rows, rows), rows)
        at = 0
        for j in range(3):
            mine, theirs = ins[2 * j], ins[2 * j + 1]
            cols = slice(at, at + mine.shape[1])
            at += mine.shape[1]
            outs[k][:, cols] = (
                mine[piece, :].astype(F32) + theirs[piece, :].astype(F32)
            ).astype(B16)


def pieces_kernel(*refs):
    refs[-1][...] = total(refs[:-1]).astype(B16)


def unpack_kernel(n, place, *refs):
    pieces = refs[: 2 * n]
    gate_o, inner_o, bcoef_o, step_o, out_o, late = refs[2 * n :]
    rows = pieces[0].shape[0]
    inner = gate_o.shape[1]
    span = bcoef_o.shape[0]
    heads = step_o.shape[0]
    for side in range(2):
        for k in range(n):
            piece = pieces[side * n + k][...].astype(F32)
            whole_half = lax.rem(lax.div(place[1], 2) - k + n, n)
            core = lax.rem(place[1] + side, 2)
            at = pl.multiple_of(core * (n * rows) + whole_half * rows, rows)
            dst = pl.ds(at, rows)
            gate_o[dst, :] = piece[:, 0:inner]
            inner_o[dst, :] = piece[:, 2 * inner : 3 * inner]
            late[dst, :] = piece[:, 3 * inner :]
            low = pl.ds(pl.multiple_of(whole_half * rows, rows), rows)

            @pl.when(core == 0)
            def _():
                out_o[low, 0:inner] = piece[:, inner : 2 * inner]

            @pl.when(core == 1)
            def _():
                out_o[low, inner:] = piece[:, inner : 2 * inner]

    turned = late[...].T
    bcoef_o[...] = turned[:span, :]
    step_o[...] = turned[span + 8 * SIG : span + 8 * SIG + heads, :]


def shape(dims, dtype=F32):
    return jax.ShapeDtypeStruct(dims, dtype)


def call(
    kernel, grid, ins, in_specs, outs, out_specs, scratch=(), scalars=(), flops=0,
    fetch=(),
):
    size = sum(a.size * a.dtype.itemsize for a in ins) + sum(
        o.size * o.dtype.itemsize for o in outs
    )
    views = list(in_specs) + list(out_specs)
    ins = [
        pltpu.with_memory_space_constraint(a, pltpu.HBM) if k in fetch else a
        for k, a in enumerate(ins)
    ]

    landing = [pltpu.VMEM(ins[k].shape, ins[k].dtype) for k in fetch]
    landing += [pltpu.SemaphoreType.DMA((len(fetch),))] if fetch else []

    def body(*refs):
        first = len(scalars)
        step = pl.program_id(0) if grid else 0
        if fetch:
            refs, local, sems = list(refs[: -len(landing)]), refs[-len(landing) : -1], refs[-1]

            sources = [refs[first + k] for k in fetch]

            def copies():
                return [
                    pltpu.make_async_copy(source, local[j], sems.at[j])
                    for j, source in enumerate(sources)
                ]

            def bring():
                for copy in copies():
                    copy.start()
                for copy in copies():
                    copy.wait()

            if grid:
                pl.when(step == 0)(bring)
            else:
                bring()
            for j, k in enumerate(fetch):
                refs[first + k] = local[j]
        seen = [
            view(ref, step, refs[:first]) if view else ref
            for view, ref in zip(views, refs[first:])
        ]
        kernel(*refs[:first], *seen, *refs[first + len(views) :])

    return pl.pallas_call(
        body,
        out_shape=outs,
        grid_spec=pltpu.PrefetchScalarGridSpec(
            num_scalar_prefetch=len(scalars),
            grid=grid,
            in_specs=[HBM if k in fetch else VMEM for k in range(len(ins))],
            out_specs=[VMEM] * len(outs),
            scratch_shapes=list(scratch) + landing,
        ),
        compiler_params=pltpu.CompilerParams(
            dimension_semantics=("arbitrary",) * len(grid) or None,
            vmem_limit_bytes=LIMIT,
        ),
        cost_estimate=pl.CostEstimate(
            flops=int(flops), bytes_accessed=size, transcendentals=0
        ),
    )(*scalars, *ins)


def ring(value, axis, distance):
    count = lax.axis_size(axis)
    return lax.ppermute(value, axis, [(i, (i + distance) % count) for i in range(count)])


def swap(value, axis, bit):
    count = lax.axis_size(axis)
    return lax.ppermute(value, axis, [(i, i ^ (1 << bit)) for i in range(count)])


def spread(value, axis):
    count = lax.axis_size(axis)
    return [value] + [ring(value, axis, k) for k in range(1, count)]


def reduce_parts(parts, axis):
    return [ring(p, axis, k) if k else p for k, p in enumerate(parts)]


def states(fin, place, reverse):
    rows, inner = fin.shape
    count = lax.axis_size("seq")
    other = swap(fin, "seq", 0)
    keep, both = call(
        functools.partial(pair_kernel, reverse), (), [fin, other], [None] * 2,
        [shape((rows - 8, inner)), shape((rows, inner), B16)], [None] * 2,
        scalars=(place,),
    )
    got = []
    for k in range(1, count // 2):
        if reverse:
            pairs = [(i + 2 * k, i) for i in range(count - 2 * k)]
        else:
            pairs = [(i, i + 2 * k) for i in range(count - 2 * k)]
        got.append(lax.ppermute(both, "seq", pairs))
    return keep, got


def per_device(
    block_in,
    in_gain,
    proj_gate,
    proj_inner,
    proj_bcoef,
    proj_step,
    conv_inner,
    conv_inner_bias,
    conv_bcoef,
    conv_bcoef_bias,
    step_bias,
    decay_log,
    skip_gain,
    norm_gain,
    proj_out,
    out_grad,
    doc_starts,
):
    n_wt, n_seq = lax.axis_size("wt"), lax.axis_size("seq")
    w, seq = lax.axis_index("wt"), lax.axis_index("seq")
    rows_own, d = block_in.shape
    length = rows_own * n_wt
    inner = proj_inner.shape[1]
    heads = step_bias.shape[0]
    span = proj_bcoef.shape[1]
    full = inner + span * n_wt
    width_all = inner * n_wt
    count = length // Q
    pairs = n_seq // 2
    place = jnp.stack([w, seq]).astype(jnp.int32)
    scalars = (place, doc_starts)

    w_bt_own = proj_bcoef.T
    quarter = span // 4
    (early,) = call(
        prep_kernel, (), [w_bt_own, conv_bcoef, conv_bcoef_bias, in_gain], [None] * 4,
        [shape((quarter + 16, d), B16)], [None], scalars=(place,),
        fetch=tuple(range(4)),
    )
    earlies = spread(early, "wt")
    rows = spread(block_in, "wt")
    (bts,) = call(
        stack_kernel, (), earlies, [None] * n_wt, [shape((quarter * n_wt, d), B16)], [None],
    )
    bts_x = swap(bts, "seq", 1)
    bts_y = [swap(b, "seq", 2) for b in (bts, bts_x)]
    tail = block_in[rows_own - 8 :]
    halos = []
    for v in range(n_wt):
        halos.append(
            lax.ppermute(
                tail, ("seq", "wt"),
                [((s - 1) * n_wt + n_wt - 1, s * n_wt + v) for s in range(1, n_seq)],
            )
        )
    cots = spread(out_grad, "wt")

    lanes, chans = np.arange(128), np.arange(inner) // (inner // heads)

    def one_hot(group):
        hit = ((lanes % 64) // 8 == group)[:, None] & ((lanes % 8)[:, None] == chans[None, :])
        return jnp.asarray(hit.astype(np.float32), B16)

    e_step, e_enter, e_end = one_hot(STEP), one_hot(ENTER), one_hot(END)
    hmap = jnp.asarray((chans[:, None] == (lanes % 8)[None, :]).astype(np.float32), B16)
    tri = jnp.asarray((np.arange(Q)[:, None] >= np.arange(Q)[None, :]).astype(np.float32), B16)

    grid = (count,)

    def at_rows(ref, index, rows=Q):
        return ref.at[pl.ds(pl.multiple_of(index * rows, rows), rows), :]

    def by_rows(reverse=False):
        if reverse:
            return lambda ref, i, p: at_rows(ref, count - 1 - i)
        return lambda ref, i, p: at_rows(ref, i)

    def by_turn():
        return lambda ref, i, p: at_rows(ref, lax.rem(i + p[0][0], count))

    def whole(*dims):
        return None

    def by_chunk(*dims, reverse=False):
        if reverse:
            return lambda ref, i, p: ref.at[pl.ds(count - 1 - i, 1)]
        return lambda ref, i, p: ref.at[pl.ds(i, 1)]

    def by_lanes(width, reverse=False):
        def view(ref, i, p):
            index = count - 1 - i if reverse else i
            return ref.at[:, pl.ds(pl.multiple_of(index * width, width), width)]

        return view

    def lead(ref, i, p):
        return ref.at[:, :inner]

    by_cols = by_lanes(Q)
    by_cols_back = by_lanes(Q, True)
    fin_spec, state_spec = whole(144, inner), whole(128, inner)
    e_spec = whole(128, inner)
    states_out = [shape((count, 128, inner)), shape((count, 8, inner)), shape((144, inner), B16)]
    w_bt, taps, gain, hp, w_s, vec = call(
        functools.partial(setup_kernel, heads, n_wt), (),
        [*earlies, bts, bts_x, *bts_y, proj_step, conv_inner, conv_inner_bias, step_bias,
         decay_log, skip_gain, norm_gain],
        [None] * (n_wt + 11),
        [shape((span * n_wt, d), B16), shape((8, full)), shape((8, d)), shape((8, 128)),
         shape((d, 128), B16), shape((8, inner))],
        [None] * 6, scalars=(place,), fetch=tuple(range(n_wt + 4, n_wt + 11)),
    )
    (normed, vals, bvals, pre, bpre, bc, pk, pk2, cumt, scaled, sent, dp, fin, hv, hn, tok,
     docrow) = call(
        functools.partial(front_kernel, n_wt), grid,
        [*rows, *halos, w_bt, taps, gain, hp, w_s, proj_inner, tri, e_step, e_enter, e_end],
        [None] * (2 * n_wt + 10),
        [shape((length, d), B16), shape((length, inner), B16), shape((length, 256), B16),
         shape((length, inner)), shape((length, 256)),
         shape((length, 256), B16), shape((length, 128)), shape((length, 128), B16),
         shape((8, length)), shape((length, inner), B16), *states_out,
         shape((8, full)), shape((8, d), B16), shape((length, 8)), shape((8, length))],
        [by_rows(), by_rows(), by_rows(), by_rows(), by_rows(), by_rows(),
         by_rows(), by_rows(),
         by_cols, by_rows(), by_chunk(128, inner), by_chunk(8, inner), fin_spec,
         whole(8, full), whole(8, d), by_rows(), by_cols],
        scratch=[pltpu.VMEM((Q + 8, full), F32), pltpu.VMEM((128, inner), F32),
                 pltpu.VMEM((8, inner), F32), pltpu.VMEM((Q, d), B16)],
        scalars=scalars, flops=2e9,
        fetch=(0, *range(2 * n_wt + 5, 2 * n_wt + 10)),
    )
    keep, got = states(fin, place, False)
    gate, y = call(
        functools.partial(intra_kernel, heads), grid,
        [normed, proj_gate, pre, bc, pk, cumt, scaled, tok, docrow, vec],
        [by_rows(), whole(d, inner), by_rows(), by_rows(), by_rows(), by_cols,
         by_rows(), by_rows(), by_cols, whole(1, inner)],
        [shape((length, inner)), shape((length, inner))],
        [by_rows(), by_rows()], flops=2e9,
    )
    got_spec = [whole(136, inner)] + [fin_spec] * (pairs - 1)
    ssd, inter, gated, squares, s_in, *mixes = call(
        functools.partial(join_kernel, n_wt, pairs - 1), grid,
        [y, gate, bc, pk2, sent, dp, keep, *got, proj_out, vec, e_enter],
        [by_rows(), by_rows(), by_rows(), by_rows(),
         by_chunk(128, inner), by_chunk(8, inner), *got_spec]
        + [whole(inner, d), whole(1, inner), e_spec],
        [shape((length, inner))] * 3 + [shape((8, length)), shape((128, inner))]
        + [shape((Q, d), B16)] * n_wt,
        [by_rows()] * 3 + [by_cols, state_spec] + [None] * n_wt,
        scalars=(place,), flops=2e9,
    )
    gn, stats, cot = call(
        functools.partial(dots_kernel, n_wt), grid,
        [gated, squares, *cots, proj_out, vec],
        [by_rows(), by_cols] + [None] * (n_wt + 2),
        [shape((length, inner)), shape((8, length)), shape((length, d), B16)],
        [by_rows(), by_cols, by_rows()],
        scalars=(place,), flops=1e9,
    )
    gnorm, gate16, gs, nsums, sb, db, back_fin, rms = call(
        functools.partial(gate_kernel, n_wt, width_all), grid,
        [ssd, gate, gn, vec, pre, bc, pk2, e_enter, *spread(stats, "wt")],
        [by_rows(True)] * 3
        + [whole(1, inner), by_rows(True), by_rows(True), by_rows(True), e_spec]
        + [by_cols_back] * n_wt,
        [shape((length, inner), B16), shape((length, inner), B16), shape((length, inner)),
         shape((8, inner)), *states_out, shape((length, 8))],
        [by_rows(True)] * 3
        + [whole(8, inner), by_chunk(128, inner, reverse=True), by_chunk(8, inner, reverse=True),
           fin_spec, by_rows(True)],
        scratch=[pltpu.VMEM((128, inner), F32), pltpu.VMEM((8, inner), F32)],
        flops=1e9,
    )
    keep_b, got_b = states(back_fin, place, True)
    gsc, rc, gbc = call(
        functools.partial(intra_back_kernel, heads), grid,
        [gs, bc, pk, pk2, cumt, scaled, tok, docrow, sent, dp, s_in, e_enter],
        [by_rows(), by_rows(), by_rows(), by_rows(), by_cols, by_rows(),
         by_rows(), by_cols, by_chunk(128, inner), by_chunk(8, inner), state_spec, e_spec],
        [shape((length, inner)), shape((length, 128)), shape((length, 256))],
        [by_rows(), by_rows(), by_rows()],
        scratch=[pltpu.VMEM((Q, Q), B16), pltpu.VMEM((8, Q), F32), pltpu.VMEM((Q, 128), F32)],
        flops=4e9,
    )

    half = d // 2
    d_half = by_lanes(half)
    keep_a, send_a = call(
        gate_grads_kernel, (2,), [gnorm, normed, gate16, cot],
        [whole(length, inner), d_half, whole(length, inner), d_half],
        [shape((half, 2 * inner), B16)] * 2, [whole(half, 2 * inner)] * 2,
        scalars=(place,), flops=2e9,
    )
    got_a = swap(send_a, "seq", 0)
    mixes = reduce_parts(mixes, "wt")

    rows_pack = length // 2 + 16
    *packs, csum_b, s_after = call(
        functools.partial(bcoef_back_kernel, count, n_wt, pairs - 1), grid,
        [gbc, bpre, bvals, pk2, scaled, tok, sb, db, taps, hv, e_end,
         keep_b, *got_b],
        [by_rows(True), by_rows(True), by_rows(True), by_rows(True),
         by_rows(True), by_rows(True), by_chunk(128, inner, reverse=True),
         by_chunk(8, inner, reverse=True), whole(8, full), whole(8, full), e_spec, *got_spec],
        [shape((rows_pack, 128), B16)] * n_wt + [shape((8, 256)), shape((128, inner))],
        [whole(rows_pack, 128)] * n_wt + [whole(8, 256), state_spec],
        scratch=[pltpu.VMEM((Q + 8, 256), F32), pltpu.VMEM((Q + 8, 8), F32),
                 pltpu.VMEM((16, 256), F32), pltpu.VMEM((8, 256), F32),
                 pltpu.VMEM((Q, 256), B16), pltpu.VMEM((n_wt, HALF, 128), B16)],
        scalars=scalars, flops=1e9,
    )
    packs = reduce_parts(packs, "wt")
    gv, step16, rim_i, csum_i, ssum = call(
        functools.partial(inner_back_kernel, count), grid,
        [gs, gsc, rc, inter, pre, vals, bc, pk, pk2, scaled, tok, sent, dp, s_in, sb, db,
         s_after, taps, hp, hv, vec, tri, e_step, e_enter, e_end, hmap],
        [by_rows(True), by_rows(True), by_rows(True), by_rows(True),
         by_rows(True), by_rows(True), by_rows(True), by_rows(True),
         by_rows(True), by_rows(True), by_rows(True),
         by_chunk(128, inner, reverse=True), by_chunk(8, inner, reverse=True), state_spec,
         by_chunk(128, inner, reverse=True), by_chunk(8, inner, reverse=True), state_spec,
         lead, whole(8, 128), lead, whole(1, inner), whole(Q, Q), e_spec,
         e_spec, e_spec, whole(inner, 128)],
        [shape((length, inner), B16), shape((length, 128), B16), shape((8, inner)),
         shape((8, inner)), shape((8, 128))],
        [by_rows(True), by_rows(True), whole(8, inner), whole(8, inner),
         whole(8, 128)],
        scratch=[pltpu.VMEM((Q + 8, inner), F32), pltpu.VMEM((Q + 8, 8), F32),
                 pltpu.VMEM((16, inner), F32)],
        scalars=scalars, flops=1e9,
    )
    t_half = lambda: lambda ref, r, p: at_rows(ref, r, length // 2)
    part, keep_i, send_i = call(
        inner_grads_kernel, (2,),
        [gv, gv, rim_i, hn, gate16, step16, normed, proj_inner, proj_gate, w_s],
        [t_half(), whole(length, inner), whole(8, inner),
         d_half, t_half(), t_half(), d_half,
         whole(d, inner), whole(d, inner), whole(d, 128)],
        [shape((length, d)), shape((half, inner), B16), shape((half, inner), B16)],
        [t_half(), whole(half, inner), whole(half, inner)],
        scalars=(place,), flops=2e9,
    )
    got_i = swap(send_i, "seq", 0)
    pack_spec = lambda ref, i, p: at_rows(ref, lax.rem(i + p[0][0], count), HALF)
    tail_spec = lambda ref, i, p: ref.at[length // 2 : length // 2 + 16, :]
    *parts, keep_p, send_p, small, local = call(
        functools.partial(bcoef_grads_kernel, count, n_wt, pack_spec, tail_spec), grid,
        [*packs, rim_i, hn, part, normed, w_bt_own, proj_inner, step16, gain, csum_b,
         csum_i, ssum, nsums],
        [None] * n_wt
        + [whole(8, inner), whole(8, d), by_turn(), by_turn(), whole(span, d),
           whole(d, inner), by_turn(), whole(8, d), whole(8, 256), whole(8, inner),
           whole(8, 128), whole(8, inner)],
        [shape((Q, d), B16)] * n_wt
        + [shape((half, 2 * span), B16)] * 2 + [shape((8, d))] * 2,
        [whole(Q, d)] * n_wt + [whole(half, 2 * span)] * 2 + [whole(8, d)] * 2,
        scratch=[pltpu.VMEM((2 * span, d), F32), pltpu.VMEM((1, d), F32)],
        scalars=(place,), flops=1e9,
    )
    parts = reduce_parts(parts, "wt")
    got_p = swap(send_p, "seq", 0)
    small, edge = call(
        small_kernel, (), [local, *spread(small, "wt")], [None] * (n_wt + 1),
        [shape((8, d))] * 2, [None] * 2,
    )
    edge = lax.ppermute(
        edge, ("seq", "wt"),
        [(s * n_wt + n_wt - 1, (s - 1) * n_wt + n_wt - 1) for s in range(1, n_seq)],
    )
    input_grad, block_out = call(
        functools.partial(last_kernel, n_wt), (),
        [block_in, out_grad, gain, edge, rms, *parts, *mixes], [None] * (5 + 2 * n_wt),
        [shape((rows_own, d)), shape((rows_own, d), B16)], [None] * 2, scalars=(place,),
    )

    def pair_ring(value, k):
        return lax.ppermute(
            value, "seq", [(i, (i + 2 * k) % n_seq) for i in range(n_seq)]
        )

    wide = 3 * inner + 2 * span
    piece_rows = half // pairs
    pieces = call(
        functools.partial(halves_kernel, pairs), (),
        [keep_a, got_a, keep_i, got_i, keep_p, got_p], [None] * 6,
        [shape((piece_rows, wide), B16)] * pairs, [None] * pairs,
        scalars=(place,),
    )
    pieces = [pair_ring(p, k) if k else p for k, p in enumerate(pieces)]
    (piece,) = call(
        pieces_kernel, (), pieces, [None] * pairs, [shape((piece_rows, wide), B16)], [None],
    )
    own = [pair_ring(piece, k) if k else piece for k in range(pairs)]
    theirs = [swap(p, "seq", 0) for p in own]
    g_gate, g_inner, g_bcoef, g_step, g_out = call(
        functools.partial(unpack_kernel, pairs), (1,), [*own, *theirs],
        [whole(piece_rows, wide)] * (2 * pairs),
        [shape((d, inner)), shape((d, inner)), shape((span, d)), shape((heads, d)),
         shape((inner, d))],
        [whole(d, inner), whole(d, inner), whole(span, d), whole(heads, d), whole(inner, d)],
        scratch=[pltpu.VMEM((d, 2 * span), F32)], scalars=(place,),
    )
    (small,) = call(
        add_kernel, (), [small, swap(small, "seq", 0)], [None] * 2,
        [shape((8, d))], [None],
    )
    smalls = [pair_ring(small, k) if k else small for k in range(pairs)]
    (g_gain, g_ci, g_cb, g_cib, g_cbb, g_sbias, g_dlog, g_skip, g_norm) = call(
        functools.partial(ends_kernel, pairs, heads), (), smalls, [None] * pairs,
        [shape((in_gain.shape[0],)), shape((4, inner)), shape((4, span)), shape((inner,)),
         shape((span,)), shape((heads,)), shape((heads,)), shape((heads,)), shape((inner,))],
        [None] * 9, scalars=(place,),
    )
    return (
        block_out,
        input_grad,
        g_gain,
        g_gate,
        g_inner,
        g_bcoef.T,
        g_step.T,
        g_ci,
        g_cb,
        g_cib,
        g_cbb,
        g_sbias,
        g_dlog,
        g_skip,
        g_norm,
        g_out,
    )


def solution(mesh):
    tokens = P(("seq", "wt"), None)
    cols, vec = P(None, "wt"), P("wt")
    return jax.shard_map(
        per_device,
        mesh=mesh,
        in_specs=(
            tokens, vec, cols, cols, cols, cols, cols, vec, cols, vec, vec, vec, vec, vec,
            P("wt", None), tokens, P(),
        ),
        out_specs=(
            tokens, tokens, vec, cols, cols, cols, cols, cols, cols, vec, vec, vec, vec, vec,
            vec, P("wt", None),
        ),
        check_vma=False,
    )
```

```python
import functools

import jax
import jax.numpy as jnp
import numpy as np
from jax import lax
from jax.experimental import pallas as pl
from jax.experimental.pallas import tpu as pltpu
from jax.sharding import PartitionSpec as P

VMEM = pl.BlockSpec(memory_space=pltpu.VMEM)
HBM = pl.BlockSpec(memory_space=pltpu.HBM)
LIMIT = 16 << 20
Q = 256
HALF = Q // 2
STEP, ENTER, END, CUMS, SIG = 0, 1, 2, 4, 5
EPSILON = 1e-05
F32 = jnp.float32
B16 = jnp.bfloat16


def nn(a, b):
    return lax.dot_general(a, b, (((1,), (0,)), ((), ())), preferred_element_type=F32)


def nt(a, b):
    return lax.dot_general(a, b, (((1,), (1,)), ((), ())), preferred_element_type=F32)


def tn(a, b):
    return lax.dot_general(a, b, (((0,), (0,)), ((), ())), preferred_element_type=F32)


def split(a):
    high = a.astype(B16)
    return high, (a - high.astype(F32))


def exact_dot(ones, a):
    high, rest = split(a)
    mid, rest = split(rest)
    return nn(ones, high) + nn(ones, mid) + nn(ones, rest.astype(B16))


def two_dot(a, ones):
    high, rest = split(a)
    return nn(high, ones) + nn(rest.astype(B16), ones)


def iota(shape, dim):
    return lax.broadcasted_iota(jnp.int32, shape, dim)


def softplus(a):
    return jnp.maximum(a, 0.0) + jnp.log1p(jnp.exp(-jnp.abs(a)))


def three(a, b):
    ah, al = split(a)
    bh, bl = split(b)
    return nt(ah, bh) + nt(al.astype(B16), bh) + nt(ah, bl.astype(B16))


def silu(a):
    return a * jax.nn.sigmoid(a)


def silu_grad(a):
    sig = jax.nn.sigmoid(a)
    return sig * (1.0 + a * (1.0 - sig))


def rms_scale(x):
    return lax.rsqrt(jnp.mean(x * x, axis=1, keepdims=True) + EPSILON)


def total(refs):
    out = refs[0][...].astype(F32)
    for extra in refs[1:]:
        out = out + extra[...].astype(F32)
    return out


def boundary(starts, base):
    found = False
    for k in range(starts.shape[0]):
        at = starts[k]
        found = found | ((at > 0) & (at > base - 3) & (at < base + Q + 3))
    return found


def prep_kernel(place, w_bt, conv, bias, gain, out):
    span, d = w_bt.shape
    quarter = span // 4
    side = lax.rem(lax.div(place[1], 2), 4)
    out[0:quarter, :] = w_bt[pl.ds(pl.multiple_of(side * quarter, quarter), quarter), :]
    rows = jnp.concatenate([conv[...], bias[...].reshape(1, span), jnp.zeros((3, span), F32)], axis=0)
    high, rest = split(rows)
    mid, rest = split(rest)
    wide = jnp.concatenate(
        [high.astype(F32), mid.astype(F32), rest, jnp.zeros((8, d - 3 * span), F32)], axis=1
    )
    row = jnp.concatenate(
        [gain[...].astype(F32).reshape(1, gain.shape[0]), jnp.zeros((1, d - gain.shape[0]), F32)],
        axis=1,
    )
    wide = jnp.where(iota((8, d), 0) == 5, row, wide)
    out[quarter:, :] = wide.astype(B16)


def stack_kernel(*refs):
    *ins, out = refs
    rows = out.shape[0] // len(ins)
    for k, ref in enumerate(ins):
        out[k * rows : (k + 1) * rows, :] = ref[0:rows, :]


def setup_kernel(heads, n, place, *refs):
    earlies, bts = refs[:n], refs[n : n + 4]
    (
        w_step, conv_i, bias_i, sbias, dlog, skips, ngain, w_bt, taps, gain, hp, w_s, vec,
    ) = refs[n + 4 :]
    inner = conv_i.shape[1]
    full = taps.shape[1]
    span = w_bt.shape[0] // n
    quarter = span // 4
    gain_own = gain.shape[1] // n
    w = place[0]
    side = lax.rem(lax.div(place[1], 2), 4)
    taps[0:4, 0:inner] = conv_i[...]
    taps[4:5, 0:inner] = bias_i[...].reshape(1, inner)
    taps[5:8, :] = jnp.zeros((3, full), F32)
    hp[...] = jnp.zeros_like(hp)
    for g in range(16):
        lanes = slice(8 * g, 8 * g + heads)
        hp[0:1, lanes] = sbias[...].reshape(1, heads)
        hp[1:2, lanes] = jnp.exp(dlog[...].reshape(1, heads))
    low = iota((1, 128), 1) < 64
    for p in range(heads // 2):
        one, two = (jnp.broadcast_to(skips[...].reshape(1, heads)[:, h : h + 1], (1, 128)) for h in (2 * p, 2 * p + 1))
        vec[0:1, p * 128 : (p + 1) * 128] = jnp.where(low, one, two)
    vec[1:2, :] = ngain[...].reshape(1, inner)
    copies = (iota((heads, 128), 0) == lax.rem(iota((heads, 128), 1), 8)).astype(F32)
    w_s[...] = nn(w_step[...], copies.astype(B16)).astype(B16)
    for k in range(n):
        v = lax.rem(w - k + n, n)
        for q in range(4):
            at = v * span + (side ^ q) * quarter
            w_bt[pl.ds(pl.multiple_of(at, quarter), quarter), :] = bts[q][
                k * quarter : (k + 1) * quarter, :
            ]
    for v in range(n):
        for k in range(n):

            @pl.when(lax.rem(w - v + n, n) == k)
            def _(v=v, k=k):
                low = inner + v * span
                small = earlies[k][quarter:, :].astype(F32)
                taps[0:5, low : low + span] = (
                    small[0:5, 0:span] + small[0:5, span : 2 * span]
                ) + small[0:5, 2 * span : 3 * span]
                gain[0:1, v * gain_own : (v + 1) * gain_own] = small[5:6, 0:gain_own]


def front_kernel(n, place, starts, *refs):
    xs, halos = refs[:n], refs[n : 2 * n]
    (
        w_bt, taps, gain, hp, w_s, w_in, tri, e_step, e_enter, e_end,
        normed_o, vals_o, bvals_o, pre_o, bpre_o, bc_o, pk_o, pk2_o, cumt_o, scaled_o, sent_o,
        dp_o, fin_o, hv_o, hn_o, tok_o, docrow_o,
        ext, state, prod, x,
    ) = refs[2 * n :]
    c = pl.program_id(0)
    inner = w_in.shape[1]
    full = ext.shape[1]
    w = place[0]

    def project(values):
        wide = values.astype(F32)
        return (wide * rms_scale(wide) * gain[0:1, :]).astype(B16)

    @pl.when(c == 0)
    def _():
        hn = project(total(halos))
        hn_o[...] = hn
        ext[0:8, 0:inner] = nn(hn, w_in[...])
        ext[0:8, inner:full] = nt(hn, w_bt[...])
        hv_o[...] = ext[0:8, :]
        state[...] = jnp.zeros_like(state)
        prod[...] = jnp.ones_like(prod)

    @pl.when(c > 0)
    def _():
        ext[0:8, :] = ext[Q : Q + 8, :]

    for k in range(n):

        @pl.when(lax.rem(w - c + n, n) == k)
        def _(k=k):
            x[...] = xs[k][...]

    def docs_at(positions):
        found = jnp.zeros(positions.shape, jnp.int32)
        for k in range(starts.shape[0]):
            found = found + (starts[k] <= positions).astype(jnp.int32)
        return found - 1

    base = (place[1] * pl.num_programs(0) + c) * Q
    here = base + iota((Q, 8), 0)
    lane = iota((Q, 8), 1)
    other = jnp.where(lane < 3, here - 3 + lane, jnp.where(lane == 3, base - 1, base + Q - 1))
    docs = docs_at(here)
    tok = jnp.where(lane == 5, docs, (docs_at(other) == docs).astype(jnp.int32)).astype(F32)
    tok_o[...] = tok
    docrow_o[...] = docs_at(base + iota((8, Q), 1)).astype(F32)

    normed = project(x[...])
    normed_o[...] = normed
    ext[8 : Q + 8, 0:inner] = nn(normed, w_in[...])
    ext[8 : Q + 8, inner:full] = nt(normed, w_bt[...])
    vals_o[...] = ext[8 : Q + 8, 0:inner].astype(B16)
    bvals_o[...] = ext[8 : Q + 8, inner:full].astype(B16)
    pre = taps[4:5, :] + taps[3:4, :] * ext[8 : Q + 8, :]
    for k in range(3):
        pre = pre + taps[k : k + 1, :] * ext[5 + k : 5 + k + Q, :]
    pre_o[...] = pre[:, :inner]
    bpre_o[...] = pre[:, inner:]

    @pl.when(boundary(starts, base))
    def _():
        again = taps[4:5, :] + taps[3:4, :] * ext[8 : Q + 8, :]
        for k in range(3):
            again = again + taps[k : k + 1, :] * ext[5 + k : 5 + k + Q, :] * tok_o[:, k : k + 1]
        pre_o[...] = again[:, :inner]
        bpre_o[...] = again[:, inner:]

    act = silu(pre_o[...])
    bc = silu(bpre_o[...]).astype(B16)
    bc_o[...] = bc
    sr = nn(normed, w_s[...]) + hp[0:1, :]
    step = softplus(sr)
    cums = exact_dot(tri[...], -hp[1:2, :] * step)
    enter = jnp.exp(cums) * tok[:, 3:4]
    end = jnp.exp(cums[Q - 1 : Q, :] - cums) * tok[:, 4:5]
    lane = iota((Q, 128), 1)
    group = lax.rem(lane, 64) // 8
    pk = jnp.where(
        group == STEP, step,
        jnp.where(
            group == ENTER, enter,
            jnp.where(group == END, end, jnp.where(group == SIG, jax.nn.sigmoid(sr), cums)),
        ),
    )
    pk_o[...] = pk
    high, low = split(pk)
    pk2 = jnp.where(lane < 64, high.astype(F32), low).astype(B16)
    pk2_o[...] = pk2
    cumt_o[...] = cums.T[0:8, :]
    scaled = nn(pk2, e_step[...]) * act
    scaled_o[...] = scaled.astype(B16)
    x16, x_lo = split(nn(pk2, e_end[...]) * scaled)
    x_lo = x_lo.astype(B16)
    carry = nn(pk2[Q - 16 :], e_enter[...])[15:16, :]
    sent_o[0] = state[...]
    dp_o[0] = prod[...]
    state[...] = carry * state[...] + tn(bc[:, :128], x16) + tn(bc[:, :128], x_lo)
    prod[...] = prod[...] * carry
    fin_o[0:128, :] = state[...].astype(B16)
    fin_o[128:144, :] = jnp.concatenate([prod[...], prod[...]], axis=0).astype(B16)


def intra_kernel(heads, normed, w_gate, pre, bc, pk, cumt, scaled, tok, docrow, vec, gate_o, y_o):
    gate_o[...] = nn(normed[...], w_gate[...])
    low = iota((HALF, 128), 1) < 64
    for block in range(2):
        rows = slice(block * HALF, (block + 1) * HALF)
        wide = (block + 1) * HALF
        scores = nt(bc[rows, 128:], bc[:wide, :128])
        mask = (block * HALF + iota((HALF, wide), 0) >= iota((HALF, wide), 1)) & (
            tok[rows, 5:6] == docrow[0:1, :wide]
        )
        for pair in range(heads // 2):
            cols = slice(pair * 128, (pair + 1) * 128)
            values = scaled[:wide, cols]
            outs = []
            for h in (2 * pair, 2 * pair + 1):
                diff = pk[rows, 8 * CUMS + h : 8 * CUMS + h + 1] - cumt[h : h + 1, :wide]
                mix = scores * jnp.where(mask, jnp.exp(diff), 0.0)
                outs.append(nn(mix.astype(B16), values))
            y_o[rows, cols] = jnp.where(low, *outs) + vec[0:1, cols] * silu(pre[rows, cols])


def fold_states(keep, others, out):
    state = jnp.zeros(out.shape, F32)
    for ref in reversed(others):
        state = ref[128:129, :].astype(F32) * state + ref[0:128, :].astype(F32)
    out[...] = keep[128:129, :] * state + keep[0:128, :]


def pair_kernel(reverse, place, own, other, keep_o, total_o):
    mine, theirs = own[...].astype(F32), other[...].astype(F32)
    earlier = lax.rem(place[1], 2) == (0 if reverse else 1)
    keep_o[0:128, :] = jnp.where(earlier, theirs[0:128, :], 0.0)
    keep_o[128:, :] = jnp.where(earlier, theirs[128:136, :], 1.0)
    total_o[0:128, :] = jnp.where(
        earlier,
        mine[128:129, :] * theirs[0:128, :] + mine[0:128, :],
        theirs[128:129, :] * mine[0:128, :] + theirs[0:128, :],
    ).astype(B16)
    total_o[128:, :] = (mine[128:, :] * theirs[128:, :]).astype(B16)


def join_kernel(n, m, place, y, gate, bc, pk2, sent, dp, keep, *refs):
    others = refs[:m]
    w_out, vec, e_enter, ssd_o, inter_o, gated_o, squares_o, s_in = refs[m : m + 8]
    mixes = refs[m + 8 :]
    c = pl.program_id(0)
    inner = y.shape[1]

    @pl.when(c == 0)
    def _():
        fold_states(keep, others, s_in)

    entering = sent[0] + dp[0, 0:1, :] * s_in[...]
    inter = nn(pk2[...], e_enter[...]) * nn(bc[:, 128:], entering.astype(B16))
    inter_o[...] = inter
    ssd = y[...] + inter
    ssd_o[...] = ssd
    gated = ssd * silu(gate[...])
    gated_o[...] = gated
    mixed = nn((gated * vec[1:2, :]).astype(B16), w_out[...]).astype(B16)
    for k in range(n):

        @pl.when(lax.rem(c - place[0] + n, n) == k)
        def _(k=k):
            mixes[k][...] = mixed

    first = (iota((inner, 128), 1) == 0).astype(F32).astype(B16)
    squares_o[...] = two_dot(gated * gated, first).T[0:8, :]


def dots_kernel(n, place, gated, squares, *refs):
    cots = refs[:n]
    w_out, vec, gn_o, stats_o, cot_o = refs[n:]
    c = pl.program_id(0)
    inner = gated.shape[1]
    for k in range(n):

        @pl.when(lax.rem(place[0] - c + n, n) == k)
        def _(k=k):
            cot_o[...] = cots[k][...]

    gn = nt(cot_o[...], w_out[...])
    gn_o[...] = gn
    second = (iota((inner, 128), 1) == 1).astype(F32).astype(B16)
    stats_o[...] = squares[...] + two_dot(vec[1:2, :] * gn * gated[...], second).T[0:8, :]


def gate_kernel(n, width_all, ssd, gate, gn, vec, pre, bc, pk2, e_enter, *refs):
    stats = refs[:n]
    norm_o, gate_o, gs_o, sums_o, sb_o, db_o, fin_o, rms_o, state, prod = refs[n:]
    i = pl.program_id(0)

    @pl.when(i == 0)
    def _():
        state[...] = jnp.zeros_like(state)
        prod[...] = jnp.ones_like(prod)
        sums_o[...] = jnp.zeros_like(sums_o)

    st = total(stats)
    rms = lax.rsqrt(st[0:1, :] / width_all + EPSILON)
    pull = rms * rms * rms * st[1:2, :] / width_all
    st = jnp.concatenate([rms, pull, jnp.zeros((126, Q), F32)], axis=0).T
    rms, pull = st[:, 0:1], st[:, 1:2]
    rms_o[...] = st[:, 0:8]
    g = gate[...]
    sig = jax.nn.sigmoid(g)
    s = ssd[...]
    act_g = g * sig
    gated = s * act_g
    scaled = gated * rms
    ngain = vec[1:2, :]
    norm_o[...] = (scaled * ngain).astype(B16)
    gn_ = gn[...]
    grad_gated = rms * (ngain * gn_) - gated * pull
    gs = grad_gated * act_g
    gs_o[...] = gs
    gate_o[...] = (grad_gated * s * (sig * (1.0 + g * (1.0 - sig)))).astype(B16)
    sums_o[0:1, :] += jnp.sum(gn_ * scaled, axis=0, keepdims=True)
    sums_o[1:2, :] += jnp.sum(gs * silu(pre[...]), axis=0, keepdims=True)
    enter = nn(pk2[...], e_enter[...])
    carry = enter[Q - 1 : Q, :]
    sb_o[0] = state[...]
    db_o[0] = prod[...]
    state[...] = carry * state[...] + tn(bc[:, 128:], (enter * gs).astype(B16)) + tn(bc[:, 128:], split(enter * gs)[1].astype(B16))
    prod[...] = prod[...] * carry
    fin_o[0:128, :] = state[...].astype(B16)
    fin_o[128:144, :] = jnp.concatenate([prod[...], prod[...]], axis=0).astype(B16)


def intra_back_kernel(
    heads, gs, bc, pk, pk2, cumt, scaled, tok, docrow, sent, dp, s_in, e_enter,
    gsc_o, rc_o, gbc_o, tot, plus, minus,
):
    low = iota((HALF, 128), 1) < 64
    g16 = gs[...].astype(B16)
    plus[...] = jnp.zeros_like(plus)
    for block in range(2):
        rows = slice(block * HALF, (block + 1) * HALF)
        wide = slice(block * HALF, Q)
        width = Q - block * HALF
        scores = nt(bc[rows, :128], bc[wide, 128:])
        mask = (iota((HALF, width), 0) <= iota((HALF, width), 1)) & (
            tok[rows, 5:6] == docrow[0:1, wide]
        )
        sums = jnp.zeros((HALF, width), F32)
        lane = iota((HALF, 128), 1)
        minus_acc = jnp.zeros((HALF, 128), F32)
        for pair in range(heads // 2):
            cols = slice(pair * 128, (pair + 1) * 128)
            mine = scaled[rows, cols]
            grads = g16[wide, cols]
            outs = []
            for h in (2 * pair, 2 * pair + 1):
                diff = cumt[h : h + 1, wide] - pk[rows, 8 * CUMS + h : 8 * CUMS + h + 1]
                decay = jnp.where(mask, jnp.exp(diff), 0.0)
                keep = low if h % 2 == 0 else ~low
                masked = jnp.where(keep, mine.astype(F32), 0.0).astype(B16)
                weighted = decay * nt(masked, grads)
                sums = sums + weighted
                ws = scores * weighted
                plus[h : h + 1, wide] += jnp.sum(ws, axis=0, keepdims=True)
                minus_acc = jnp.where(
                    lax.rem(lane, 8) == h, jnp.sum(ws, axis=1, keepdims=True), minus_acc
                )
                outs.append(nn((scores * decay).astype(B16), grads))
            gsc_o[rows, cols] = jnp.where(low, *outs)
        minus[rows, :] = minus_acc
        tot[rows, wide] = sums.astype(B16)
    tot[HALF:, :HALF] = jnp.zeros((HALF, HALF), B16)
    rc_o[...] = jnp.concatenate([plus[...]] * 16, axis=0).T - minus[...]
    entering = sent[0] + dp[0, 0:1, :] * s_in[...]
    t16 = tot[...]
    enter = nn(pk2[...], e_enter[...]) * gs[...]
    gbc_o[:, :128] = nn(t16, bc[:, 128:])
    gbc_o[:, 128:] = tn(t16, bc[:, :128]) + three(enter, entering)


def conv_back(i, count, masked, gp, tok, taps, vals, hv, ext, mext, shift, out, sums_o, rim_o):
    ch = gp.shape[1]

    @pl.when(i == 0)
    def _():
        ext[Q : Q + 8, :] = jnp.zeros((8, ch), F32)
        mext[Q : Q + 8, :] = jnp.zeros((8, 8), F32)
        sums_o[...] = jnp.zeros_like(sums_o)

    @pl.when(i > 0)
    def _():
        ext[Q : Q + 8, :] = ext[0:8, :]
        mext[Q : Q + 8, :] = mext[0:8, :]

    ext[0:Q, :] = gp
    mext[0:Q, :] = tok
    sums_o[4:5, :] += jnp.sum(gp, axis=0, keepdims=True)

    def sweep(use_mask):
        vals_ = vals.astype(F32)
        acc = jnp.zeros((Q, ch), F32)
        for k in range(4):
            z = ext[3 - k : 3 - k + Q, :]
            if k < 3 and use_mask:
                z = z * mext[3 - k : 3 - k + Q, k : k + 1]
            acc = acc + taps[k : k + 1, :] * z
            sums_o[k : k + 1, :] += jnp.sum(vals_ * z, axis=0, keepdims=True)
        out[...] = acc.astype(B16)

    @pl.when(masked)
    def _():
        sweep(True)

    @pl.when(jnp.logical_not(masked))
    def _():
        sweep(False)

    @pl.when(i == count - 1)
    def _():
        rim = jnp.zeros((8, ch), F32)
        shift[0:8, :] = jnp.zeros((8, ch), F32)
        for k in range(3):
            shift[8:16, :] = ext[0:8, :] * mext[0:8, k : k + 1]
            moved = shift[3 - k : 11 - k, :]
            rim = rim + taps[k : k + 1, :] * moved
            sums_o[k : k + 1, :] += jnp.sum(hv * moved, axis=0, keepdims=True)
        rim_o[...] = rim


def chunk_base(place, count, i):
    return (place[1] * count + (count - 1 - i)) * Q


def bcoef_back_kernel(
    count, n, m, place, starts, gbc, pre, vals, pk2, scaled, tok, sb, db, taps, hv, e_end,
    keep, *refs
):
    others, packs = refs[:m], refs[m : m + n]
    sums_o, s_after, ext, mext, shift, rim_o, out, pieces = refs[m + n :]
    i = pl.program_id(0)
    inner = scaled.shape[1]

    @pl.when(i == 0)
    def _():
        fold_states(keep, others, s_after)

    after_ = sb[0] + db[0, 0:1, :] * s_after[...]
    x16 = nn(pk2[...], e_end[...]) * scaled[...].astype(F32)
    gbm = gbc[:, :128] + three(x16, after_)
    gp = jnp.concatenate([gbm, gbc[:, 128:]], axis=1) * silu_grad(pre[...])
    conv_back(
        i, count, boundary(starts, chunk_base(place, count, i)), gp, tok[...],
        taps[:, inner:], vals[...], hv[:, inner:], ext, mext, shift, out, sums_o, rim_o,
    )
    span = 256 // n
    row = pl.multiple_of((count - 1 - i) * HALF, HALF)
    for v in range(n):
        piece = out[:, v * span : (v + 1) * span]
        pieces[v] = jnp.concatenate([piece[:HALF], piece[HALF:]], axis=1)
    for k in range(n):
        packs[k][pl.ds(row, HALF), :] = pieces[lax.rem(place[0] + k, n)]

    @pl.when(i == count - 1)
    def _():
        for v in range(n):
            edge = rim_o[:, v * span : (v + 1) * span]
            pieces[v, 0:16, 0:span] = jnp.concatenate([edge, edge], axis=0).astype(B16)
        for k in range(n):
            packs[k][count * HALF :, :] = pieces[lax.rem(place[0] + k, n), 0:16, :]


def inner_back_kernel(
    count, place, starts, gs, gsc, rc, inter, pre, vals, bc, pk, pk2, scaled, tok, sent,
    dp, s_in, sb, db, s_after, taps, hp, hv, vec, tri, e_step, e_enter, e_end, hmap,
    gv_o, step_o, rim_o, sums_o, small_o, ext, mext, shift,
):
    i = pl.program_id(0)
    entering = sent[0] + dp[0, 0:1, :] * s_in[...]
    after_ = sb[0] + db[0, 0:1, :] * s_after[...]
    p = pre[...]
    sig_p = jax.nn.sigmoid(p)
    act = p * sig_p
    weights = pk2[...]
    end_state = nn(weights, e_end[...]) * nn(bc[:, :128], after_.astype(B16))
    gsc_ = gsc[...] + end_state
    grad = gs[...]
    end_terms = scaled[...].astype(F32) * end_state
    carry = nn(weights[Q - 16 :], e_enter[...])[15:16, :]
    closing = jnp.sum(end_terms, axis=0, keepdims=True) + carry * jnp.sum(
        after_ * entering, axis=0, keepdims=True
    )
    closing = two_dot(jnp.broadcast_to(closing, (8, closing.shape[1])), hmap[...])[0:1, :]
    grad_cums = rc[...] + two_dot(grad * inter[...] - end_terms, hmap[...])
    grad_cums = grad_cums + jnp.where(iota((Q, 128), 0) == Q - 1, closing, 0.0)
    high, low = split(grad_cums)
    grad_decay = tn(tri[...], high) + tn(tri[...], low.astype(B16))
    drive = hp[1:2, :] * grad_decay
    raw = (nn((gsc_ * act).astype(B16), hmap[...]) - drive) * pk[...]
    lane = iota((Q, 128), 1)
    step_o[...] = jnp.where(lane // 8 == SIG, raw, 0.0).astype(B16)

    @pl.when(i == 0)
    def _():
        small_o[...] = jnp.zeros_like(small_o)

    small_o[0:1, :] += jnp.sum(raw, axis=0, keepdims=True)
    small_o[1:2, :] -= jnp.sum(drive * pk[...], axis=0, keepdims=True)
    gp = (nn(weights, e_step[...]) * gsc_ + vec[0:1, :] * grad) * (
        sig_p * (1.0 + p * (1.0 - sig_p))
    )
    conv_back(
        i, count, boundary(starts, chunk_base(place, count, i)), gp, tok[...], taps[...],
        vals[...], hv[...], ext, mext, shift, gv_o, sums_o, rim_o,
    )


def gate_grads_kernel(place, gnorm, normed, gate16, cot, keep_o, send_o):
    r = pl.program_id(0)
    core = lax.rem(place[1], 2)
    inner = gate16.shape[1]
    left = tn(normed[...], gate16[...]).astype(B16)
    right = tn(gnorm[...], cot[...]).astype(B16)

    @pl.when(r == core)
    def _():
        keep_o[:, 0:inner] = left
        keep_o[:, inner:] = right

    @pl.when(r != core)
    def _():
        send_o[:, 0:inner] = left
        send_o[:, inner:] = right


def inner_grads_kernel(
    place, gv, gv_all, rim, hn, gate16, step16, normed, w_in, w_gate, w_s, part_o, keep_o, send_o
):
    r = pl.program_id(0)
    core = lax.rem(place[1], 2)
    part_o[...] = nt(gv[...], w_in[...]) + nt(gate16[...], w_gate[...]) + nt(step16[...], w_s[...])
    grads = (tn(normed[...], gv_all[...]) + tn(hn[...], rim[...].astype(B16))).astype(B16)

    @pl.when(r == core)
    def _():
        keep_o[...] = grads

    @pl.when(r != core)
    def _():
        send_o[...] = grads


def bcoef_grads_kernel(count, n, pack_view, tail_view, place, *refs):
    packs = [pack_view(ref, pl.program_id(0), (place,)) for ref in refs[:n]]
    tails = [tail_view(ref, 0, (place,)) for ref in refs[:n]]
    (
        rim_i, hn, part, normed, w_bt, w_in, step16, gain, csum_b, csum_i, ssum, nsums,
    ) = refs[n : n + 12]
    parts = refs[n + 12 : 2 * n + 12]
    keep_o, send_o, small_o, local_o, acc, gsum = refs[2 * n + 12 :]
    i = pl.program_id(0)
    span, d = w_bt.shape
    inner = w_in.shape[1]

    @pl.when(i == 0)
    def _():
        rim16 = total(tails)[0:8, :span].astype(B16)
        edge = nn(rim16, w_bt[...]) + nt(rim_i[...].astype(B16), w_in[...])
        small_o[3:8, :] = edge[3:8, :]
        gsum[...] = jnp.sum(edge * hn[...].astype(F32), axis=0, keepdims=True)
        acc[...] = tn(jnp.concatenate([rim16, jnp.zeros((8, span), B16)], axis=1), hn[...])

    packed = total(packs)
    v16 = jnp.concatenate([packed[:, :span], packed[:, span:]], axis=0).astype(B16)
    sums = part[...] + nn(v16, w_bt[...])
    for k in range(n):

        @pl.when(i == k)
        def _(k=k):
            parts[k][...] = sums.astype(B16)

    x16 = normed[...]
    gsum[...] += jnp.sum(sums * x16.astype(F32), axis=0, keepdims=True)
    acc[...] += tn(jnp.concatenate([v16, step16[:, :span]], axis=1), x16)

    @pl.when(i == count - 1)
    def _():
        turned = acc[...].T.astype(B16)
        core = lax.rem(place[1], 2)
        half = d // 2

        @pl.when(core == 0)
        def _():
            keep_o[...] = turned[:half]
            send_o[...] = turned[half:]

        @pl.when(core == 1)
        def _():
            keep_o[...] = turned[half:]
            send_o[...] = turned[:half]

        small_o[0:1, :] = gsum[...] / gain[0:1, :]
        for k in range(3):
            small_o[1:2, k * 256 : (k + 1) * 256] = csum_b[k : k + 1, :]
            local_o[3 + k : 4 + k, 0:inner] = csum_i[2 * k : 2 * k + 1, :]
        for k in range(2):
            small_o[2:3, k * 256 : (k + 1) * 256] = csum_b[3 + k : 4 + k, :]
            local_o[3 + k : 4 + k, inner:] = csum_i[2 * k + 1 : 2 * k + 2, :]
        local_o[5:6, inner:] = nsums[1:2, :]
        local_o[6:7, 0:inner] = nsums[0:1, :]
        local_o[6:7, inner : inner + 128] = ssum[0:1, :]
        local_o[6:7, inner + 128 : inner + 256] = ssum[1:2, :]


def small_kernel(local, *refs):
    *ins, small_o, edge_o = refs
    both = total(ins)
    small_o[0:3, :] = both[0:3, :]
    small_o[3:8, :] = local[3:8, :]
    edge_o[0:3, :] = jnp.zeros((3, both.shape[1]), F32)
    edge_o[3:8, :] = both[3:8, :]


def last_kernel(n, place, x, cot, gain, edge, rms, *refs):
    parts, mixes, (grad_o, block_o) = refs[:n], refs[n : 2 * n], refs[2 * n :]
    sums = total(parts)
    rows = sums.shape[0]
    sums = jnp.concatenate([sums[: rows - 8], sums[rows - 8 :] + edge[...]], axis=0)
    wide = x[...].astype(F32)
    own = rms[pl.ds(pl.multiple_of(place[0] * rows, rows), rows), 0:1]
    block_o[...] = (wide + own * total(mixes)).astype(B16)
    scale = rms_scale(wide)
    scaled = gain[0:1, :] * sums
    dot = jnp.sum(scaled * wide, axis=1, keepdims=True)
    width = wide.shape[1]
    grad_o[...] = (
        cot[...].astype(F32) + scale * scaled - wide * (scale * scale * scale * dot / width)
    )


def add_kernel(a, b, out):
    out[...] = a[...] + b[...]


def ends_kernel(n, heads, place, *refs):
    smalls = refs[:n]
    gain_o, taps_i_o, taps_b_o, bias_i_o, bias_b_o, sbias_o, dlog_o, skip_o, ngain_o = refs[n:]
    sums = total(smalls)
    inner, span = ngain_o.shape[0], bias_b_o.shape[0]
    count, own = 256 // span, gain_o.shape[0]
    for v in range(count):

        @pl.when(place[0] == v)
        def _(v=v):
            gain_o[...] = sums[0:1, v * own : (v + 1) * own].reshape(own)
            low = v * span
            for k in range(4):
                row, at = (1, 256 * k) if k < 3 else (2, 0)
                taps_b_o[k : k + 1, :] = sums[row : row + 1, at + low : at + low + span]
            bias_b_o[...] = sums[2:3, 256 + low : 256 + low + span].reshape(span)

    taps_i_o[0:1, :] = sums[3:4, :inner]
    taps_i_o[1:2, :] = sums[3:4, inner:]
    taps_i_o[2:3, :] = sums[4:5, :inner]
    taps_i_o[3:4, :] = sums[4:5, inner:]
    bias_i_o[...] = sums[5:6, :inner].reshape(inner)
    ngain_o[...] = sums[6:7, :inner].reshape(inner)
    raw_at, decay_at = inner + 8 * SIG, inner + 128 + 8 * STEP
    sbias_o[...] = sums[6:7, raw_at : raw_at + heads].reshape(heads)
    dlog_o[...] = sums[6:7, decay_at : decay_at + heads].reshape(heads)
    hit = iota((8, inner), 1) // (inner // heads) == iota((8, inner), 0)
    rows = jnp.where(hit, sums[5:6, inner:], 0.0)
    column = jnp.sum(rows, axis=1, keepdims=True)
    skip_o[...] = jnp.broadcast_to(column, (8, 128)).T[0:1, 0:heads].reshape(heads)


def halves_kernel(n, place, *refs):
    ins, outs = refs[:6], refs[6:]
    rows = outs[0].shape[0]
    for k in range(n):
        piece = pl.ds(pl.multiple_of(lax.rem(lax.div(place[1], 2) + k, n) * rows, rows), rows)
        at = 0
        for j in range(3):
            mine, theirs = ins[2 * j], ins[2 * j + 1]
            cols = slice(at, at + mine.shape[1])
            at += mine.shape[1]
            outs[k][:, cols] = (
                mine[piece, :].astype(F32) + theirs[piece, :].astype(F32)
            ).astype(B16)


def pieces_kernel(*refs):
    refs[-1][...] = total(refs[:-1]).astype(B16)


def unpack_kernel(n, place, *refs):
    pieces = refs[: 2 * n]
    gate_o, inner_o, bcoef_o, step_o, out_o, late = refs[2 * n :]
    rows = pieces[0].shape[0]
    inner = gate_o.shape[1]
    span = bcoef_o.shape[0]
    heads = step_o.shape[0]
    for side in range(2):
        for k in range(n):
            piece = pieces[side * n + k][...].astype(F32)
            whole_half = lax.rem(lax.div(place[1], 2) - k + n, n)
            core = lax.rem(place[1] + side, 2)
            at = pl.multiple_of(core * (n * rows) + whole_half * rows, rows)
            dst = pl.ds(at, rows)
            gate_o[dst, :] = piece[:, 0:inner]
            inner_o[dst, :] = piece[:, 2 * inner : 3 * inner]
            late[dst, :] = piece[:, 3 * inner :]
            low = pl.ds(pl.multiple_of(whole_half * rows, rows), rows)

            @pl.when(core == 0)
            def _():
                out_o[low, 0:inner] = piece[:, inner : 2 * inner]

            @pl.when(core == 1)
            def _():
                out_o[low, inner:] = piece[:, inner : 2 * inner]

    turned = late[...].T
    bcoef_o[...] = turned[:span, :]
    step_o[...] = turned[span + 8 * SIG : span + 8 * SIG + heads, :]


def shape(dims, dtype=F32):
    return jax.ShapeDtypeStruct(dims, dtype)


def call(
    kernel, grid, ins, in_specs, outs, out_specs, scratch=(), scalars=(), flops=0,
    fetch=(),
):
    size = sum(a.size * a.dtype.itemsize for a in ins) + sum(
        o.size * o.dtype.itemsize for o in outs
    )
    views = list(in_specs) + list(out_specs)
    ins = [
        pltpu.with_memory_space_constraint(a, pltpu.HBM) if k in fetch else a
        for k, a in enumerate(ins)
    ]

    landing = [pltpu.VMEM(ins[k].shape, ins[k].dtype) for k in fetch]
    landing += [pltpu.SemaphoreType.DMA((len(fetch),))] if fetch else []

    def body(*refs):
        first = len(scalars)
        step = pl.program_id(0) if grid else 0
        if fetch:
            refs, local, sems = list(refs[: -len(landing)]), refs[-len(landing) : -1], refs[-1]

            sources = [refs[first + k] for k in fetch]

            def copies():
                return [
                    pltpu.make_async_copy(source, local[j], sems.at[j])
                    for j, source in enumerate(sources)
                ]

            def bring():
                for copy in copies():
                    copy.start()
                for copy in copies():
                    copy.wait()

            if grid:
                pl.when(step == 0)(bring)
            else:
                bring()
            for j, k in enumerate(fetch):
                refs[first + k] = local[j]
        seen = [
            view(ref, step, refs[:first]) if view else ref
            for view, ref in zip(views, refs[first:])
        ]
        kernel(*refs[:first], *seen, *refs[first + len(views) :])

    return pl.pallas_call(
        body,
        out_shape=outs,
        grid_spec=pltpu.PrefetchScalarGridSpec(
            num_scalar_prefetch=len(scalars),
            grid=grid,
            in_specs=[HBM if k in fetch else VMEM for k in range(len(ins))],
            out_specs=[VMEM] * len(outs),
            scratch_shapes=list(scratch) + landing,
        ),
        compiler_params=pltpu.CompilerParams(
            dimension_semantics=("arbitrary",) * len(grid) or None,
            vmem_limit_bytes=LIMIT,
        ),
        cost_estimate=pl.CostEstimate(
            flops=int(flops), bytes_accessed=size, transcendentals=0
        ),
    )(*scalars, *ins)


def ring(value, axis, distance):
    count = lax.axis_size(axis)
    return lax.ppermute(value, axis, [(i, (i + distance) % count) for i in range(count)])


def swap(value, axis, bit):
    count = lax.axis_size(axis)
    return lax.ppermute(value, axis, [(i, i ^ (1 << bit)) for i in range(count)])


def spread(value, axis):
    count = lax.axis_size(axis)
    return [value] + [ring(value, axis, k) for k in range(1, count)]


def reduce_parts(parts, axis):
    return [ring(p, axis, k) if k else p for k, p in enumerate(parts)]


def states(fin, place, reverse):
    rows, inner = fin.shape
    count = lax.axis_size("seq")
    other = swap(fin, "seq", 0)
    keep, both = call(
        functools.partial(pair_kernel, reverse), (), [fin, other], [None] * 2,
        [shape((rows - 8, inner)), shape((rows, inner), B16)], [None] * 2,
        scalars=(place,),
    )
    got = []
    for k in range(1, count // 2):
        if reverse:
            pairs = [(i + 2 * k, i) for i in range(count - 2 * k)]
        else:
            pairs = [(i, i + 2 * k) for i in range(count - 2 * k)]
        got.append(lax.ppermute(both, "seq", pairs))
    return keep, got


def per_device(
    block_in,
    in_gain,
    proj_gate,
    proj_inner,
    proj_bcoef,
    proj_step,
    conv_inner,
    conv_inner_bias,
    conv_bcoef,
    conv_bcoef_bias,
    step_bias,
    decay_log,
    skip_gain,
    norm_gain,
    proj_out,
    out_grad,
    doc_starts,
):
    n_wt, n_seq = lax.axis_size("wt"), lax.axis_size("seq")
    w, seq = lax.axis_index("wt"), lax.axis_index("seq")
    rows_own, d = block_in.shape
    length = rows_own * n_wt
    inner = proj_inner.shape[1]
    heads = step_bias.shape[0]
    span = proj_bcoef.shape[1]
    full = inner + span * n_wt
    width_all = inner * n_wt
    count = length // Q
    pairs = n_seq // 2
    place = jnp.stack([w, seq]).astype(jnp.int32)
    scalars = (place, doc_starts)

    w_bt_own = proj_bcoef.T
    quarter = span // 4
    (early,) = call(
        prep_kernel, (), [w_bt_own, conv_bcoef, conv_bcoef_bias, in_gain], [None] * 4,
        [shape((quarter + 8, d), B16)], [None], scalars=(place,),
        fetch=tuple(range(4)),
    )
    earlies = spread(early, "wt")
    rows = spread(block_in, "wt")
    (bts,) = call(
        stack_kernel, (), earlies, [None] * n_wt, [shape((quarter * n_wt, d), B16)], [None],
    )
    bts_x = swap(bts, "seq", 1)
    bts_y = [swap(b, "seq", 2) for b in (bts, bts_x)]
    tail = block_in[rows_own - 8 :]
    halos = []
    for v in range(n_wt):
        halos.append(
            lax.ppermute(
                tail, ("seq", "wt"),
                [((s - 1) * n_wt + n_wt - 1, s * n_wt + v) for s in range(1, n_seq)],
            )
        )
    cots = spread(out_grad, "wt")

    lanes, chans = np.arange(128), np.arange(inner) // (inner // heads)

    def one_hot(group):
        hit = ((lanes % 64) // 8 == group)[:, None] & ((lanes % 8)[:, None] == chans[None, :])
        return jnp.asarray(hit.astype(np.float32), B16)

    e_step, e_enter, e_end = one_hot(STEP), one_hot(ENTER), one_hot(END)
    hmap = jnp.asarray((chans[:, None] == (lanes % 8)[None, :]).astype(np.float32), B16)
    tri = jnp.asarray((np.arange(Q)[:, None] >= np.arange(Q)[None, :]).astype(np.float32), B16)

    grid = (count,)

    def at_rows(ref, index, rows=Q):
        return ref.at[pl.ds(pl.multiple_of(index * rows, rows), rows), :]

    def by_rows(reverse=False):
        if reverse:
            return lambda ref, i, p: at_rows(ref, count - 1 - i)
        return lambda ref, i, p: at_rows(ref, i)

    def by_turn():
        return lambda ref, i, p: at_rows(ref, lax.rem(i + p[0][0], count))

    def whole(*dims):
        return None

    def by_chunk(*dims, reverse=False):
        if reverse:
            return lambda ref, i, p: ref.at[pl.ds(count - 1 - i, 1)]
        return lambda ref, i, p: ref.at[pl.ds(i, 1)]

    def by_lanes(width, reverse=False):
        def view(ref, i, p):
            index = count - 1 - i if reverse else i
            return ref.at[:, pl.ds(pl.multiple_of(index * width, width), width)]

        return view

    def lead(ref, i, p):
        return ref.at[:, :inner]

    by_cols = by_lanes(Q)
    by_cols_back = by_lanes(Q, True)
    fin_spec, state_spec = whole(144, inner), whole(128, inner)
    e_spec = whole(128, inner)
    states_out = [shape((count, 128, inner)), shape((count, 8, inner)), shape((144, inner), B16)]
    w_bt, taps, gain, hp, w_s, vec = call(
        functools.partial(setup_kernel, heads, n_wt), (),
        [*earlies, bts, bts_x, *bts_y, proj_step, conv_inner, conv_inner_bias, step_bias,
         decay_log, skip_gain, norm_gain],
        [None] * (n_wt + 11),
        [shape((span * n_wt, d), B16), shape((8, full)), shape((8, d)), shape((8, 128)),
         shape((d, 128), B16), shape((8, inner))],
        [None] * 6, scalars=(place,), fetch=tuple(range(n_wt + 4, n_wt + 11)),
    )
    (normed, vals, bvals, pre, bpre, bc, pk, pk2, cumt, scaled, sent, dp, fin, hv, hn, tok,
     docrow) = call(
        functools.partial(front_kernel, n_wt), grid,
        [*rows, *halos, w_bt, taps, gain, hp, w_s, proj_inner, tri, e_step, e_enter, e_end],
        [None] * (2 * n_wt + 10),
        [shape((length, d), B16), shape((length, inner), B16), shape((length, 256), B16),
         shape((length, inner)), shape((length, 256)),
         shape((length, 256), B16), shape((length, 128)), shape((length, 128), B16),
         shape((8, length)), shape((length, inner), B16), *states_out,
         shape((8, full)), shape((8, d), B16), shape((length, 8)), shape((8, length))],
        [by_rows(), by_rows(), by_rows(), by_rows(), by_rows(), by_rows(),
         by_rows(), by_rows(),
         by_cols, by_rows(), by_chunk(128, inner), by_chunk(8, inner), fin_spec,
         whole(8, full), whole(8, d), by_rows(), by_cols],
        scratch=[pltpu.VMEM((Q + 8, full), F32), pltpu.VMEM((128, inner), F32),
                 pltpu.VMEM((8, inner), F32), pltpu.VMEM((Q, d), B16)],
        scalars=scalars, flops=2e9,
        fetch=(0, *range(2 * n_wt + 5, 2 * n_wt + 10)),
    )
    keep, got = states(fin, place, False)
    gate, y = call(
        functools.partial(intra_kernel, heads), grid,
        [normed, proj_gate, pre, bc, pk, cumt, scaled, tok, docrow, vec],
        [by_rows(), whole(d, inner), by_rows(), by_rows(), by_rows(), by_cols,
         by_rows(), by_rows(), by_cols, whole(1, inner)],
        [shape((length, inner)), shape((length, inner))],
        [by_rows(), by_rows()], flops=2e9,
    )
    got_spec = [whole(136, inner)] + [fin_spec] * (pairs - 1)
    ssd, inter, gated, squares, s_in, *mixes = call(
        functools.partial(join_kernel, n_wt, pairs - 1), grid,
        [y, gate, bc, pk2, sent, dp, keep, *got, proj_out, vec, e_enter],
        [by_rows(), by_rows(), by_rows(), by_rows(),
         by_chunk(128, inner), by_chunk(8, inner), *got_spec]
        + [whole(inner, d), whole(1, inner), e_spec],
        [shape((length, inner))] * 3 + [shape((8, length)), shape((128, inner))]
        + [shape((Q, d), B16)] * n_wt,
        [by_rows()] * 3 + [by_cols, state_spec] + [None] * n_wt,
        scalars=(place,), flops=2e9,
    )
    gn, stats, cot = call(
        functools.partial(dots_kernel, n_wt), grid,
        [gated, squares, *cots, proj_out, vec],
        [by_rows(), by_cols] + [None] * (n_wt + 2),
        [shape((length, inner)), shape((8, length)), shape((length, d), B16)],
        [by_rows(), by_cols, by_rows()],
        scalars=(place,), flops=1e9,
    )
    gnorm, gate16, gs, nsums, sb, db, back_fin, rms = call(
        functools.partial(gate_kernel, n_wt, width_all), grid,
        [ssd, gate, gn, vec, pre, bc, pk2, e_enter, *spread(stats, "wt")],
        [by_rows(True)] * 3
        + [whole(1, inner), by_rows(True), by_rows(True), by_rows(True), e_spec]
        + [by_cols_back] * n_wt,
        [shape((length, inner), B16), shape((length, inner), B16), shape((length, inner)),
         shape((8, inner)), *states_out, shape((length, 8))],
        [by_rows(True)] * 3
        + [whole(8, inner), by_chunk(128, inner, reverse=True), by_chunk(8, inner, reverse=True),
           fin_spec, by_rows(True)],
        scratch=[pltpu.VMEM((128, inner), F32), pltpu.VMEM((8, inner), F32)],
        flops=1e9,
    )
    keep_b, got_b = states(back_fin, place, True)
    gsc, rc, gbc = call(
        functools.partial(intra_back_kernel, heads), grid,
        [gs, bc, pk, pk2, cumt, scaled, tok, docrow, sent, dp, s_in, e_enter],
        [by_rows(), by_rows(), by_rows(), by_rows(), by_cols, by_rows(),
         by_rows(), by_cols, by_chunk(128, inner), by_chunk(8, inner), state_spec, e_spec],
        [shape((length, inner)), shape((length, 128)), shape((length, 256))],
        [by_rows(), by_rows(), by_rows()],
        scratch=[pltpu.VMEM((Q, Q), B16), pltpu.VMEM((8, Q), F32), pltpu.VMEM((Q, 128), F32)],
        flops=4e9,
    )

    half = d // 2
    d_half = by_lanes(half)
    keep_a, send_a = call(
        gate_grads_kernel, (2,), [gnorm, normed, gate16, cot],
        [whole(length, inner), d_half, whole(length, inner), d_half],
        [shape((half, 2 * inner), B16)] * 2, [whole(half, 2 * inner)] * 2,
        scalars=(place,), flops=2e9,
    )
    got_a = swap(send_a, "seq", 0)
    mixes = reduce_parts(mixes, "wt")

    rows_pack = length // 2 + 16
    *packs, csum_b, s_after = call(
        functools.partial(bcoef_back_kernel, count, n_wt, pairs - 1), grid,
        [gbc, bpre, bvals, pk2, scaled, tok, sb, db, taps, hv, e_end,
         keep_b, *got_b],
        [by_rows(True), by_rows(True), by_rows(True), by_rows(True),
         by_rows(True), by_rows(True), by_chunk(128, inner, reverse=True),
         by_chunk(8, inner, reverse=True), whole(8, full), whole(8, full), e_spec, *got_spec],
        [shape((rows_pack, 128), B16)] * n_wt + [shape((8, 256)), shape((128, inner))],
        [whole(rows_pack, 128)] * n_wt + [whole(8, 256), state_spec],
        scratch=[pltpu.VMEM((Q + 8, 256), F32), pltpu.VMEM((Q + 8, 8), F32),
                 pltpu.VMEM((16, 256), F32), pltpu.VMEM((8, 256), F32),
                 pltpu.VMEM((Q, 256), B16), pltpu.VMEM((n_wt, HALF, 128), B16)],
        scalars=scalars, flops=1e9,
    )
    packs = reduce_parts(packs, "wt")
    gv, step16, rim_i, csum_i, ssum = call(
        functools.partial(inner_back_kernel, count), grid,
        [gs, gsc, rc, inter, pre, vals, bc, pk, pk2, scaled, tok, sent, dp, s_in, sb, db,
         s_after, taps, hp, hv, vec, tri, e_step, e_enter, e_end, hmap],
        [by_rows(True), by_rows(True), by_rows(True), by_rows(True),
         by_rows(True), by_rows(True), by_rows(True), by_rows(True),
         by_rows(True), by_rows(True), by_rows(True),
         by_chunk(128, inner, reverse=True), by_chunk(8, inner, reverse=True), state_spec,
         by_chunk(128, inner, reverse=True), by_chunk(8, inner, reverse=True), state_spec,
         lead, whole(8, 128), lead, whole(1, inner), whole(Q, Q), e_spec,
         e_spec, e_spec, whole(inner, 128)],
        [shape((length, inner), B16), shape((length, 128), B16), shape((8, inner)),
         shape((8, inner)), shape((8, 128))],
        [by_rows(True), by_rows(True), whole(8, inner), whole(8, inner),
         whole(8, 128)],
        scratch=[pltpu.VMEM((Q + 8, inner), F32), pltpu.VMEM((Q + 8, 8), F32),
                 pltpu.VMEM((16, inner), F32)],
        scalars=scalars, flops=1e9,
    )
    t_half = lambda: lambda ref, r, p: at_rows(ref, r, length // 2)
    part, keep_i, send_i = call(
        inner_grads_kernel, (2,),
        [gv, gv, rim_i, hn, gate16, step16, normed, proj_inner, proj_gate, w_s],
        [t_half(), whole(length, inner), whole(8, inner),
         d_half, t_half(), t_half(), d_half,
         whole(d, inner), whole(d, inner), whole(d, 128)],
        [shape((length, d)), shape((half, inner), B16), shape((half, inner), B16)],
        [t_half(), whole(half, inner), whole(half, inner)],
        scalars=(place,), flops=2e9,
    )
    got_i = swap(send_i, "seq", 0)
    pack_spec = lambda ref, i, p: at_rows(ref, lax.rem(i + p[0][0], count), HALF)
    tail_spec = lambda ref, i, p: ref.at[length // 2 : length // 2 + 16, :]
    *parts, keep_p, send_p, small, local = call(
        functools.partial(bcoef_grads_kernel, count, n_wt, pack_spec, tail_spec), grid,
        [*packs, rim_i, hn, part, normed, w_bt_own, proj_inner, step16, gain, csum_b,
         csum_i, ssum, nsums],
        [None] * n_wt
        + [whole(8, inner), whole(8, d), by_turn(), by_turn(), whole(span, d),
           whole(d, inner), by_turn(), whole(8, d), whole(8, 256), whole(8, inner),
           whole(8, 128), whole(8, inner)],
        [shape((Q, d), B16)] * n_wt
        + [shape((half, 2 * span), B16)] * 2 + [shape((8, d))] * 2,
        [whole(Q, d)] * n_wt + [whole(half, 2 * span)] * 2 + [whole(8, d)] * 2,
        scratch=[pltpu.VMEM((2 * span, d), F32), pltpu.VMEM((1, d), F32)],
        scalars=(place,), flops=1e9,
    )
    parts = reduce_parts(parts, "wt")
    got_p = swap(send_p, "seq", 0)
    small, edge = call(
        small_kernel, (), [local, *spread(small, "wt")], [None] * (n_wt + 1),
        [shape((8, d))] * 2, [None] * 2,
    )
    edge = lax.ppermute(
        edge, ("seq", "wt"),
        [(s * n_wt + n_wt - 1, (s - 1) * n_wt + n_wt - 1) for s in range(1, n_seq)],
    )
    input_grad, block_out = call(
        functools.partial(last_kernel, n_wt), (),
        [block_in, out_grad, gain, edge, rms, *parts, *mixes], [None] * (5 + 2 * n_wt),
        [shape((rows_own, d)), shape((rows_own, d), B16)], [None] * 2, scalars=(place,),
    )

    def pair_ring(value, k):
        return lax.ppermute(
            value, "seq", [(i, (i + 2 * k) % n_seq) for i in range(n_seq)]
        )

    wide = 3 * inner + 2 * span
    piece_rows = half // pairs
    pieces = call(
        functools.partial(halves_kernel, pairs), (),
        [keep_a, got_a, keep_i, got_i, keep_p, got_p], [None] * 6,
        [shape((piece_rows, wide), B16)] * pairs, [None] * pairs,
        scalars=(place,),
    )
    pieces = [pair_ring(p, k) if k else p for k, p in enumerate(pieces)]
    (piece,) = call(
        pieces_kernel, (), pieces, [None] * pairs, [shape((piece_rows, wide), B16)], [None],
    )
    own = [pair_ring(piece, k) if k else piece for k in range(pairs)]
    theirs = [swap(p, "seq", 0) for p in own]
    g_gate, g_inner, g_bcoef, g_step, g_out = call(
        functools.partial(unpack_kernel, pairs), (1,), [*own, *theirs],
        [whole(piece_rows, wide)] * (2 * pairs),
        [shape((d, inner)), shape((d, inner)), shape((span, d)), shape((heads, d)),
         shape((inner, d))],
        [whole(d, inner), whole(d, inner), whole(span, d), whole(heads, d), whole(inner, d)],
        scratch=[pltpu.VMEM((d, 2 * span), F32)], scalars=(place,),
    )
    (small,) = call(
        add_kernel, (), [small, swap(small, "seq", 0)], [None] * 2,
        [shape((8, d))], [None],
    )
    smalls = [pair_ring(small, k) if k else small for k in range(pairs)]
    (g_gain, g_ci, g_cb, g_cib, g_cbb, g_sbias, g_dlog, g_skip, g_norm) = call(
        functools.partial(ends_kernel, pairs, heads), (), smalls, [None] * pairs,
        [shape((in_gain.shape[0],)), shape((4, inner)), shape((4, span)), shape((inner,)),
         shape((span,)), shape((heads,)), shape((heads,)), shape((heads,)), shape((inner,))],
        [None] * 9, scalars=(place,),
    )
    return (
        block_out,
        input_grad,
        g_gain,
        g_gate,
        g_inner,
        g_bcoef.T,
        g_step.T,
        g_ci,
        g_cb,
        g_cib,
        g_cbb,
        g_sbias,
        g_dlog,
        g_skip,
        g_norm,
        g_out,
    )


def solution(mesh):
    tokens = P(("seq", "wt"), None)
    cols, vec = P(None, "wt"), P("wt")
    return jax.shard_map(
        per_device,
        mesh=mesh,
        in_specs=(
            tokens, vec, cols, cols, cols, cols, cols, vec, cols, vec, vec, vec, vec, vec,
            P("wt", None), tokens, P(),
        ),
        out_specs=(
            tokens, tokens, vec, cols, cols, cols, cols, cols, cols, vec, vec, vec, vec, vec,
            vec, P("wt", None),
        ),
        check_vma=False,
    )
```
